32 devices in a mesh: groups: 2 (over y), seq: 4 (over z), mp: 4 (over x, core).
Axes of the slice: x: 2, y: 2, z: 4, core: 2. Of those that a mesh axis runs over, the one named last changes fastest.
Arguments:
- nucleotide_features: bfloat16 [3072, 1536], P(('groups', 'seq')), parts along dimension 0, may hold values from -36 to 36
- location_table: bfloat16 [1536, 1536], P('seq'), may hold values from -6 to 6
- premix_rescaler: float32 [1536], replicated, may hold values from 0.5 to 1.5
- probe_lookup_matrices: bfloat16 [2, 1536, 1024], P(None, None, 'mp'), may hold values from -0.15625 to 0.15625
- payload_projector: bfloat16 [1536, 1536], P(None, 'mp'), may hold values from -0.15625 to 0.15625
- logit_sharpness: float32 [8], P('mp'), may hold values from 8 to 32
- mixing_projector: bfloat16 [1536, 1536], P('mp'), may hold values from -0.15625 to 0.15625
- premlp_rescaler: float32 [1536], replicated, may hold values from 0.5 to 1.5
- widening_matrix: bfloat16 [1536, 3072], P(None, 'mp'), may hold values from -0.15625 to 0.15625
- narrowing_matrix: bfloat16 [3072, 1536], P('mp'), may hold values from -0.109375 to 0.109375
Outputs:
- averaged: float32 [3072, 1536], P(('groups', 'seq'), 'mp'), parts along dimension 0
The draws below stay inside these ranges and needn't reach their ends.
There are 2 independent parts, one for each index of `groups`. The reference program is written for one: setup_inputs(seed, part) draws one part's arguments, and reference() takes and returns one part's arrays. A program takes and returns all parts, laid end to end along the dimension named above; an argument that names none is the same for every part. Nothing has to cross between parts.
All inputs are finite; a program needn't handle non-finite values.
Results may differ from the reference program's by a relative error of at most 0.0033.
Values may be sent and summed in bfloat16 or wider, within the bound.
A program may use at most 128 MiB of HBM per device.

```python
import math
import jax
import jax.numpy as jnp
from jax import lax

D = 1536
NUM_SUBSPACES = 8
QK = 128
VD = 192
FF = 3072
SEQ_LEN = 1536


def draw_nucleotide_features(key, part):
    key_rows, key_cols, key_base = jax.random.split(key, 3)
    row_scale = jnp.exp(jax.random.uniform(key_rows, (SEQ_LEN, 1), jnp.float32, math.log(0.3), math.log(3.0)))
    col_scale = jnp.exp(jax.random.uniform(key_cols, (1, D), jnp.float32, math.log(0.3), math.log(3.0)))
    payload_vectors = jnp.clip(jax.random.normal(key_base, (SEQ_LEN, D), jnp.float32), -4.0, 4.0)
    return (payload_vectors * row_scale * col_scale).astype(jnp.bfloat16)


def levels(key, dims, pieces, low, largest):
    gain, own = 1.0, jax.random.fold_in(key, 6)
    for dim, blocks in pieces:
        heights = jnp.exp(jax.random.uniform(jax.random.fold_in(own, dim), (blocks,), jnp.float32, low / len(pieces), largest / len(pieces)))
        gain = gain * jnp.repeat(heights, dims[dim] // blocks).reshape([-1 if axis == dim else 1 for axis in range(len(dims))])
    return gain


def gaussian(rng, extent, spread, most, cuts=(), kind=jnp.bfloat16):
    level = levels(rng, extent, cuts, -0.22, 0.18) if cuts else 1.0
    result = jax.random.normal(rng, extent, jnp.float32) * spread * level
    return jnp.minimum(jnp.maximum(result, -most), most).astype(kind)


def setup_inputs(seed: int = 0, part: int = 0) -> dict:
    arg_keys = jax.random.split(jax.random.key(seed), 11)
    part_keys = jax.random.split(jax.random.fold_in(arg_keys[10], part), 11)
    nucleotide_features = draw_nucleotide_features(jax.random.fold_in(jax.random.fold_in(arg_keys[10], part), 71), part)
    location_table = gaussian(arg_keys[1], (SEQ_LEN, D), 1.0, 6.0, ((0, 4),))
    premix_rescaler = jnp.clip(1.0 + 0.1 * jax.random.normal(arg_keys[2], (D,), jnp.float32), 0.5, 1.5)
    probe_lookup_matrices = gaussian(arg_keys[3], (2, D, NUM_SUBSPACES * QK), D ** -0.5, 0.15625, ((2, 4),))
    payload_projector = gaussian(arg_keys[4], (D, NUM_SUBSPACES * VD), D ** -0.5, 0.15625, ((1, 4),))
    logit_sharpness = jnp.clip(jnp.exp(math.log(32.0) - 1.3862944 * jax.random.uniform(arg_keys[5], (NUM_SUBSPACES,), jnp.float32) ** levels(arg_keys[5], (NUM_SUBSPACES,), ((0, 4),), -0.2, 0.2)), 8.0, 32.0)
    mixing_projector = gaussian(arg_keys[6], (NUM_SUBSPACES * VD, D), (NUM_SUBSPACES * VD) ** -0.5, 0.15625, ((0, 4),))
    premlp_rescaler = jnp.clip(1.0 + 0.1 * jax.random.normal(arg_keys[7], (D,), jnp.float32), 0.5, 1.5)
    widening_matrix = gaussian(arg_keys[8], (D, FF), D ** -0.5, 0.15625, ((1, 4),))
    narrowing_matrix = gaussian(arg_keys[9], (FF, D), FF ** -0.5, 0.109375, ((0, 4),))
    return {"nucleotide_features": nucleotide_features, "location_table": location_table, "premix_rescaler": premix_rescaler, "probe_lookup_matrices": probe_lookup_matrices, "payload_projector": payload_projector, "logit_sharpness": logit_sharpness, "mixing_projector": mixing_projector, "premlp_rescaler": premlp_rescaler, "widening_matrix": widening_matrix, "narrowing_matrix": narrowing_matrix}


epsilon = 1e-06

def normalize(payload_vectors):
    return payload_vectors * lax.rsqrt(lax.optimization_barrier(jnp.mean(payload_vectors * payload_vectors, axis=-1, keepdims=True)) + epsilon)

def twin_helix_transformer(running_sum_hidden, premix_rescaler, probe_lookup_matrices, payload_projector, logit_sharpness, mixing_projector, premlp_rescaler, widening_matrix, narrowing_matrix):
    length = running_sum_hidden.shape[0]
    subspace_results = logit_sharpness.shape[0]
    lookup_dimension = probe_lookup_matrices.shape[2] // subspace_results
    value_size = payload_projector.shape[1] // subspace_results
    normed = (normalize(running_sum_hidden) * premix_rescaler).astype(jnp.bfloat16)
    query = jnp.dot(normed, probe_lookup_matrices[0], preferred_element_type=jnp.float32).reshape(length, subspace_results, lookup_dimension)
    keys = jnp.dot(normed, probe_lookup_matrices[1], preferred_element_type=jnp.float32).reshape(length, subspace_results, lookup_dimension)
    probe_unit_vectors = normalize(query).astype(jnp.bfloat16)
    lookup_unit_vectors = normalize(keys).astype(jnp.bfloat16)
    payload_vectors = jnp.dot(normed, payload_projector, preferred_element_type=jnp.float32).astype(jnp.bfloat16).reshape(length, subspace_results, value_size)

    def one_subspace(inputs):
        query_head, key_head, value_head, scale_head = inputs
        scores = jnp.dot(query_head, key_head.T, preferred_element_type=jnp.float32) * (scale_head / lookup_dimension)
        weight_exp = jnp.exp(scores)
        totals = lax.optimization_barrier(jnp.sum(weight_exp, axis=1, keepdims=True))
        numer = jnp.dot(weight_exp.astype(jnp.bfloat16), value_head, preferred_element_type=jnp.float32)
        return (numer / totals).astype(jnp.bfloat16)
    mixed_positions = lax.map(one_subspace, (jnp.transpose(probe_unit_vectors, (1, 0, 2)), jnp.transpose(lookup_unit_vectors, (1, 0, 2)), jnp.transpose(payload_vectors, (1, 0, 2)), logit_sharpness))
    mixed_positions = jnp.transpose(mixed_positions, (1, 0, 2)).reshape(length, subspace_results * value_size)
    middle = running_sum_hidden + jnp.dot(mixed_positions, mixing_projector, preferred_element_type=jnp.float32)
    normed_mid = (normalize(middle) * premlp_rescaler).astype(jnp.bfloat16)
    expanded = jax.nn.gelu(jnp.dot(normed_mid, widening_matrix, preferred_element_type=jnp.float32), approximate=True).astype(jnp.bfloat16)
    return middle + jnp.dot(expanded, narrowing_matrix, preferred_element_type=jnp.float32)

def reference(nucleotide_features, location_table, premix_rescaler, probe_lookup_matrices, payload_projector, logit_sharpness, mixing_projector, premlp_rescaler, widening_matrix, narrowing_matrix):
    reversed_tokens = jnp.flip(nucleotide_features, 0)
    plus_sequence = nucleotide_features.astype(jnp.float32) + location_table.astype(jnp.float32)
    complement_sequence = reversed_tokens.astype(jnp.float32) + location_table.astype(jnp.float32)
    plus_result = twin_helix_transformer(plus_sequence, premix_rescaler, probe_lookup_matrices, payload_projector, logit_sharpness, mixing_projector, premlp_rescaler, widening_matrix, narrowing_matrix)
    complement_result = twin_helix_transformer(complement_sequence, premix_rescaler, probe_lookup_matrices, payload_projector, logit_sharpness, mixing_projector, premlp_rescaler, widening_matrix, narrowing_matrix)
    return 0.5 * (plus_result + jnp.flip(complement_result, 0))
```

```python
import functools

import jax
import jax.numpy as jnp
from jax import lax
from jax.experimental import pallas as pl
from jax.experimental.pallas import tpu as pltpu
from jax.sharding import PartitionSpec as P

epsilon = 1e-06
MESH = pl.DeviceIdType.MESH
f32 = jnp.float32
bf16 = jnp.bfloat16


def normalize(v):
    return v * lax.rsqrt(jnp.mean(v * v, axis=-1, keepdims=True) + epsilon)


def halves(rows, nm):
    return rows // nm % 32 == 0


def gather_kernel(nz, nm, *refs):
    src = refs[0:2]
    out = refs[2:4]
    stage, lsem, zs, zr, xs, xr, cs, cr, ys, yr, fs, fr = refs[4:]
    g = lax.axis_index("groups")
    nx = nm // 2
    z = lax.axis_index("seq")
    m = lax.axis_index("mp")
    x, c = m // 2, m % 2
    rows = src[0].shape[0]
    piece = rows // nm

    split = halves(rows, nm)
    half = piece // 2

    def at(a, zsrc, mm, peer=False):
        if a == 1 and split:
            gg = 1 - g if peer else g
            return pl.ds(pl.multiple_of(zsrc * rows + mm * piece + gg * half, half), half)
        return pl.ds(pl.multiple_of(zsrc * rows + mm * piece, piece), piece)

    others = [lax.rem(x + d, nx) for d in range(1, nx)]
    barrier = pltpu.get_barrier_semaphore()

    @pl.when(z > 0)
    def _():
        pl.semaphore_signal(barrier, inc=1, device_id={"seq": z - 1}, device_id_type=MESH)

    @pl.when(z < nz - 1)
    def _():
        pl.semaphore_signal(barrier, inc=1, device_id={"seq": z + 1}, device_id_type=MESH)

    for o in others:
        pl.semaphore_signal(barrier, inc=1, device_id={"mp": o * 2 + c}, device_id_type=MESH)
    pl.semaphore_signal(barrier, inc=1, device_id={"mp": x * 2 + 1 - c}, device_id_type=MESH)
    if split:
        pl.semaphore_signal(barrier, inc=1, device_id={"groups": 1 - g}, device_id_type=MESH)

    loads = [pltpu.make_async_copy(src[a], stage.at[a], lsem.at[a]) for a in range(2)]
    for cp in loads:
        cp.start()

    pl.semaphore_wait(barrier, nx + int(split) + jnp.where(z > 0, 1, 0) + jnp.where(z < nz - 1, 1, 0))

    def zsend(a, dist, right):
        zsrc = z - dist if right else z + dist
        s = at(a, zsrc, m)
        if dist == 0:
            ref = src[a].at[at(a, 0, m)]
        else:
            ref = out[a].at[s]
        k = 0 if right else 1
        return pltpu.make_async_remote_copy(
            src_ref=ref, dst_ref=out[a].at[s],
            send_sem=zs.at[a, k, dist], recv_sem=zr.at[a, k, dist],
            device_id={"seq": z + 1 if right else z - 1}, device_id_type=MESH)

    def zrecv(a, dist, right):
        zsrc = z - dist if right else z + dist
        s = at(a, zsrc, m)
        k = 0 if right else 1
        return pltpu.make_async_remote_copy(
            src_ref=out[a].at[s], dst_ref=out[a].at[s],
            send_sem=zs.at[a, k, dist - 1], recv_sem=zr.at[a, k, dist - 1],
            device_id={"seq": z + 1 if right else z - 1}, device_id_type=MESH)

    def xcopy(a, k, dist, d, right, mine):
        zsrc = z - dist if right else z + dist
        o = lax.rem(x + d, nx) if mine else lax.rem(x - d + nx, nx)
        s = at(a, zsrc, m if mine else o * 2 + c)
        return pltpu.make_async_remote_copy(
            src_ref=out[a].at[s], dst_ref=out[a].at[s],
            send_sem=xs.at[a, k, dist - 1, d - 1], recv_sem=xr.at[a, k, dist - 1, d - 1],
            device_id={"mp": o * 2 + c}, device_id_type=MESH)

    def ccopy(a, k, dist, d, right, mine):
        zsrc = z - dist if right else z + dist
        o = lax.rem(x - d + nx, nx)
        s = at(a, zsrc, o * 2 + (c if mine else 1 - c))
        return pltpu.make_async_remote_copy(
            src_ref=out[a].at[s], dst_ref=out[a].at[s],
            send_sem=cs.at[a, k, dist - 1, d], recv_sem=cr.at[a, k, dist - 1, d],
            device_id={"mp": x * 2 + 1 - c}, device_id_type=MESH)

    def ycopy(k, dist, d, right, mine):
        zsrc = z - dist if right else z + dist
        s = at(1, zsrc, lax.rem(x - d + nx, nx) * 2 + c, not mine)
        return pltpu.make_async_remote_copy(
            src_ref=out[1].at[s], dst_ref=out[1].at[s],
            send_sem=ys.at[k, dist - 1, d], recv_sem=yr.at[k, dist - 1, d],
            device_id={"groups": 1 - g}, device_id_type=MESH)

    def fcopy(k, dist, d, right, mine):
        zsrc = z - dist if right else z + dist
        s = at(1, zsrc, lax.rem(x - d + nx, nx) * 2 + (c if mine else 1 - c), True)
        return pltpu.make_async_remote_copy(
            src_ref=out[1].at[s], dst_ref=out[1].at[s],
            send_sem=fs.at[k, dist - 1, d], recv_sem=fr.at[k, dist - 1, d],
            device_id={"mp": x * 2 + 1 - c}, device_id_type=MESH)

    def when(cond, f):
        @pl.when(cond)
        def _():
            f()

    can = {True: z < nz - 1, False: z > 0}

    for a in (1, 0):
        for right in (True, False):
            when(can[right], lambda a=a, right=right: zsend(a, 0, right).start())
    for a in range(2):
        loads[a].wait()
        st = pltpu.make_async_copy(
            stage.at[a], out[a].at[pl.ds(pl.multiple_of(z * rows, rows), rows)], lsem.at[a])
        st.start()

    def has(dist, right):
        return z - dist >= 0 if right else z + dist <= nz - 1

    def zstep(dist):
        for a in (1, 0):
            for right in (True, False):
                k = 0 if right else 1

                def got(a=a, right=right, k=k):
                    zrecv(a, dist, right).wait_recv()
                    if dist < nz - 1:
                        when(can[right], lambda: zsend(a, dist, right).start())
                    for d in range(1, nx):
                        xcopy(a, k, dist, d, right, True).start()
                    if a == 1 and split:
                        ycopy(k, dist, 0, right, True).start()
                    ccopy(a, k, dist, 0, right, True).start()

                when(has(dist, right), got)

    def xstep(dist):
        for a in (1, 0):
            for right in (True, False):
                k = 0 if right else 1

                def got(a=a, right=right, k=k):
                    for d in range(1, nx):
                        xcopy(a, k, dist, d, right, False).wait_recv()
                        if a == 1 and split:
                            ycopy(k, dist, d, right, True).start()
                        ccopy(a, k, dist, d, right, True).start()

                when(has(dist, right), got)

    def ystep(dist, ds):
        if not split or dist < 1:
            return
        for right in (True, False):
            k = 0 if right else 1

            def got(right=right, k=k):
                for d in ds:
                    ycopy(k, dist, d, right, False).wait_recv()
                    fcopy(k, dist, d, right, True).start()

            when(has(dist, right), got)

    far = tuple(range(1, nx))
    for dist in range(1, nz):
        zstep(dist)
        if dist > 1:
            xstep(dist - 1)
        ystep(dist - 1, (0,))
        ystep(dist - 2, far)
    ystep(nz - 2, far)
    ystep(nz - 1, (0,))
    xstep(nz - 1)
    ystep(nz - 1, far)

    for a in range(2):
        pltpu.make_async_copy(
            stage.at[a], out[a].at[pl.ds(pl.multiple_of(z * rows, rows), rows)], lsem.at[a]).wait()
    for dist in range(0, nz):
        for a in range(2):
            for right in (True, False):
                k = 0 if right else 1
                if dist < nz - 1:
                    cond = can[right] if dist == 0 else has(dist, right) & can[right]
                    when(cond, lambda a=a, right=right: zsend(a, dist, right).wait_send())
                if dist > 0:
                    def fin(a=a, right=right, k=k):
                        for d in range(1, nx):
                            xcopy(a, k, dist, d, right, True).wait_send()
                        for d in range(nx):
                            ccopy(a, k, dist, d, right, True).wait_send()
                            ccopy(a, k, dist, d, right, False).wait_recv()
                            if a == 1 and split:
                                ycopy(k, dist, d, right, True).wait_send()
                                fcopy(k, dist, d, right, True).wait_send()
                                fcopy(k, dist, d, right, False).wait_recv()
                    when(has(dist, right), fin)


def gather_inputs(nuc, loc, nz, nm):
    rows, width = nuc.shape
    nx = nm // 2
    dma = pltpu.SemaphoreType.DMA
    anyspec = pl.BlockSpec(memory_space=pl.ANY)
    shape = jax.ShapeDtypeStruct((nz * rows, width), bf16)
    ex = (2, nz - 1, nx) if halves(rows, nm) else (1,)
    return pl.pallas_call(
        functools.partial(gather_kernel, nz, nm),
        out_shape=(shape, shape),
        in_specs=[anyspec] * 2,
        out_specs=[anyspec] * 2,
        scratch_shapes=[
            pltpu.VMEM((2, rows, width), bf16),
            dma((2,)),
            dma((2, 2, nz)), dma((2, 2, nz)),
            dma((2, 2, nz - 1, nx)), dma((2, 2, nz - 1, nx)),
            dma((2, 2, nz - 1, nx)), dma((2, 2, nz - 1, nx)),
            dma(ex), dma(ex), dma(ex), dma(ex),
        ],
        compiler_params=pltpu.CompilerParams(collective_id=0, has_side_effects=True),
        name="gather_inputs",
    )(nuc, loc)


def attend_kernel(nz, nm, heads, qk, vd, sharp, nuc, loc, gain, wqk, wv, mix, out, mix_all,
                  q_s, k_s, v_s, xs, xr, ys, yr, cs, cr, os, orr):
    share_mix(nz, nm, mix, mix_all, xs, xr, ys, yr, cs, cr, os, orr, 0)
    t, j = pl.program_id(0), pl.program_id(1)
    z = lax.axis_index("seq")
    rows = nuc.shape[0]
    b = 128

    def body(flip):
        r_i = lax.broadcasted_iota(jnp.int32, (b, b), 0)
        c_i = lax.broadcasted_iota(jnp.int32, (b, b), 1)
        anti = jnp.where(r_i + c_i == b - 1, 1.0, 0.0).astype(bf16)
        parts = []
        nb = rows // b
        for i in range(nb):
            if flip:
                l = jnp.dot(anti, loc[(nb - 1 - i) * b:(nb - i) * b, :], preferred_element_type=f32)
            else:
                l = loc[i * b:(i + 1) * b, :].astype(f32)
            s = nuc[i * b:(i + 1) * b, :].astype(f32) + l
            parts.append((normalize(s) * gain[...]).astype(bf16))
        normed = jnp.concatenate(parts, axis=0)
        here = pl.ds(pl.multiple_of(j * rows, rows), rows)
        key = jnp.dot(normed, wqk[1], preferred_element_type=f32)
        for h in range(heads):
            k_s[here, h * qk:(h + 1) * qk] = normalize(key[:, h * qk:(h + 1) * qk]).astype(bf16)
        v_s[here, :] = jnp.dot(normed, wv[...], preferred_element_type=f32).astype(bf16)

        @pl.when(j == z)
        def _():
            query = jnp.dot(normed, wqk[0], preferred_element_type=f32)
            for h in range(heads):
                q_s[:, h * qk:(h + 1) * qk] = normalize(query[:, h * qk:(h + 1) * qk]).astype(bf16)

    @pl.when(t == 0)
    def _():
        body(False)

    @pl.when(t == 1)
    def _():
        body(True)

    @pl.when(j == nz - 1)
    def _():
        s_all = k_s.shape[0]
        chunk = 128
        wide = heads * vd
        for i in range(rows // chunk):
            rr = slice(i * chunk, (i + 1) * chunk)
            if i == 1:
                share_mix(nz, nm, mix, mix_all, xs, xr, ys, yr, cs, cr, os, orr, 2)
            res = []
            for h in range(heads):
                lo = (h * vd) // 128 * 128
                hi = min(-(-((h + 1) * vd) // 128) * 128, wide)
                num = jnp.zeros((chunk, hi - lo), f32)
                tot = jnp.zeros((chunk, 1), f32)
                step = 1536
                for kk in range(0, s_all, step):
                    sc = lax.dot_general(
                        q_s[rr, h * qk:(h + 1) * qk], k_s[kk:kk + step, h * qk:(h + 1) * qk],
                        (((1,), (1,)), ((), ())), preferred_element_type=f32)
                    w = jnp.exp(sc * (sharp[h] / qk))
                    tot = tot + jnp.sum(w, axis=-1, keepdims=True)
                    num = num + jnp.dot(w.astype(bf16), v_s[kk:kk + step, lo:hi],
                                        preferred_element_type=f32)
                res.append((lo, hi, num / tot))
            if heads == 1:
                out[rr, :] = res[0][2].astype(bf16)
            else:
                for lo in range(0, wide, 128):
                    hi = min(lo + 128, wide)
                    col = lo + lax.broadcasted_iota(jnp.int32, (chunk, hi - lo), 1)
                    val = None
                    for h in range(heads):
                        l0, h0, r = res[h]
                        if h * vd < hi and (h + 1) * vd > lo:
                            v = r[:, lo - l0:hi - l0]
                            val = v if val is None else jnp.where(col < h * vd, val, v)
                    out[rr, lo:hi] = val.astype(bf16)

    share_mix(nz, nm, mix, mix_all, xs, xr, ys, yr, cs, cr, os, orr, 1)


def share_mix(nz, nm, mix, mix_all, xs, xr, ys, yr, cs, cr, os, orr, phase):
    nx = nm // 2
    step = pl.program_id(0) * nz + pl.program_id(1)
    m = lax.axis_index("mp")
    g = lax.axis_index("groups")
    x, c = m // 2, m % 2
    n = 4 if mix.shape[0] % 128 == 0 else 2
    size = mix.shape[0] // (2 * n)

    def rows(gg, p):
        return pl.ds(pl.multiple_of((gg * n + p) * size, size), size)

    def xcopy(p, d, mine):
        o = lax.rem(x + d, nx) if mine else lax.rem(x - d + nx, nx)
        k = m if mine else o * 2 + c
        return pltpu.make_async_remote_copy(
            src_ref=mix.at[rows(g, p)], dst_ref=mix_all.at[k, rows(g, p)],
            send_sem=xs.at[p, d - 1], recv_sem=xr.at[p, d - 1],
            device_id={"mp": o * 2 + c}, device_id_type=MESH)

    def ycopy(p, d, mine):
        k = lax.rem(x - d + nx, nx) * 2 + c
        r = rows(g if mine else 1 - g, p)
        return pltpu.make_async_remote_copy(
            src_ref=mix_all.at[k, r], dst_ref=mix_all.at[k, r],
            send_sem=ys.at[p, d - 1], recv_sem=yr.at[p, d - 1],
            device_id={"groups": 1 - g}, device_id_type=MESH)

    def ccopy(p, d, far, mine):
        k = lax.rem(x - d + nx, nx) * 2 + (c if mine else 1 - c)
        r = rows(1 - g if far else g, p)
        f = 1 if far else 0
        return pltpu.make_async_remote_copy(
            src_ref=mix_all.at[k, r], dst_ref=mix_all.at[k, r],
            send_sem=cs.at[p, d - 1, f], recv_sem=cr.at[p, d - 1, f],
            device_id={"mp": x * 2 + 1 - c}, device_id_type=MESH)

    def own(mine):
        return pltpu.make_async_remote_copy(
            src_ref=mix, dst_ref=mix_all.at[m if mine else x * 2 + 1 - c],
            send_sem=os, recv_sem=orr,
            device_id={"mp": x * 2 + 1 - c}, device_id_type=MESH)

    def pass_on(p):
        for d in range(1, nx):
            xcopy(p, d, False).wait_recv()
            ycopy(p, d, True).start()
            ccopy(p, d, False, True).start()

    def bring(p):
        for d in range(1, nx):
            ycopy(p, d, False).wait_recv()
            ccopy(p, d, True, True).start()

    if phase == 0:
        @pl.when(step == 0)
        def _():
            barrier = pltpu.get_barrier_semaphore()
            for d in range(1, nx):
                pl.semaphore_signal(barrier, inc=1, device_id={"mp": lax.rem(x + d, nx) * 2 + c}, device_id_type=MESH)
            pl.semaphore_signal(barrier, inc=1, device_id={"mp": x * 2 + 1 - c}, device_id_type=MESH)
            pl.semaphore_signal(barrier, inc=1, device_id={"groups": 1 - g}, device_id_type=MESH)
            pl.semaphore_wait(barrier, nx + 1)
            for p in range(n):
                for d in range(1, nx):
                    xcopy(p, d, True).start()
            own(True).start()

        turns = {4: (nz - 1, None, nz, nz + 2), 2: (nz, nz + 2)}[n]
        for p in range(n):
            if turns[p] is not None:
                pl.when(step == turns[p])(functools.partial(pass_on, p))

        @pl.when(step == 2 * nz - 1)
        def _():
            for p in range(n // 2):
                bring(p)
    elif phase == 2:
        if n == 4:
            pl.when(step == nz - 1)(functools.partial(pass_on, 1))
    else:
        @pl.when(step == 2 * nz - 1)
        def _():
            for p in range(n // 2, n):
                bring(p)
            own(True).wait_send()
            own(False).wait_recv()
            for p in range(n):
                for d in range(1, nx):
                    xcopy(p, d, True).wait_send()
                    ycopy(p, d, True).wait_send()
                    for far in (False, True):
                        ccopy(p, d, far, True).wait_send()
                        ccopy(p, d, far, False).wait_recv()


def attend(nuc_all, loc_all, gain, wqk, wv, sharp, mix, nz, nm, rows):
    heads = sharp.shape[0]
    width = nuc_all.shape[1]
    qk = wqk.shape[2] // heads
    vd = wv.shape[1] // heads
    s_all = nuc_all.shape[0]
    nx = nm // 2
    dma = pltpu.SemaphoreType.DMA
    full = lambda a: pl.BlockSpec(a.shape, lambda t, j: (0,) * a.ndim, pipeline_mode=pl.Buffered(1))
    anyspec = pl.BlockSpec(memory_space=pl.ANY)
    gain = gain.reshape(1, width)
    return pl.pallas_call(
        functools.partial(attend_kernel, nz, nm, heads, qk, vd),
        grid=(2, nz),
        out_shape=(jax.ShapeDtypeStruct((2, rows, heads * vd), bf16),
                   jax.ShapeDtypeStruct((nm,) + mix.shape, bf16)),
        in_specs=[
            pl.BlockSpec(memory_space=pltpu.SMEM),
            pl.BlockSpec((rows, width), lambda t, j: (j, 0)),
            pl.BlockSpec((rows, width), lambda t, j: (t * (nz - 1 - j) + (1 - t) * j, 0)),
            full(gain), full(wqk), full(wv), anyspec,
        ],
        out_specs=(pl.BlockSpec((pl.Squeezed(), rows, heads * vd), lambda t, j: (t, 0, 0)), anyspec),
        scratch_shapes=[
            pltpu.VMEM((rows, heads * qk), bf16),
            pltpu.VMEM((s_all, heads * qk), bf16),
            pltpu.VMEM((s_all, heads * vd), bf16),
            dma((4, nx)), dma((4, nx)), dma((4, nx)), dma((4, nx)),
            dma((4, nx, 2)), dma((4, nx, 2)), dma, dma,
        ],
        compiler_params=pltpu.CompilerParams(
            collective_id=2, has_side_effects=True, vmem_limit_bytes=56 << 20),
        name="attend",
    )(sharp, nuc_all, loc_all, gain, wqk, wv, mix)


def tail_kernel(nz, nm, att, nuc_h, loc_h, loc_all, gain, mix, mix_all, widen_h, narrow_h, out,
                att_all, nuc, loc, locm, mixv, widen, narrow, sbuf, rbuf, mid,
                lsem, msem, xs, xr, cs, cr, ss, sr):
    nx = nm // 2
    rows, width = nuc.shape
    share = width // nm
    b = 128
    parts = rows // b
    z = lax.axis_index("seq")
    m = lax.axis_index("mp")
    x, c = m // 2, m % 2
    barrier = pltpu.get_barrier_semaphore()
    for d in range(1, nm):
        pl.semaphore_signal(barrier, inc=1, device_id={"mp": lax.rem(m + d, nm)}, device_id_type=MESH)
    loads = [
        pltpu.make_async_copy(att, att_all.at[m], lsem.at[0]),
        pltpu.make_async_copy(nuc_h, nuc, lsem.at[1]),
        pltpu.make_async_copy(loc_h, loc, lsem.at[2]),
        pltpu.make_async_copy(loc_all.at[pl.ds(pl.multiple_of((nz - 1 - z) * rows, rows), rows)], locm, lsem.at[3]),
        pltpu.make_async_copy(widen_h, widen, lsem.at[4]),
        pltpu.make_async_copy(narrow_h, narrow, lsem.at[5]),
    ]
    mloads = [pltpu.make_async_copy(mix, mixv.at[m], msem.at[0])]
    for d in range(1, nm):
        k = lax.rem(m + d, nm)
        mloads.append(pltpu.make_async_copy(mix_all.at[k], mixv.at[k], msem.at[d]))
    for cp in loads[:4] + mloads + loads[4:]:
        cp.start()
    pl.semaphore_wait(barrier, nm - 1)

    def xcopy(i, d, mine):
        o = lax.rem(x + d, nx) if mine else lax.rem(x - d + nx, nx)
        k = m if mine else o * 2 + c
        r = pl.ds(i * b, b)
        return pltpu.make_async_remote_copy(
            src_ref=att.at[:, r], dst_ref=att_all.at[k, :, r], send_sem=xs.at[i, d - 1],
            recv_sem=xr.at[i, d - 1], device_id={"mp": o * 2 + c}, device_id_type=MESH)

    def ccopy(i, d, mine):
        o = lax.rem(x - d + nx, nx)
        k = o * 2 + (c if mine else 1 - c)
        r = pl.ds(i * b, b)
        ref = att.at[:, r] if d == 0 else att_all.at[k, :, r]
        return pltpu.make_async_remote_copy(
            src_ref=ref, dst_ref=att_all.at[k, :, r], send_sem=cs.at[i, d], recv_sem=cr.at[i, d],
            device_id={"mp": x * 2 + 1 - c}, device_id_type=MESH)

    def scopy(i, d):
        k = lax.rem(m + d, nm)
        return pltpu.make_async_remote_copy(
            src_ref=sbuf.at[i, k], dst_ref=rbuf.at[i, d - 1], send_sem=ss.at[i, d - 1],
            recv_sem=sr.at[i, d - 1], device_id={"mp": k}, device_id_type=MESH)

    for i in range(parts):
        for d in range(1, nx):
            xcopy(i, d, True).start()
        ccopy(i, 0, True).start()

    def pass_on(i):
        for d in range(1, nx):
            xcopy(i, d, False).wait_recv()
            ccopy(i, d, True).start()

    r_i = lax.broadcasted_iota(jnp.int32, (b, b), 0)
    c_i = lax.broadcasted_iota(jnp.int32, (b, b), 1)
    anti = jnp.where(r_i + c_i == b - 1, 1.0, 0.0).astype(bf16)
    for cp in loads[:4]:
        cp.wait()
    pass_on(0)
    for cp in mloads:
        cp.wait()
    for i in range(parts):
        r = slice(i * b, (i + 1) * b)
        n = nuc[r, :].astype(f32)
        s0 = n + loc[r, :].astype(f32)
        s1 = n + jnp.dot(anti, locm[(parts - 1 - i) * b:(parts - i) * b, :], preferred_element_type=f32)
        middle = jnp.concatenate([s0, s1], axis=0)
        for d in range(nx):
            ccopy(i, d, False).wait_recv()
        for k in range(nm):
            a = jnp.concatenate([att_all[k, 0, r, :], att_all[k, 1, r, :]], axis=0)
            middle = middle + jnp.dot(a, mixv[k], preferred_element_type=f32)
        if i + 1 < parts:
            pass_on(i + 1)
        normed = (normalize(middle) * gain[...]).astype(bf16)
        if i == 0:
            for cp in loads[4:]:
                cp.wait()
        up = jax.nn.gelu(jnp.dot(normed, widen[...], preferred_element_type=f32), approximate=True)
        both = (up[:b] + up[b:]).astype(bf16)
        down = jnp.dot(both, narrow[...], preferred_element_type=f32)
        total = middle[:b] + middle[b:] + down
        down = down.astype(bf16)
        for k in range(nm):
            sbuf[i, k] = down[:, k * share:(k + 1) * share]
            mid[i, k] = total[:, k * share:(k + 1) * share]
        for d in range(1, nm):
            scopy(i, d).start()
    for i in range(parts):
        acc = mid[i, m]
        for d in range(1, nm):
            scopy(i, d).wait_recv()
            acc = acc + rbuf[i, d - 1].astype(f32)
        out[i * b:(i + 1) * b, :] = 0.5 * acc
    for i in range(parts):
        for d in range(1, nx):
            xcopy(i, d, True).wait_send()
        for d in range(nx):
            ccopy(i, d, True).wait_send()
        for d in range(1, nm):
            scopy(i, d).wait_send()


def tail(att, nuc, loc, loc_all, gain, mix, mix_all, widen, narrow, nz, nm):
    rows, width = nuc.shape
    share = width // nm
    nx = nm // 2
    parts = rows // 128
    dma = pltpu.SemaphoreType.DMA
    anyspec = pl.BlockSpec(memory_space=pl.ANY)
    vm = pl.BlockSpec(memory_space=pltpu.VMEM)
    v = pltpu.VMEM
    return pl.pallas_call(
        functools.partial(tail_kernel, nz, nm),
        out_shape=jax.ShapeDtypeStruct((rows, share), f32),
        in_specs=[vm, anyspec, anyspec, anyspec, vm, anyspec, anyspec, anyspec, anyspec],
        out_specs=vm,
        scratch_shapes=[
            v((nm,) + att.shape, bf16), v(nuc.shape, bf16), v(nuc.shape, bf16), v(nuc.shape, bf16),
            v((nm,) + mix.shape, bf16), v(widen.shape, bf16), v(narrow.shape, bf16),
            v((parts, nm, 128, share), bf16), v((parts, nm - 1, 128, share), bf16),
            v((parts, nm, 128, share), f32),
            dma((6,)), dma((nm,)),
            dma((parts, nx)), dma((parts, nx)), dma((parts, nx)), dma((parts, nx)),
            dma((parts, nm)), dma((parts, nm)),
        ],
        compiler_params=pltpu.CompilerParams(
            collective_id=3, has_side_effects=True, vmem_limit_bytes=56 << 20),
        name="tail",
    )(att, nuc, loc, loc_all, gain.reshape(1, width), mix, mix_all, widen, narrow)


PLANES = ((0, 3), (1, 2))


def fused(nz, nm, heads, qk, vd, rows):
    return nz == 4 and nm == 4 and heads == 2 and qk == 128 and vd == 192 and rows % 128 == 0


def block_kernel(nz, nm, sharp, gain1, gain2, nuc_h, loc_h, wqk_h, wv_h, mix_h, widen_h, narrow_h, out,
                 nuc, loc, locm, rloc, nbuf, wqk, wv, send, recv, kbuf, vbuf, asend, att, abuf,
                 mixv, widen, narrow, mid0, up0, mids, sbuf, rbuf,
                 lsem, ms, mr, xs, xr, qs, qr, ql, rs, rr, rl, hs, hr, ss, sr):
    rows, width = nuc.shape
    share = width // nm
    b = 128
    hb = b // 2
    parts = rows // b
    depth = mix_h.shape[0]
    g = lax.axis_index("groups")
    z = lax.axis_index("seq")
    m = lax.axis_index("mp")
    x, c = m // 2, m % 2
    to_x = {"mp": (1 - x) * 2 + c}
    to_y = {"groups": 1 - g}
    to_c = {"mp": x * 2 + 1 - c}

    def remote(src, dst, ssem, rsem, dev):
        return pltpu.make_async_remote_copy(
            src_ref=src, dst_ref=dst, send_sem=ssem, recv_sem=rsem, device_id=dev, device_id_type=MESH)

    barrier = pltpu.get_barrier_semaphore()
    for d in range(1, nz):
        pl.semaphore_signal(barrier, inc=1, device_id={"seq": lax.rem(z + d, nz)}, device_id_type=MESH)
    for d in range(1, nm):
        pl.semaphore_signal(barrier, inc=1, device_id={"mp": lax.rem(m + d, nm)}, device_id_type=MESH)
    pl.semaphore_signal(barrier, inc=1, device_id=to_y, device_id_type=MESH)

    loads = [
        pltpu.make_async_copy(nuc_h, nuc, lsem.at[0]),
        pltpu.make_async_copy(loc_h, loc, lsem.at[1]),
        pltpu.make_async_copy(wqk_h, wqk, lsem.at[2]),
        pltpu.make_async_copy(wv_h, wv, lsem.at[3]),
        pltpu.make_async_copy(widen_h, widen, lsem.at[4]),
        pltpu.make_async_copy(narrow_h, narrow, lsem.at[5]),
    ]
    own_mix = pltpu.make_async_copy(mix_h, mixv.at[pl.ds(pl.multiple_of(m * depth, depth), depth)], lsem.at[6])
    for cp in loads[:4]:
        cp.start()

    sl = rows // 8

    def piece(xx, gg, cc):
        return pl.ds(pl.multiple_of(((xx * 2 + gg) * 2 + cc) * sl, sl), sl)

    def loc_z():
        return remote(loc_h.at[piece(x, g, c)], locm.at[piece(x, g, c)], ms.at[0], mr.at[0], {"seq": nz - 1 - z})

    def loc_y():
        r = locm.at[piece(x, g, c)]
        return remote(r, r, ms.at[1], mr.at[1], to_y)

    def loc_x(k):
        r = locm.at[piece(x, g if k == 0 else 1 - g, c)]
        return remote(r, r, ms.at[2 + k], mr.at[2 + k], to_x)

    def loc_c(k):
        r = locm.at[piece(x if k < 2 else 1 - x, g if k % 2 == 0 else 1 - g, c)]
        return remote(r, r, ms.at[4 + k], mr.at[4 + k], to_c)

    size = depth // 4

    def mrows(mm, gg, p):
        return pl.ds(pl.multiple_of(mm * depth + (gg * 2 + p) * size, size), size)

    def mix_x(p):
        return remote(mix_h.at[mrows(0, g, p)], mixv.at[mrows(m, g, p)], xs.at[p], xr.at[p], to_x)

    def mix_y(p):
        r = mixv.at[mrows((1 - x) * 2 + c, g, p)]
        return remote(r, r, xs.at[2 + p], xr.at[2 + p], to_y)

    def mix_c(p, far):
        r = mixv.at[mrows((1 - x) * 2 + c, 1 - g if far else g, p)]
        k = (6 if far else 4) + p
        return remote(r, r, xs.at[k], xr.at[k], to_c)

    def mix_own():
        return remote(mix_h, mixv.at[pl.ds(pl.multiple_of(m * depth, depth), depth)], xs.at[8], xr.at[8], to_c)

    pl.semaphore_wait(barrier, nz + nm - 1)
    loc_z().start()
    mix_x(0).start()
    mix_own().start()
    own_mix.start()
    for cp in loads[4:]:
        cp.start()

    r_i = lax.broadcasted_iota(jnp.int32, (b, b), 0)
    c_i = lax.broadcasted_iota(jnp.int32, (b, b), 1)
    anti = jnp.where(r_i + c_i == b - 1, 1.0, 0.0).astype(bf16)
    low = lax.broadcasted_iota(jnp.int32, (hb, b), 1) < hb

    def chunk(i):
        return slice(i * b, (i + 1) * b)

    def qkv_send(t, h, i):
        return remote(send.at[t, h, i], recv.at[z, i], qs.at[t, h, i], qr.at[z, i], {"seq": PLANES[t][h]})

    def qkv_keep(t, h, i):
        return pltpu.make_async_copy(send.at[t, h, i], recv.at[z, i], ql.at[i])

    def project(t):
        other = loc if t == 0 else rloc
        for i in range(parts):
            if t == 1:
                rloc[chunk(i), :] = jnp.dot(
                    anti, locm[chunk(parts - 1 - i), :], preferred_element_type=f32).astype(bf16)
            s = nuc[chunk(i), :].astype(f32) + other[chunk(i), :].astype(f32)
            nbuf[chunk(i), :] = (normalize(s) * gain1[...]).astype(bf16)
        query = jnp.dot(nbuf[...], wqk[0], preferred_element_type=f32)
        key = jnp.dot(nbuf[...], wqk[1], preferred_element_type=f32)
        value = jnp.dot(nbuf[...], wv[...], preferred_element_type=f32)
        for i in range(parts):
            rest = value[chunk(i), b:2 * b]
            first, second = rest[:hb], pltpu.roll(rest[hb:], hb, 1)
            for h in range(2):
                send[t, h, i, 0:b, :] = normalize(query[chunk(i), h * b:(h + 1) * b]).astype(bf16)
                send[t, h, i, b:2 * b, :] = normalize(key[chunk(i), h * b:(h + 1) * b]).astype(bf16)
                send[t, h, i, 2 * b:3 * b, :] = value[chunk(i), 2 * h * b:(2 * h + 1) * b].astype(bf16)
                fold = jnp.where(low, first, second) if h == 0 else jnp.where(low, second, first)
                send[t, h, i, 3 * b:3 * b + hb, :] = fold.astype(bf16)
            for h in range(2):
                @pl.when(z != PLANES[t][h])
                def _(h=h, i=i):
                    qkv_send(t, h, i).start()

                @pl.when(z == PLANES[t][h])
                def _(h=h, i=i):
                    qkv_keep(t, h, i).start()

    def att_send(t, h, blk, i):
        return remote(asend.at[blk, i], att.at[m, t, i, h], rs.at[blk, i], rr.at[t, h, i], {"seq": blk})

    def att_keep(t, h, i):
        return pltpu.make_async_copy(asend.at[z, i], att.at[m, t, i, h], rl.at[i])

    def attend(t):
        h = jnp.where(z == PLANES[t][0], 0, 1)
        mask = low == (h == 0)
        for src in range(nz):
            for i in range(parts):
                @pl.when(z != src)
                def _():
                    remote(recv.at[src, i], recv.at[src, i], qs.at[0, 0, i], qr.at[src, i], {"seq": src}).wait_recv()

                @pl.when(z == src)
                def _():
                    qkv_keep(t, 0, i).wait()

                r0 = (src * parts + i) * b
                kbuf[r0:r0 + b, :] = recv[src, i, b:2 * b, :]
                vbuf[r0:r0 + b, 0:b] = recv[src, i, 2 * b:3 * b, :]
                fold = recv[src, i, 3 * b:3 * b + hb, :].astype(f32)
                turned = pltpu.roll(fold, hb, 1)
                vbuf[r0:r0 + hb, b:2 * b] = jnp.where(mask, fold, turned).astype(bf16)
                vbuf[r0 + hb:r0 + b, b:2 * b] = jnp.where(mask, turned, fold).astype(bf16)
        scale = sharp[h] * (1.4426950408889634 / b)
        up = z < nz // 2
        order = [jnp.where(up, 3, 0), jnp.where(up, 2, 1), z + 1 - 2 * lax.rem(z, 2), z]

        def step(i, carry):
            for s in range(nz):
                blk = order[s]
                sc = lax.dot_general(recv[blk, i, 0:b, :], kbuf[...], (((1,), (1,)), ((), ())),
                                     preferred_element_type=f32)
                w = jnp.exp2(sc * scale)
                tot = jnp.sum(w, axis=-1, keepdims=True)
                res = jnp.dot(w.astype(bf16), vbuf[...], preferred_element_type=f32) / tot
                asend[blk, i, 0:b, :] = res[:, :b].astype(bf16)
                asend[blk, i, b:b + hb, :] = jnp.where(mask, res[:hb, b:], res[hb:, b:]).astype(bf16)
                if s < nz - 1:
                    att_send(t, h, blk, i).start()
                else:
                    att_keep(t, h, i).start()
            return carry

        lax.fori_loop(0, parts, step, 0)

    def share_x(t, i):
        r = att.at[m, t, i]
        return remote(r, r, hs.at[t, i, 0], hr.at[t, i, 0], to_x)

    def share_c(t, i, k):
        r = att.at[m if k == 0 else (1 - x) * 2 + c, t, i]
        return remote(r, r, hs.at[t, i, 1 + k], hr.at[t, i, 1 + k], to_c)

    def relay(t, i):
        for h in range(2):
            src = PLANES[t][h]

            @pl.when(z != src)
            def _():
                r = att.at[m, t, i, h]
                remote(r, r, rs.at[0, i], rr.at[t, h, i], {"seq": src}).wait_recv()

            @pl.when(z == src)
            def _():
                att_keep(t, h, i).wait()
        share_x(t, i).start()
        share_c(t, i, 0).start()

    def relay_c(t, i):
        share_x(t, i).wait_recv()
        share_c(t, i, 1).start()

    def middle(t, i):
        for k in range(2):
            share_c(t, i, k).wait_recv()
        for k in range(nm):
            f0, f1 = att[k, t, i, 0, b:b + hb, :].astype(f32), att[k, t, i, 1, b:b + hb, :].astype(f32)
            lo = k * 3 * b
            abuf[chunk(i), lo:lo + b] = att[k, t, i, 0, 0:b, :]
            abuf[i * b:i * b + hb, lo + b:lo + 2 * b] = jnp.where(low, f0, f1).astype(bf16)
            abuf[i * b + hb:(i + 1) * b, lo + b:lo + 2 * b] = pltpu.roll(jnp.where(low, f1, f0), hb, 1).astype(bf16)
            abuf[chunk(i), lo + 2 * b:lo + 3 * b] = att[k, t, i, 1, 0:b, :]

    def upper(t, r):
        s = nuc[r, :].astype(f32) + (loc if t == 0 else rloc)[r, :].astype(f32)
        mid = s + jnp.dot(abuf[r, :], mixv[...], preferred_element_type=f32)
        normed = (normalize(mid) * gain2[...]).astype(bf16)
        return mid, jax.nn.gelu(jnp.dot(normed, widen[...], preferred_element_type=f32), approximate=True)

    def scopy(i, d):
        k = lax.rem(m + d, nm)
        return remote(sbuf.at[i, k], rbuf.at[i, d - 1], ss.at[i, d - 1], sr.at[i, d - 1], {"mp": k})

    for cp in loads[:4]:
        cp.wait()
    project(0)
    loc_z().wait_recv()
    loc_y().start()
    loc_x(0).start()
    loc_c(0).start()
    mix_x(0).wait_recv()
    loc_y().wait_recv()
    loc_x(1).start()
    loc_c(1).start()
    mix_x(1).start()
    mix_y(0).start()
    mix_c(0, False).start()
    loc_x(0).wait_recv()
    loc_c(2).start()
    loc_x(1).wait_recv()
    loc_c(3).start()
    for k in range(4):
        loc_c(k).wait_recv()
    project(1)
    mix_y(0).wait_recv()
    mix_c(0, True).start()

    @pl.when((z == PLANES[0][0]) | (z == PLANES[0][1]))
    def _():
        attend(0)

    mix_x(1).wait_recv()
    mix_y(1).start()
    mix_c(1, False).start()
    for i in range(parts):
        relay(0, i)
    mix_y(1).wait_recv()
    mix_c(1, True).start()
    for i in range(parts):
        relay_c(0, i)
    own_mix.wait()
    mix_own().wait_recv()
    for p in range(2):
        for far in (False, True):
            mix_c(p, far).wait_recv()
    for cp in loads[4:]:
        cp.wait()
    for i in range(parts):
        middle(0, i)
    for i in range(parts):
        mid, up = upper(0, chunk(i))
        mid0[chunk(i), :] = mid
        up0[chunk(i), :] = up

    @pl.when((z == PLANES[1][0]) | (z == PLANES[1][1]))
    def _():
        attend(1)

    for i in range(parts):
        relay(1, i)
        relay_c(1, i)
        middle(1, i)
        mid, up = upper(1, chunk(i))
        both = (up + up0[chunk(i), :]).astype(bf16)
        down = jnp.dot(both, narrow[...], preferred_element_type=f32)
        total = mid + mid0[chunk(i), :] + down
        down = down.astype(bf16)
        for k in range(nm):
            sbuf[i, k] = down[:, k * share:(k + 1) * share]
            mids[i, k] = total[:, k * share:(k + 1) * share]
        for d in range(1, nm):
            scopy(i, d).start()
    for i in range(parts):
        acc = mids[i, m]
        for d in range(1, nm):
            scopy(i, d).wait_recv()
            acc = acc + rbuf[i, d - 1].astype(f32)
        out[chunk(i), :] = 0.5 * acc

    loc_z().wait_send()
    loc_y().wait_send()
    for k in range(2):
        loc_x(k).wait_send()
    for k in range(4):
        loc_c(k).wait_send()
    mix_own().wait_send()
    for p in range(2):
        mix_x(p).wait_send()
        mix_y(p).wait_send()
        for far in (False, True):
            mix_c(p, far).wait_send()
    for i in range(parts):
        for t in range(2):
            for h in range(2):
                @pl.when(z != PLANES[t][h])
                def _():
                    qkv_send(t, h, i).wait_send()
            share_x(t, i).wait_send()
            for k in range(2):
                share_c(t, i, k).wait_send()
        for blk in range(nz):
            @pl.when(z != blk)
            def _():
                att_send(0, 0, blk, i).wait_send()
        for d in range(1, nm):
            scopy(i, d).wait_send()


def block(nuc, loc, premix, wqk, wv, sharp, mix, premlp, widen, narrow, nz, nm):
    rows, width = nuc.shape
    parts = rows // 128
    hidden = widen.shape[1]
    share = width // nm
    dma = pltpu.SemaphoreType.DMA
    anyspec = pl.BlockSpec(memory_space=pl.ANY)
    vm = pl.BlockSpec(memory_space=pltpu.VMEM)
    v = pltpu.VMEM
    return pl.pallas_call(
        functools.partial(block_kernel, nz, nm),
        out_shape=jax.ShapeDtypeStruct((rows, share), f32),
        in_specs=[pl.BlockSpec(memory_space=pltpu.SMEM), vm, vm] + [anyspec] * 7,
        out_specs=vm,
        scratch_shapes=[
            v(nuc.shape, bf16), v(nuc.shape, bf16), v(nuc.shape, bf16), v(nuc.shape, bf16), v(nuc.shape, bf16),
            v(wqk.shape, bf16), v(wv.shape, bf16),
            v((2, 2, parts, 448, 128), bf16), v((nz, parts, 448, 128), bf16),
            v((nz * rows, 128), bf16), v((nz * rows, 256), bf16),
            v((nz, parts, 192, 128), bf16), v((nm, 2, parts, 2, 192, 128), bf16), v((rows, width), bf16),
            v((nm * mix.shape[0], width), bf16), v(widen.shape, bf16), v(narrow.shape, bf16),
            v((rows, width), f32), v((rows, hidden), f32),
            v((parts, nm, 128, share), f32), v((parts, nm, 128, share), bf16), v((parts, nm - 1, 128, share), bf16),
            dma((7,)), dma((8,)), dma((8,)), dma((9,)), dma((9,)),
            dma((2, 2, parts)), dma((nz, parts)), dma((parts,)),
            dma((nz, parts)), dma((2, 2, parts)), dma((parts,)),
            dma((2, parts, 3)), dma((2, parts, 3)), dma((parts, nm)), dma((parts, nm)),
        ],
        compiler_params=pltpu.CompilerParams(
            collective_id=1, has_side_effects=True, vmem_limit_bytes=58 << 20),
        name="block",
    )(sharp, premix.reshape(1, width), premlp.reshape(1, width), nuc, loc, wqk, wv, mix, widen, narrow)


def shards(nuc, loc, premix, wqk, wv, sharp, mixing, premlp, widen, narrow):
    rows = nuc.shape[0]
    nz, nm = lax.axis_size("seq"), lax.axis_size("mp")
    heads = sharp.shape[0]
    if fused(nz, nm, heads, wqk.shape[2] // heads, wv.shape[1] // heads, rows):
        return block(nuc, loc, premix, wqk, wv, sharp, mixing, premlp, widen, narrow, nz, nm)
    nuc_all, loc_all = gather_inputs(nuc, loc, nz, nm)
    att, mix_all = attend(nuc_all, loc_all, premix, wqk, wv, sharp, mixing, nz, nm, rows)
    return tail(att, nuc, loc, loc_all, premlp, mixing, mix_all, widen, narrow, nz, nm)


def solution(mesh):
    return jax.shard_map(
        shards,
        mesh=mesh,
        in_specs=(
            P(("groups", "seq"), None),
            P("seq", None),
            P(),
            P(None, None, "mp"),
            P(None, "mp"),
            P("mp"),
            P("mp", None),
            P(),
            P(None, "mp"),
            P("mp", None),
        ),
        out_specs=P(("groups", "seq"), "mp"),
        check_vma=False,
    )
```

```python
import functools

import jax
import jax.numpy as jnp
from jax import lax
from jax.experimental import pallas as pl
from jax.experimental.pallas import tpu as pltpu
from jax.sharding import PartitionSpec as P

epsilon = 1e-06
MESH = pl.DeviceIdType.MESH
f32 = jnp.float32
bf16 = jnp.bfloat16


def normalize(v):
    return v * lax.rsqrt(jnp.mean(v * v, axis=-1, keepdims=True) + epsilon)


def halves(rows, nm):
    return rows // nm % 32 == 0


def gather_kernel(nz, nm, *refs):
    src = refs[0:2]
    out = refs[2:4]
    stage, lsem, zs, zr, xs, xr, cs, cr, ys, yr, fs, fr = refs[4:]
    g = lax.axis_index("groups")
    nx = nm // 2
    z = lax.axis_index("seq")
    m = lax.axis_index("mp")
    x, c = m // 2, m % 2
    rows = src[0].shape[0]
    piece = rows // nm

    split = halves(rows, nm)
    half = piece // 2

    def at(a, zsrc, mm, peer=False):
        if a == 1 and split:
            gg = 1 - g if peer else g
            return pl.ds(pl.multiple_of(zsrc * rows + mm * piece + gg * half, half), half)
        return pl.ds(pl.multiple_of(zsrc * rows + mm * piece, piece), piece)

    others = [lax.rem(x + d, nx) for d in range(1, nx)]
    barrier = pltpu.get_barrier_semaphore()

    @pl.when(z > 0)
    def _():
        pl.semaphore_signal(barrier, inc=1, device_id={"seq": z - 1}, device_id_type=MESH)

    @pl.when(z < nz - 1)
    def _():
        pl.semaphore_signal(barrier, inc=1, device_id={"seq": z + 1}, device_id_type=MESH)

    for o in others:
        pl.semaphore_signal(barrier, inc=1, device_id={"mp": o * 2 + c}, device_id_type=MESH)
    pl.semaphore_signal(barrier, inc=1, device_id={"mp": x * 2 + 1 - c}, device_id_type=MESH)
    if split:
        pl.semaphore_signal(barrier, inc=1, device_id={"groups": 1 - g}, device_id_type=MESH)

    loads = [pltpu.make_async_copy(src[a], stage.at[a], lsem.at[a]) for a in range(2)]
    for cp in loads:
        cp.start()

    pl.semaphore_wait(barrier, nx + int(split) + jnp.where(z > 0, 1, 0) + jnp.where(z < nz - 1, 1, 0))

    def zsend(a, dist, right):
        zsrc = z - dist if right else z + dist
        s = at(a, zsrc, m)
        if dist == 0:
            ref = src[a].at[at(a, 0, m)]
        else:
            ref = out[a].at[s]
        k = 0 if right else 1
        return pltpu.make_async_remote_copy(
            src_ref=ref, dst_ref=out[a].at[s],
            send_sem=zs.at[a, k, dist], recv_sem=zr.at[a, k, dist],
            device_id={"seq": z + 1 if right else z - 1}, device_id_type=MESH)

    def zrecv(a, dist, right):
        zsrc = z - dist if right else z + dist
        s = at(a, zsrc, m)
        k = 0 if right else 1
        return pltpu.make_async_remote_copy(
            src_ref=out[a].at[s], dst_ref=out[a].at[s],
            send_sem=zs.at[a, k, dist - 1], recv_sem=zr.at[a, k, dist - 1],
            device_id={"seq": z + 1 if right else z - 1}, device_id_type=MESH)

    def xcopy(a, k, dist, d, right, mine):
        zsrc = z - dist if right else z + dist
        o = lax.rem(x + d, nx) if mine else lax.rem(x - d + nx, nx)
        s = at(a, zsrc, m if mine else o * 2 + c)
        return pltpu.make_async_remote_copy(
            src_ref=out[a].at[s], dst_ref=out[a].at[s],
            send_sem=xs.at[a, k, dist - 1, d - 1], recv_sem=xr.at[a, k, dist - 1, d - 1],
            device_id={"mp": o * 2 + c}, device_id_type=MESH)

    def ccopy(a, k, dist, d, right, mine):
        zsrc = z - dist if right else z + dist
        o = lax.rem(x - d + nx, nx)
        s = at(a, zsrc, o * 2 + (c if mine else 1 - c))
        return pltpu.make_async_remote_copy(
            src_ref=out[a].at[s], dst_ref=out[a].at[s],
            send_sem=cs.at[a, k, dist - 1, d], recv_sem=cr.at[a, k, dist - 1, d],
            device_id={"mp": x * 2 + 1 - c}, device_id_type=MESH)

    def ycopy(k, dist, d, right, mine):
        zsrc = z - dist if right else z + dist
        s = at(1, zsrc, lax.rem(x - d + nx, nx) * 2 + c, not mine)
        return pltpu.make_async_remote_copy(
            src_ref=out[1].at[s], dst_ref=out[1].at[s],
            send_sem=ys.at[k, dist - 1, d], recv_sem=yr.at[k, dist - 1, d],
            device_id={"groups": 1 - g}, device_id_type=MESH)

    def fcopy(k, dist, d, right, mine):
        zsrc = z - dist if right else z + dist
        s = at(1, zsrc, lax.rem(x - d + nx, nx) * 2 + (c if mine else 1 - c), True)
        return pltpu.make_async_remote_copy(
            src_ref=out[1].at[s], dst_ref=out[1].at[s],
            send_sem=fs.at[k, dist - 1, d], recv_sem=fr.at[k, dist - 1, d],
            device_id={"mp": x * 2 + 1 - c}, device_id_type=MESH)

    def when(cond, f):
        @pl.when(cond)
        def _():
            f()

    can = {True: z < nz - 1, False: z > 0}

    for a in (1, 0):
        for right in (True, False):
            when(can[right], lambda a=a, right=right: zsend(a, 0, right).start())
    for a in range(2):
        loads[a].wait()
        st = pltpu.make_async_copy(
            stage.at[a], out[a].at[pl.ds(pl.multiple_of(z * rows, rows), rows)], lsem.at[a])
        st.start()

    def has(dist, right):
        return z - dist >= 0 if right else z + dist <= nz - 1

    def zstep(dist):
        for a in (1, 0):
            for right in (True, False):
                k = 0 if right else 1

                def got(a=a, right=right, k=k):
                    zrecv(a, dist, right).wait_recv()
                    if dist < nz - 1:
                        when(can[right], lambda: zsend(a, dist, right).start())
                    for d in range(1, nx):
                        xcopy(a, k, dist, d, right, True).start()
                    if a == 1 and split:
                        ycopy(k, dist, 0, right, True).start()
                    ccopy(a, k, dist, 0, right, True).start()

                when(has(dist, right), got)

    def xstep(dist):
        for a in (1, 0):
            for right in (True, False):
                k = 0 if right else 1

                def got(a=a, right=right, k=k):
                    for d in range(1, nx):
                        xcopy(a, k, dist, d, right, False).wait_recv()
                        if a == 1 and split:
                            ycopy(k, dist, d, right, True).start()
                        ccopy(a, k, dist, d, right, True).start()

                when(has(dist, right), got)

    def ystep(dist, ds):
        if not split or dist < 1:
            return
        for right in (True, False):
            k = 0 if right else 1

            def got(right=right, k=k):
                for d in ds:
                    ycopy(k, dist, d, right, False).wait_recv()
                    fcopy(k, dist, d, right, True).start()

            when(has(dist, right), got)

    far = tuple(range(1, nx))
    for dist in range(1, nz):
        zstep(dist)
        if dist > 1:
            xstep(dist - 1)
        ystep(dist - 1, (0,))
        ystep(dist - 2, far)
    ystep(nz - 2, far)
    ystep(nz - 1, (0,))
    xstep(nz - 1)
    ystep(nz - 1, far)

    for a in range(2):
        pltpu.make_async_copy(
            stage.at[a], out[a].at[pl.ds(pl.multiple_of(z * rows, rows), rows)], lsem.at[a]).wait()
    for dist in range(0, nz):
        for a in range(2):
            for right in (True, False):
                k = 0 if right else 1
                if dist < nz - 1:
                    cond = can[right] if dist == 0 else has(dist, right) & can[right]
                    when(cond, lambda a=a, right=right: zsend(a, dist, right).wait_send())
                if dist > 0:
                    def fin(a=a, right=right, k=k):
                        for d in range(1, nx):
                            xcopy(a, k, dist, d, right, True).wait_send()
                        for d in range(nx):
                            ccopy(a, k, dist, d, right, True).wait_send()
                            ccopy(a, k, dist, d, right, False).wait_recv()
                            if a == 1 and split:
                                ycopy(k, dist, d, right, True).wait_send()
                                fcopy(k, dist, d, right, True).wait_send()
                                fcopy(k, dist, d, right, False).wait_recv()
                    when(has(dist, right), fin)


def gather_inputs(nuc, loc, nz, nm):
    rows, width = nuc.shape
    nx = nm // 2
    dma = pltpu.SemaphoreType.DMA
    anyspec = pl.BlockSpec(memory_space=pl.ANY)
    shape = jax.ShapeDtypeStruct((nz * rows, width), bf16)
    ex = (2, nz - 1, nx) if halves(rows, nm) else (1,)
    return pl.pallas_call(
        functools.partial(gather_kernel, nz, nm),
        out_shape=(shape, shape),
        in_specs=[anyspec] * 2,
        out_specs=[anyspec] * 2,
        scratch_shapes=[
            pltpu.VMEM((2, rows, width), bf16),
            dma((2,)),
            dma((2, 2, nz)), dma((2, 2, nz)),
            dma((2, 2, nz - 1, nx)), dma((2, 2, nz - 1, nx)),
            dma((2, 2, nz - 1, nx)), dma((2, 2, nz - 1, nx)),
            dma(ex), dma(ex), dma(ex), dma(ex),
        ],
        compiler_params=pltpu.CompilerParams(collective_id=0, has_side_effects=True),
        name="gather_inputs",
    )(nuc, loc)


def attend_kernel(nz, nm, heads, qk, vd, sharp, nuc, loc, gain, wqk, wv, mix, out, mix_all,
                  q_s, k_s, v_s, xs, xr, ys, yr, cs, cr, os, orr):
    share_mix(nz, nm, mix, mix_all, xs, xr, ys, yr, cs, cr, os, orr, 0)
    t, j = pl.program_id(0), pl.program_id(1)
    z = lax.axis_index("seq")
    rows = nuc.shape[0]
    b = 128

    def body(flip):
        r_i = lax.broadcasted_iota(jnp.int32, (b, b), 0)
        c_i = lax.broadcasted_iota(jnp.int32, (b, b), 1)
        anti = jnp.where(r_i + c_i == b - 1, 1.0, 0.0).astype(bf16)
        parts = []
        nb = rows // b
        for i in range(nb):
            if flip:
                l = jnp.dot(anti, loc[(nb - 1 - i) * b:(nb - i) * b, :], preferred_element_type=f32)
            else:
                l = loc[i * b:(i + 1) * b, :].astype(f32)
            s = nuc[i * b:(i + 1) * b, :].astype(f32) + l
            parts.append((normalize(s) * gain[...]).astype(bf16))
        normed = jnp.concatenate(parts, axis=0)
        here = pl.ds(pl.multiple_of(j * rows, rows), rows)
        key = jnp.dot(normed, wqk[1], preferred_element_type=f32)
        for h in range(heads):
            k_s[here, h * qk:(h + 1) * qk] = normalize(key[:, h * qk:(h + 1) * qk]).astype(bf16)
        v_s[here, :] = jnp.dot(normed, wv[...], preferred_element_type=f32).astype(bf16)

        @pl.when(j == z)
        def _():
            query = jnp.dot(normed, wqk[0], preferred_element_type=f32)
            for h in range(heads):
                q_s[:, h * qk:(h + 1) * qk] = normalize(query[:, h * qk:(h + 1) * qk]).astype(bf16)

    @pl.when(t == 0)
    def _():
        body(False)

    @pl.when(t == 1)
    def _():
        body(True)

    @pl.when(j == nz - 1)
    def _():
        s_all = k_s.shape[0]
        chunk = 128
        wide = heads * vd
        for i in range(rows // chunk):
            rr = slice(i * chunk, (i + 1) * chunk)
            if i == 1:
                share_mix(nz, nm, mix, mix_all, xs, xr, ys, yr, cs, cr, os, orr, 2)
            res = []
            for h in range(heads):
                lo = (h * vd) // 128 * 128
                hi = min(-(-((h + 1) * vd) // 128) * 128, wide)
                num = jnp.zeros((chunk, hi - lo), f32)
                tot = jnp.zeros((chunk, 1), f32)
                step = 1536
                for kk in range(0, s_all, step):
                    sc = lax.dot_general(
                        q_s[rr, h * qk:(h + 1) * qk], k_s[kk:kk + step, h * qk:(h + 1) * qk],
                        (((1,), (1,)), ((), ())), preferred_element_type=f32)
                    w = jnp.exp(sc * (sharp[h] / qk))
                    tot = tot + jnp.sum(w, axis=-1, keepdims=True)
                    num = num + jnp.dot(w.astype(bf16), v_s[kk:kk + step, lo:hi],
                                        preferred_element_type=f32)
                res.append((lo, hi, num / tot))
            if heads == 1:
                out[rr, :] = res[0][2].astype(bf16)
            else:
                for lo in range(0, wide, 128):
                    hi = min(lo + 128, wide)
                    col = lo + lax.broadcasted_iota(jnp.int32, (chunk, hi - lo), 1)
                    val = None
                    for h in range(heads):
                        l0, h0, r = res[h]
                        if h * vd < hi and (h + 1) * vd > lo:
                            v = r[:, lo - l0:hi - l0]
                            val = v if val is None else jnp.where(col < h * vd, val, v)
                    out[rr, lo:hi] = val.astype(bf16)

    share_mix(nz, nm, mix, mix_all, xs, xr, ys, yr, cs, cr, os, orr, 1)


def share_mix(nz, nm, mix, mix_all, xs, xr, ys, yr, cs, cr, os, orr, phase):
    nx = nm // 2
    step = pl.program_id(0) * nz + pl.program_id(1)
    m = lax.axis_index("mp")
    g = lax.axis_index("groups")
    x, c = m // 2, m % 2
    n = 4 if mix.shape[0] % 128 == 0 else 2
    size = mix.shape[0] // (2 * n)

    def rows(gg, p):
        return pl.ds(pl.multiple_of((gg * n + p) * size, size), size)

    def xcopy(p, d, mine):
        o = lax.rem(x + d, nx) if mine else lax.rem(x - d + nx, nx)
        k = m if mine else o * 2 + c
        return pltpu.make_async_remote_copy(
            src_ref=mix.at[rows(g, p)], dst_ref=mix_all.at[k, rows(g, p)],
            send_sem=xs.at[p, d - 1], recv_sem=xr.at[p, d - 1],
            device_id={"mp": o * 2 + c}, device_id_type=MESH)

    def ycopy(p, d, mine):
        k = lax.rem(x - d + nx, nx) * 2 + c
        r = rows(g if mine else 1 - g, p)
        return pltpu.make_async_remote_copy(
            src_ref=mix_all.at[k, r], dst_ref=mix_all.at[k, r],
            send_sem=ys.at[p, d - 1], recv_sem=yr.at[p, d - 1],
            device_id={"groups": 1 - g}, device_id_type=MESH)

    def ccopy(p, d, far, mine):
        k = lax.rem(x - d + nx, nx) * 2 + (c if mine else 1 - c)
        r = rows(1 - g if far else g, p)
        f = 1 if far else 0
        return pltpu.make_async_remote_copy(
            src_ref=mix_all.at[k, r], dst_ref=mix_all.at[k, r],
            send_sem=cs.at[p, d - 1, f], recv_sem=cr.at[p, d - 1, f],
            device_id={"mp": x * 2 + 1 - c}, device_id_type=MESH)

    def own(mine):
        return pltpu.make_async_remote_copy(
            src_ref=mix, dst_ref=mix_all.at[m if mine else x * 2 + 1 - c],
            send_sem=os, recv_sem=orr,
            device_id={"mp": x * 2 + 1 - c}, device_id_type=MESH)

    def pass_on(p):
        for d in range(1, nx):
            xcopy(p, d, False).wait_recv()
            ycopy(p, d, True).start()
            ccopy(p, d, False, True).start()

    def bring(p):
        for d in range(1, nx):
            ycopy(p, d, False).wait_recv()
            ccopy(p, d, True, True).start()

    if phase == 0:
        @pl.when(step == 0)
        def _():
            barrier = pltpu.get_barrier_semaphore()
            for d in range(1, nx):
                pl.semaphore_signal(barrier, inc=1, device_id={"mp": lax.rem(x + d, nx) * 2 + c}, device_id_type=MESH)
            pl.semaphore_signal(barrier, inc=1, device_id={"mp": x * 2 + 1 - c}, device_id_type=MESH)
            pl.semaphore_signal(barrier, inc=1, device_id={"groups": 1 - g}, device_id_type=MESH)
            pl.semaphore_wait(barrier, nx + 1)
            for p in range(n):
                for d in range(1, nx):
                    xcopy(p, d, True).start()
            own(True).start()

        turns = {4: (nz - 1, None, nz, nz + 2), 2: (nz, nz + 2)}[n]
        for p in range(n):
            if turns[p] is not None:
                pl.when(step == turns[p])(functools.partial(pass_on, p))

        @pl.when(step == 2 * nz - 1)
        def _():
            for p in range(n // 2):
                bring(p)
    elif phase == 2:
        if n == 4:
            pl.when(step == nz - 1)(functools.partial(pass_on, 1))
    else:
        @pl.when(step == 2 * nz - 1)
        def _():
            for p in range(n // 2, n):
                bring(p)
            own(True).wait_send()
            own(False).wait_recv()
            for p in range(n):
                for d in range(1, nx):
                    xcopy(p, d, True).wait_send()
                    ycopy(p, d, True).wait_send()
                    for far in (False, True):
                        ccopy(p, d, far, True).wait_send()
                        ccopy(p, d, far, False).wait_recv()


def attend(nuc_all, loc_all, gain, wqk, wv, sharp, mix, nz, nm, rows):
    heads = sharp.shape[0]
    width = nuc_all.shape[1]
    qk = wqk.shape[2] // heads
    vd = wv.shape[1] // heads
    s_all = nuc_all.shape[0]
    nx = nm // 2
    dma = pltpu.SemaphoreType.DMA
    full = lambda a: pl.BlockSpec(a.shape, lambda t, j: (0,) * a.ndim, pipeline_mode=pl.Buffered(1))
    anyspec = pl.BlockSpec(memory_space=pl.ANY)
    gain = gain.reshape(1, width)
    return pl.pallas_call(
        functools.partial(attend_kernel, nz, nm, heads, qk, vd),
        grid=(2, nz),
        out_shape=(jax.ShapeDtypeStruct((2, rows, heads * vd), bf16),
                   jax.ShapeDtypeStruct((nm,) + mix.shape, bf16)),
        in_specs=[
            pl.BlockSpec(memory_space=pltpu.SMEM),
            pl.BlockSpec((rows, width), lambda t, j: (j, 0)),
            pl.BlockSpec((rows, width), lambda t, j: (t * (nz - 1 - j) + (1 - t) * j, 0)),
            full(gain), full(wqk), full(wv), anyspec,
        ],
        out_specs=(pl.BlockSpec((pl.Squeezed(), rows, heads * vd), lambda t, j: (t, 0, 0)), anyspec),
        scratch_shapes=[
            pltpu.VMEM((rows, heads * qk), bf16),
            pltpu.VMEM((s_all, heads * qk), bf16),
            pltpu.VMEM((s_all, heads * vd), bf16),
            dma((4, nx)), dma((4, nx)), dma((4, nx)), dma((4, nx)),
            dma((4, nx, 2)), dma((4, nx, 2)), dma, dma,
        ],
        compiler_params=pltpu.CompilerParams(
            collective_id=2, has_side_effects=True, vmem_limit_bytes=56 << 20),
        name="attend",
    )(sharp, nuc_all, loc_all, gain, wqk, wv, mix)


def tail_kernel(nz, nm, att, nuc_h, loc_h, loc_all, gain, mix, mix_all, widen_h, narrow_h, out,
                att_all, nuc, loc, locm, mixv, widen, narrow, sbuf, rbuf, mid,
                lsem, msem, xs, xr, cs, cr, ss, sr):
    nx = nm // 2
    rows, width = nuc.shape
    share = width // nm
    b = 128
    parts = rows // b
    z = lax.axis_index("seq")
    m = lax.axis_index("mp")
    x, c = m // 2, m % 2
    barrier = pltpu.get_barrier_semaphore()
    for d in range(1, nm):
        pl.semaphore_signal(barrier, inc=1, device_id={"mp": lax.rem(m + d, nm)}, device_id_type=MESH)
    loads = [
        pltpu.make_async_copy(att, att_all.at[m], lsem.at[0]),
        pltpu.make_async_copy(nuc_h, nuc, lsem.at[1]),
        pltpu.make_async_copy(loc_h, loc, lsem.at[2]),
        pltpu.make_async_copy(loc_all.at[pl.ds(pl.multiple_of((nz - 1 - z) * rows, rows), rows)], locm, lsem.at[3]),
        pltpu.make_async_copy(widen_h, widen, lsem.at[4]),
        pltpu.make_async_copy(narrow_h, narrow, lsem.at[5]),
    ]
    mloads = [pltpu.make_async_copy(mix, mixv.at[m], msem.at[0])]
    for d in range(1, nm):
        k = lax.rem(m + d, nm)
        mloads.append(pltpu.make_async_copy(mix_all.at[k], mixv.at[k], msem.at[d]))
    for cp in loads[:4] + mloads + loads[4:]:
        cp.start()
    pl.semaphore_wait(barrier, nm - 1)

    def xcopy(i, d, mine):
        o = lax.rem(x + d, nx) if mine else lax.rem(x - d + nx, nx)
        k = m if mine else o * 2 + c
        r = pl.ds(i * b, b)
        return pltpu.make_async_remote_copy(
            src_ref=att.at[:, r], dst_ref=att_all.at[k, :, r], send_sem=xs.at[i, d - 1],
            recv_sem=xr.at[i, d - 1], device_id={"mp": o * 2 + c}, device_id_type=MESH)

    def ccopy(i, d, mine):
        o = lax.rem(x - d + nx, nx)
        k = o * 2 + (c if mine else 1 - c)
        r = pl.ds(i * b, b)
        ref = att.at[:, r] if d == 0 else att_all.at[k, :, r]
        return pltpu.make_async_remote_copy(
            src_ref=ref, dst_ref=att_all.at[k, :, r], send_sem=cs.at[i, d], recv_sem=cr.at[i, d],
            device_id={"mp": x * 2 + 1 - c}, device_id_type=MESH)

    def scopy(i, d):
        k = lax.rem(m + d, nm)
        return pltpu.make_async_remote_copy(
            src_ref=sbuf.at[i, k], dst_ref=rbuf.at[i, d - 1], send_sem=ss.at[i, d - 1],
            recv_sem=sr.at[i, d - 1], device_id={"mp": k}, device_id_type=MESH)

    for i in range(parts):
        for d in range(1, nx):
            xcopy(i, d, True).start()
        ccopy(i, 0, True).start()

    def pass_on(i):
        for d in range(1, nx):
            xcopy(i, d, False).wait_recv()
            ccopy(i, d, True).start()

    r_i = lax.broadcasted_iota(jnp.int32, (b, b), 0)
    c_i = lax.broadcasted_iota(jnp.int32, (b, b), 1)
    anti = jnp.where(r_i + c_i == b - 1, 1.0, 0.0).astype(bf16)
    for cp in loads[:4]:
        cp.wait()
    pass_on(0)
    for cp in mloads:
        cp.wait()
    for i in range(parts):
        r = slice(i * b, (i + 1) * b)
        n = nuc[r, :].astype(f32)
        s0 = n + loc[r, :].astype(f32)
        s1 = n + jnp.dot(anti, locm[(parts - 1 - i) * b:(parts - i) * b, :], preferred_element_type=f32)
        middle = jnp.concatenate([s0, s1], axis=0)
        for d in range(nx):
            ccopy(i, d, False).wait_recv()
        for k in range(nm):
            a = jnp.concatenate([att_all[k, 0, r, :], att_all[k, 1, r, :]], axis=0)
            middle = middle + jnp.dot(a, mixv[k], preferred_element_type=f32)
        if i + 1 < parts:
            pass_on(i + 1)
        normed = (normalize(middle) * gain[...]).astype(bf16)
        if i == 0:
            for cp in loads[4:]:
                cp.wait()
        up = jax.nn.gelu(jnp.dot(normed, widen[...], preferred_element_type=f32), approximate=True)
        both = (up[:b] + up[b:]).astype(bf16)
        down = jnp.dot(both, narrow[...], preferred_element_type=f32)
        total = middle[:b] + middle[b:] + down
        down = down.astype(bf16)
        for k in range(nm):
            sbuf[i, k] = down[:, k * share:(k + 1) * share]
            mid[i, k] = total[:, k * share:(k + 1) * share]
        for d in range(1, nm):
            scopy(i, d).start()
    for i in range(parts):
        acc = mid[i, m]
        for d in range(1, nm):
            scopy(i, d).wait_recv()
            acc = acc + rbuf[i, d - 1].astype(f32)
        out[i * b:(i + 1) * b, :] = 0.5 * acc
    for i in range(parts):
        for d in range(1, nx):
            xcopy(i, d, True).wait_send()
        for d in range(nx):
            ccopy(i, d, True).wait_send()
        for d in range(1, nm):
            scopy(i, d).wait_send()


def tail(att, nuc, loc, loc_all, gain, mix, mix_all, widen, narrow, nz, nm):
    rows, width = nuc.shape
    share = width // nm
    nx = nm // 2
    parts = rows // 128
    dma = pltpu.SemaphoreType.DMA
    anyspec = pl.BlockSpec(memory_space=pl.ANY)
    vm = pl.BlockSpec(memory_space=pltpu.VMEM)
    v = pltpu.VMEM
    return pl.pallas_call(
        functools.partial(tail_kernel, nz, nm),
        out_shape=jax.ShapeDtypeStruct((rows, share), f32),
        in_specs=[vm, anyspec, anyspec, anyspec, vm, anyspec, anyspec, anyspec, anyspec],
        out_specs=vm,
        scratch_shapes=[
            v((nm,) + att.shape, bf16), v(nuc.shape, bf16), v(nuc.shape, bf16), v(nuc.shape, bf16),
            v((nm,) + mix.shape, bf16), v(widen.shape, bf16), v(narrow.shape, bf16),
            v((parts, nm, 128, share), bf16), v((parts, nm - 1, 128, share), bf16),
            v((parts, nm, 128, share), f32),
            dma((6,)), dma((nm,)),
            dma((parts, nx)), dma((parts, nx)), dma((parts, nx)), dma((parts, nx)),
            dma((parts, nm)), dma((parts, nm)),
        ],
        compiler_params=pltpu.CompilerParams(
            collective_id=3, has_side_effects=True, vmem_limit_bytes=56 << 20),
        name="tail",
    )(att, nuc, loc, loc_all, gain.reshape(1, width), mix, mix_all, widen, narrow)


PLANES = ((0, 3), (1, 2))


def fused(nz, nm, heads, qk, vd, rows):
    return nz == 4 and nm == 4 and heads == 2 and qk == 128 and vd == 192 and rows % 128 == 0


def block_kernel(nz, nm, sharp, gain1, gain2, nuc_h, loc_h, wqk_h, wv_h, mix_h, widen_h, narrow_h, out,
                 nuc, loc, locm, rloc, nbuf, wqk, wv, send, recv, kbuf, vbuf, asend, att, abuf,
                 mixv, widen, narrow, mid0, up0, mids, downs, sbuf, rbuf, xbuf, fbuf,
                 lsem, ms, mr, xs, xr, qs, qr, ql, rs, rr, rl, hs, hr, ss, sr):
    rows, width = nuc.shape
    share = width // nm
    b = 128
    hb = b // 2
    parts = rows // b
    depth = mix_h.shape[0]
    g = lax.axis_index("groups")
    z = lax.axis_index("seq")
    m = lax.axis_index("mp")
    x, c = m // 2, m % 2
    to_x = {"mp": (1 - x) * 2 + c}
    to_y = {"groups": 1 - g}
    to_d = {"groups": 1 - g, "mp": (1 - x) * 2 + c}
    to_c = {"mp": x * 2 + 1 - c}

    def remote(src, dst, ssem, rsem, dev):
        return pltpu.make_async_remote_copy(
            src_ref=src, dst_ref=dst, send_sem=ssem, recv_sem=rsem, device_id=dev, device_id_type=MESH)

    barrier = pltpu.get_barrier_semaphore()
    for d in range(1, nz):
        pl.semaphore_signal(barrier, inc=1, device_id={"seq": lax.rem(z + d, nz)}, device_id_type=MESH)
    for d in range(1, nm):
        pl.semaphore_signal(barrier, inc=1, device_id={"mp": lax.rem(m + d, nm)}, device_id_type=MESH)
    pl.semaphore_signal(barrier, inc=1, device_id=to_y, device_id_type=MESH)
    pl.semaphore_signal(barrier, inc=1, device_id=to_d, device_id_type=MESH)

    loads = [
        pltpu.make_async_copy(nuc_h, nuc, lsem.at[0]),
        pltpu.make_async_copy(loc_h, loc, lsem.at[1]),
        pltpu.make_async_copy(wqk_h, wqk, lsem.at[2]),
        pltpu.make_async_copy(wv_h, wv, lsem.at[3]),
        pltpu.make_async_copy(widen_h, widen, lsem.at[4]),
        pltpu.make_async_copy(narrow_h, narrow, lsem.at[5]),
    ]
    own_mix = pltpu.make_async_copy(mix_h, mixv.at[pl.ds(pl.multiple_of(m * depth, depth), depth)], lsem.at[6])
    for cp in loads[:4]:
        cp.start()

    sl = rows // 8

    def piece(xx, gg, cc):
        return pl.ds(pl.multiple_of(((xx * 2 + gg) * 2 + cc) * sl, sl), sl)

    def loc_z():
        return remote(loc_h.at[piece(x, g, c)], locm.at[piece(x, g, c)], ms.at[0], mr.at[0], {"seq": nz - 1 - z})

    def loc_on(k):
        r = locm.at[piece(x, g, c)]
        return remote(r, r, ms.at[1 + k], mr.at[1 + k], (to_x, to_y, to_d)[k])

    def loc_c(k):
        r = locm.at[piece(x if k % 2 == 0 else 1 - x, g if k < 2 else 1 - g, c)]
        return remote(r, r, ms.at[4 + k], mr.at[4 + k], to_c)

    size = depth // 4

    def mrows(mm, gg, p):
        return pl.ds(pl.multiple_of(mm * depth + (gg * 2 + p) * size, size), size)

    def mix_x(p):
        return remote(mix_h.at[mrows(0, g, p)], mixv.at[mrows(m, g, p)], xs.at[p], xr.at[p], to_x)

    def mix_y(p):
        r = mixv.at[mrows((1 - x) * 2 + c, g, p)]
        return remote(r, r, xs.at[2 + p], xr.at[2 + p], to_y)

    def mix_c(p, far):
        r = mixv.at[mrows((1 - x) * 2 + c, 1 - g if far else g, p)]
        k = (6 if far else 4) + p
        return remote(r, r, xs.at[k], xr.at[k], to_c)

    def mix_own():
        return remote(mix_h, mixv.at[pl.ds(pl.multiple_of(m * depth, depth), depth)], xs.at[8], xr.at[8], to_c)

    pl.semaphore_wait(barrier, nz + nm)
    loc_z().start()
    mix_x(0).start()
    mix_own().start()
    own_mix.start()
    for cp in loads[4:]:
        cp.start()

    r_i = lax.broadcasted_iota(jnp.int32, (b, b), 0)
    c_i = lax.broadcasted_iota(jnp.int32, (b, b), 1)
    anti = jnp.where(r_i + c_i == b - 1, 1.0, 0.0).astype(bf16)
    low = lax.broadcasted_iota(jnp.int32, (hb, b), 1) < hb

    def chunk(i):
        return slice(i * b, (i + 1) * b)

    def qkv_send(t, h, i):
        return remote(send.at[t, h, i], recv.at[z, i], qs.at[t, h, i], qr.at[z, i], {"seq": PLANES[t][h]})

    def qkv_keep(t, h, i):
        return pltpu.make_async_copy(send.at[t, h, i], recv.at[z, i], ql.at[i])

    def project(t):
        other = loc if t == 0 else rloc
        for i in range(parts):
            if t == 1:
                rloc[chunk(i), :] = jnp.dot(
                    anti, locm[chunk(parts - 1 - i), :], preferred_element_type=f32).astype(bf16)
            s = nuc[chunk(i), :].astype(f32) + other[chunk(i), :].astype(f32)
            nbuf[chunk(i), :] = (normalize(s) * gain1[...]).astype(bf16)
        query = jnp.dot(nbuf[...], wqk[0], preferred_element_type=f32)
        key = jnp.dot(nbuf[...], wqk[1], preferred_element_type=f32)
        value = jnp.dot(nbuf[...], wv[...], preferred_element_type=f32)
        for i in range(parts):
            rest = value[chunk(i), b:2 * b]
            first, second = rest[:hb], pltpu.roll(rest[hb:], hb, 1)
            for h in range(2):
                send[t, h, i, 0:b, :] = normalize(query[chunk(i), h * b:(h + 1) * b]).astype(bf16)
                send[t, h, i, b:2 * b, :] = normalize(key[chunk(i), h * b:(h + 1) * b]).astype(bf16)
                send[t, h, i, 2 * b:3 * b, :] = value[chunk(i), 2 * h * b:(2 * h + 1) * b].astype(bf16)
                fold = jnp.where(low, first, second) if h == 0 else jnp.where(low, second, first)
                send[t, h, i, 3 * b:3 * b + hb, :] = fold.astype(bf16)
            for h in range(2):
                @pl.when(z != PLANES[t][h])
                def _(h=h, i=i):
                    qkv_send(t, h, i).start()

                @pl.when(z == PLANES[t][h])
                def _(h=h, i=i):
                    qkv_keep(t, h, i).start()

    def att_send(t, h, blk, i):
        return remote(asend.at[blk, i], att.at[m, t, i, h], rs.at[blk, i], rr.at[t, h, i], {"seq": blk})

    def att_keep(t, h, i):
        return pltpu.make_async_copy(asend.at[z, i], att.at[m, t, i, h], rl.at[i])

    def attend(t):
        h = jnp.where(z == PLANES[t][0], 0, 1)
        mask = low == (h == 0)
        for src in range(nz):
            for i in range(parts):
                @pl.when(z != src)
                def _():
                    remote(recv.at[src, i], recv.at[src, i], qs.at[0, 0, i], qr.at[src, i], {"seq": src}).wait_recv()

                @pl.when(z == src)
                def _():
                    qkv_keep(t, 0, i).wait()

                r0 = (src * parts + i) * b
                kbuf[r0:r0 + b, :] = recv[src, i, b:2 * b, :]
                vbuf[r0:r0 + b, 0:b] = recv[src, i, 2 * b:3 * b, :]
                fold = recv[src, i, 3 * b:3 * b + hb, :].astype(f32)
                turned = pltpu.roll(fold, hb, 1)
                vbuf[r0:r0 + hb, b:2 * b] = jnp.where(mask, fold, turned).astype(bf16)
                vbuf[r0 + hb:r0 + b, b:2 * b] = jnp.where(mask, turned, fold).astype(bf16)
        scale = sharp[h] * (1.4426950408889634 / b)
        up = z < nz // 2
        order = [jnp.where(up, 3, 0), jnp.where(up, 2, 1), z + 1 - 2 * lax.rem(z, 2), z]

        def step(i, carry):
            for s in range(nz):
                blk = order[s]
                sc = lax.dot_general(recv[blk, i, 0:b, :], kbuf[...], (((1,), (1,)), ((), ())),
                                     preferred_element_type=f32)
                w = jnp.exp2(sc * scale)
                tot = jnp.sum(w, axis=-1, keepdims=True)
                res = jnp.dot(w.astype(bf16), vbuf[...], preferred_element_type=f32) / tot
                asend[blk, i, 0:b, :] = res[:, :b].astype(bf16)
                asend[blk, i, b:b + hb, :] = jnp.where(mask, res[:hb, b:], res[hb:, b:]).astype(bf16)
                if s < nz - 1:
                    att_send(t, h, blk, i).start()
                else:
                    att_keep(t, h, i).start()
            return carry

        lax.fori_loop(0, parts, step, 0)

    def share_x(t, i):
        r = att.at[m, t, i]
        return remote(r, r, hs.at[t, i, 0], hr.at[t, i, 0], to_x)

    def share_c(t, i, k):
        r = att.at[m if k == 0 else (1 - x) * 2 + c, t, i]
        return remote(r, r, hs.at[t, i, 1 + k], hr.at[t, i, 1 + k], to_c)

    def relay(t, i):
        for h in range(2):
            src = PLANES[t][h]

            @pl.when(z != src)
            def _():
                r = att.at[m, t, i, h]
                remote(r, r, rs.at[0, i], rr.at[t, h, i], {"seq": src}).wait_recv()

            @pl.when(z == src)
            def _():
                att_keep(t, h, i).wait()
        share_x(t, i).start()
        share_c(t, i, 0).start()

    def relay_c(t, i):
        share_x(t, i).wait_recv()
        share_c(t, i, 1).start()

    def middle(t, i):
        for k in range(2):
            share_c(t, i, k).wait_recv()
        for k in range(nm):
            f0, f1 = att[k, t, i, 0, b:b + hb, :].astype(f32), att[k, t, i, 1, b:b + hb, :].astype(f32)
            lo = k * 3 * b
            abuf[chunk(i), lo:lo + b] = att[k, t, i, 0, 0:b, :]
            abuf[i * b:i * b + hb, lo + b:lo + 2 * b] = jnp.where(low, f0, f1).astype(bf16)
            abuf[i * b + hb:(i + 1) * b, lo + b:lo + 2 * b] = pltpu.roll(jnp.where(low, f1, f0), hb, 1).astype(bf16)
            abuf[chunk(i), lo + 2 * b:lo + 3 * b] = att[k, t, i, 1, 0:b, :]

    def upper(t, r):
        s = nuc[r, :].astype(f32) + (loc if t == 0 else rloc)[r, :].astype(f32)
        mid = s + jnp.dot(abuf[r, :], mixv[...], preferred_element_type=f32)
        normed = (normalize(mid) * gain2[...]).astype(bf16)
        return mid, jax.nn.gelu(jnp.dot(normed, widen[...], preferred_element_type=f32), approximate=True)

    def pair_copy(i):
        return remote(sbuf.at[i, 1 - c], rbuf.at[i], ss.at[i, 0], sr.at[i, 0], to_c)

    def sum_copy(i):
        return remote(xbuf.at[i], fbuf.at[i], ss.at[i, 1], sr.at[i, 1], to_x)

    def pass_sum(i):
        pair_copy(i).wait_recv()
        xbuf[i] = (downs[i, c, 1 - x] + rbuf[i, 1 - x].astype(f32)).astype(bf16)
        sum_copy(i).start()

    first = (z == PLANES[0][0]) | (z == PLANES[0][1])
    second = (z == PLANES[1][0]) | (z == PLANES[1][1])
    for cp in loads[:4]:
        cp.wait()
    project(0)
    loc_z().wait_recv()
    for k in (2, 0, 1):
        loc_on(k).start()
    loc_c(0).start()
    mix_x(0).wait_recv()
    mix_y(0).start()
    mix_c(0, False).start()
    for k in range(3):
        loc_on(k).wait_recv()
        loc_c(k + 1).start()
    mix_x(1).start()
    for k in range(4):
        loc_c(k).wait_recv()
    project(1)
    mix_y(0).wait_recv()
    mix_c(0, True).start()
    mix_x(1).wait_recv()
    mix_y(1).start()
    mix_c(1, False).start()

    @pl.when(first)
    def _():
        attend(0)

    for i in range(parts):
        relay(0, i)
    mix_y(1).wait_recv()
    mix_c(1, True).start()

    @pl.when(second)
    def _():
        attend(1)

    for i in range(parts):
        relay_c(0, i)
    own_mix.wait()
    mix_own().wait_recv()
    for p in range(2):
        for far in (False, True):
            mix_c(p, far).wait_recv()
    for cp in loads[4:]:
        cp.wait()
    for i in range(parts):
        middle(0, i)
    for i in range(parts):
        pl.when(second)(functools.partial(relay, 1, i))
        mid, up = upper(0, chunk(i))
        mid0[chunk(i), :] = mid
        up0[chunk(i), :] = up
    pl.when(first)(functools.partial(relay, 1, 0))
    for i in range(parts):
        if i + 1 < parts:
            pl.when(first)(functools.partial(relay, 1, i + 1))
        relay_c(1, i)
        if i > 0:
            pass_sum(i - 1)
        middle(1, i)
        mid, up = upper(1, chunk(i))
        both = (up + up0[chunk(i), :]).astype(bf16)
        down = jnp.dot(both, narrow[...], preferred_element_type=f32)
        total = mid + mid0[chunk(i), :] + down
        for k in range(nm):
            cols = slice(k * share, (k + 1) * share)
            sbuf[i, k % 2, k // 2] = down[:, cols].astype(bf16)
            downs[i, k % 2, k // 2] = down[:, cols]
            mids[i, k] = total[:, cols]
        pair_copy(i).start()
    pass_sum(parts - 1)
    for i in range(parts):
        sum_copy(i).wait_recv()
        out[chunk(i), :] = 0.5 * (mids[i, m] + rbuf[i, x].astype(f32) + fbuf[i].astype(f32))

    loc_z().wait_send()
    for k in range(3):
        loc_on(k).wait_send()
    for k in range(4):
        loc_c(k).wait_send()
    mix_own().wait_send()
    for p in range(2):
        mix_x(p).wait_send()
        mix_y(p).wait_send()
        for far in (False, True):
            mix_c(p, far).wait_send()
    for i in range(parts):
        for t in range(2):
            for h in range(2):
                @pl.when(z != PLANES[t][h])
                def _():
                    qkv_send(t, h, i).wait_send()
            share_x(t, i).wait_send()
            for k in range(2):
                share_c(t, i, k).wait_send()
        for blk in range(nz):
            @pl.when(z != blk)
            def _():
                att_send(0, 0, blk, i).wait_send()
        pair_copy(i).wait_send()
        sum_copy(i).wait_send()


def block(nuc, loc, premix, wqk, wv, sharp, mix, premlp, widen, narrow, nz, nm):
    rows, width = nuc.shape
    parts = rows // 128
    hidden = widen.shape[1]
    share = width // nm
    dma = pltpu.SemaphoreType.DMA
    anyspec = pl.BlockSpec(memory_space=pl.ANY)
    vm = pl.BlockSpec(memory_space=pltpu.VMEM)
    v = pltpu.VMEM
    return pl.pallas_call(
        functools.partial(block_kernel, nz, nm),
        out_shape=jax.ShapeDtypeStruct((rows, share), f32),
        in_specs=[pl.BlockSpec(memory_space=pltpu.SMEM), vm, vm] + [anyspec] * 7,
        out_specs=vm,
        scratch_shapes=[
            v(nuc.shape, bf16), v(nuc.shape, bf16), v(nuc.shape, bf16), v(nuc.shape, bf16), v(nuc.shape, bf16),
            v(wqk.shape, bf16), v(wv.shape, bf16),
            v((2, 2, parts, 448, 128), bf16), v((nz, parts, 448, 128), bf16),
            v((nz * rows, 128), bf16), v((nz * rows, 256), bf16),
            v((nz, parts, 192, 128), bf16), v((nm, 2, parts, 2, 192, 128), bf16), v((rows, width), bf16),
            v((nm * mix.shape[0], width), bf16), v(widen.shape, bf16), v(narrow.shape, bf16),
            v((rows, width), f32), v((rows, hidden), f32),
            v((parts, nm, 128, share), f32), v((parts, 2, 2, 128, share), f32),
            v((parts, 2, 2, 128, share), bf16), v((parts, 2, 128, share), bf16),
            v((parts, 128, share), bf16), v((parts, 128, share), bf16),
            dma((7,)), dma((8,)), dma((8,)), dma((9,)), dma((9,)),
            dma((2, 2, parts)), dma((nz, parts)), dma((parts,)),
            dma((nz, parts)), dma((2, 2, parts)), dma((parts,)),
            dma((2, parts, 3)), dma((2, parts, 3)), dma((parts, 2)), dma((parts, 2)),
        ],
        compiler_params=pltpu.CompilerParams(
            collective_id=1, has_side_effects=True, vmem_limit_bytes=58 << 20),
        name="block",
    )(sharp, premix, premlp, nuc, loc, wqk, wv, mix, widen, narrow)


def shards(nuc, loc, premix, wqk, wv, sharp, mixing, premlp, widen, narrow):
    rows = nuc.shape[0]
    nz, nm = lax.axis_size("seq"), lax.axis_size("mp")
    heads = sharp.shape[0]
    if fused(nz, nm, heads, wqk.shape[2] // heads, wv.shape[1] // heads, rows):
        return block(nuc, loc, premix, wqk, wv, sharp, mixing, premlp, widen, narrow, nz, nm)
    nuc_all, loc_all = gather_inputs(nuc, loc, nz, nm)
    att, mix_all = attend(nuc_all, loc_all, premix, wqk, wv, sharp, mixing, nz, nm, rows)
    return tail(att, nuc, loc, loc_all, premlp, mixing, mix_all, widen, narrow, nz, nm)


def solution(mesh):
    return jax.shard_map(
        shards,
        mesh=mesh,
        in_specs=(
            P(("groups", "seq"), None),
            P("seq", None),
            P(),
            P(None, None, "mp"),
            P(None, "mp"),
            P("mp"),
            P("mp", None),
            P(),
            P(None, "mp"),
            P("mp", None),
        ),
        out_specs=P(("groups", "seq"), "mp"),
        check_vma=False,
    )
```

```python
import functools

import jax
import jax.numpy as jnp
from jax import lax
from jax.experimental import pallas as pl
from jax.experimental.pallas import tpu as pltpu
from jax.sharding import PartitionSpec as P

epsilon = 1e-06
MESH = pl.DeviceIdType.MESH
f32 = jnp.float32
bf16 = jnp.bfloat16


def normalize(v):
    return v * lax.rsqrt(jnp.mean(v * v, axis=-1, keepdims=True) + epsilon)


def halves(rows, nm):
    return rows // nm % 32 == 0


def gather_kernel(nz, nm, *refs):
    src = refs[0:2]
    out = refs[2:4]
    stage, lsem, zs, zr, xs, xr, cs, cr, ys, yr, fs, fr = refs[4:]
    g = lax.axis_index("groups")
    nx = nm // 2
    z = lax.axis_index("seq")
    m = lax.axis_index("mp")
    x, c = m // 2, m % 2
    rows = src[0].shape[0]
    piece = rows // nm

    split = halves(rows, nm)
    half = piece // 2

    def at(a, zsrc, mm, peer=False):
        if a == 1 and split:
            gg = 1 - g if peer else g
            return pl.ds(pl.multiple_of(zsrc * rows + mm * piece + gg * half, half), half)
        return pl.ds(pl.multiple_of(zsrc * rows + mm * piece, piece), piece)

    others = [lax.rem(x + d, nx) for d in range(1, nx)]
    barrier = pltpu.get_barrier_semaphore()

    @pl.when(z > 0)
    def _():
        pl.semaphore_signal(barrier, inc=1, device_id={"seq": z - 1}, device_id_type=MESH)

    @pl.when(z < nz - 1)
    def _():
        pl.semaphore_signal(barrier, inc=1, device_id={"seq": z + 1}, device_id_type=MESH)

    for o in others:
        pl.semaphore_signal(barrier, inc=1, device_id={"mp": o * 2 + c}, device_id_type=MESH)
    pl.semaphore_signal(barrier, inc=1, device_id={"mp": x * 2 + 1 - c}, device_id_type=MESH)
    if split:
        pl.semaphore_signal(barrier, inc=1, device_id={"groups": 1 - g}, device_id_type=MESH)

    loads = [pltpu.make_async_copy(src[a], stage.at[a], lsem.at[a]) for a in range(2)]
    for cp in loads:
        cp.start()

    pl.semaphore_wait(barrier, nx + int(split) + jnp.where(z > 0, 1, 0) + jnp.where(z < nz - 1, 1, 0))

    def zsend(a, dist, right):
        zsrc = z - dist if right else z + dist
        s = at(a, zsrc, m)
        if dist == 0:
            ref = src[a].at[at(a, 0, m)]
        else:
            ref = out[a].at[s]
        k = 0 if right else 1
        return pltpu.make_async_remote_copy(
            src_ref=ref, dst_ref=out[a].at[s],
            send_sem=zs.at[a, k, dist], recv_sem=zr.at[a, k, dist],
            device_id={"seq": z + 1 if right else z - 1}, device_id_type=MESH)

    def zrecv(a, dist, right):
        zsrc = z - dist if right else z + dist
        s = at(a, zsrc, m)
        k = 0 if right else 1
        return pltpu.make_async_remote_copy(
            src_ref=out[a].at[s], dst_ref=out[a].at[s],
            send_sem=zs.at[a, k, dist - 1], recv_sem=zr.at[a, k, dist - 1],
            device_id={"seq": z + 1 if right else z - 1}, device_id_type=MESH)

    def xcopy(a, k, dist, d, right, mine):
        zsrc = z - dist if right else z + dist
        o = lax.rem(x + d, nx) if mine else lax.rem(x - d + nx, nx)
        s = at(a, zsrc, m if mine else o * 2 + c)
        return pltpu.make_async_remote_copy(
            src_ref=out[a].at[s], dst_ref=out[a].at[s],
            send_sem=xs.at[a, k, dist - 1, d - 1], recv_sem=xr.at[a, k, dist - 1, d - 1],
            device_id={"mp": o * 2 + c}, device_id_type=MESH)

    def ccopy(a, k, dist, d, right, mine):
        zsrc = z - dist if right else z + dist
        o = lax.rem(x - d + nx, nx)
        s = at(a, zsrc, o * 2 + (c if mine else 1 - c))
        return pltpu.make_async_remote_copy(
            src_ref=out[a].at[s], dst_ref=out[a].at[s],
            send_sem=cs.at[a, k, dist - 1, d], recv_sem=cr.at[a, k, dist - 1, d],
            device_id={"mp": x * 2 + 1 - c}, device_id_type=MESH)

    def ycopy(k, dist, d, right, mine):
        zsrc = z - dist if right else z + dist
        s = at(1, zsrc, lax.rem(x - d + nx, nx) * 2 + c, not mine)
        return pltpu.make_async_remote_copy(
            src_ref=out[1].at[s], dst_ref=out[1].at[s],
            send_sem=ys.at[k, dist - 1, d], recv_sem=yr.at[k, dist - 1, d],
            device_id={"groups": 1 - g}, device_id_type=MESH)

    def fcopy(k, dist, d, right, mine):
        zsrc = z - dist if right else z + dist
        s = at(1, zsrc, lax.rem(x - d + nx, nx) * 2 + (c if mine else 1 - c), True)
        return pltpu.make_async_remote_copy(
            src_ref=out[1].at[s], dst_ref=out[1].at[s],
            send_sem=fs.at[k, dist - 1, d], recv_sem=fr.at[k, dist - 1, d],
            device_id={"mp": x * 2 + 1 - c}, device_id_type=MESH)

    def when(cond, f):
        @pl.when(cond)
        def _():
            f()

    can = {True: z < nz - 1, False: z > 0}

    for a in (1, 0):
        for right in (True, False):
            when(can[right], lambda a=a, right=right: zsend(a, 0, right).start())
    for a in range(2):
        loads[a].wait()
        st = pltpu.make_async_copy(
            stage.at[a], out[a].at[pl.ds(pl.multiple_of(z * rows, rows), rows)], lsem.at[a])
        st.start()

    def has(dist, right):
        return z - dist >= 0 if right else z + dist <= nz - 1

    def zstep(dist):
        for a in (1, 0):
            for right in (True, False):
                k = 0 if right else 1

                def got(a=a, right=right, k=k):
                    zrecv(a, dist, right).wait_recv()
                    if dist < nz - 1:
                        when(can[right], lambda: zsend(a, dist, right).start())
                    for d in range(1, nx):
                        xcopy(a, k, dist, d, right, True).start()
                    if a == 1 and split:
                        ycopy(k, dist, 0, right, True).start()
                    ccopy(a, k, dist, 0, right, True).start()

                when(has(dist, right), got)

    def xstep(dist):
        for a in (1, 0):
            for right in (True, False):
                k = 0 if right else 1

                def got(a=a, right=right, k=k):
                    for d in range(1, nx):
                        xcopy(a, k, dist, d, right, False).wait_recv()
                        if a == 1 and split:
                            ycopy(k, dist, d, right, True).start()
                        ccopy(a, k, dist, d, right, True).start()

                when(has(dist, right), got)

    def ystep(dist, ds):
        if not split or dist < 1:
            return
        for right in (True, False):
            k = 0 if right else 1

            def got(right=right, k=k):
                for d in ds:
                    ycopy(k, dist, d, right, False).wait_recv()
                    fcopy(k, dist, d, right, True).start()

            when(has(dist, right), got)

    far = tuple(range(1, nx))
    for dist in range(1, nz):
        zstep(dist)
        if dist > 1:
            xstep(dist - 1)
        ystep(dist - 1, (0,))
        ystep(dist - 2, far)
    ystep(nz - 2, far)
    ystep(nz - 1, (0,))
    xstep(nz - 1)
    ystep(nz - 1, far)

    for a in range(2):
        pltpu.make_async_copy(
            stage.at[a], out[a].at[pl.ds(pl.multiple_of(z * rows, rows), rows)], lsem.at[a]).wait()
    for dist in range(0, nz):
        for a in range(2):
            for right in (True, False):
                k = 0 if right else 1
                if dist < nz - 1:
                    cond = can[right] if dist == 0 else has(dist, right) & can[right]
                    when(cond, lambda a=a, right=right: zsend(a, dist, right).wait_send())
                if dist > 0:
                    def fin(a=a, right=right, k=k):
                        for d in range(1, nx):
                            xcopy(a, k, dist, d, right, True).wait_send()
                        for d in range(nx):
                            ccopy(a, k, dist, d, right, True).wait_send()
                            ccopy(a, k, dist, d, right, False).wait_recv()
                            if a == 1 and split:
                                ycopy(k, dist, d, right, True).wait_send()
                                fcopy(k, dist, d, right, True).wait_send()
                                fcopy(k, dist, d, right, False).wait_recv()
                    when(has(dist, right), fin)


def gather_inputs(nuc, loc, nz, nm):
    rows, width = nuc.shape
    nx = nm // 2
    dma = pltpu.SemaphoreType.DMA
    anyspec = pl.BlockSpec(memory_space=pl.ANY)
    shape = jax.ShapeDtypeStruct((nz * rows, width), bf16)
    ex = (2, nz - 1, nx) if halves(rows, nm) else (1,)
    return pl.pallas_call(
        functools.partial(gather_kernel, nz, nm),
        out_shape=(shape, shape),
        in_specs=[anyspec] * 2,
        out_specs=[anyspec] * 2,
        scratch_shapes=[
            pltpu.VMEM((2, rows, width), bf16),
            dma((2,)),
            dma((2, 2, nz)), dma((2, 2, nz)),
            dma((2, 2, nz - 1, nx)), dma((2, 2, nz - 1, nx)),
            dma((2, 2, nz - 1, nx)), dma((2, 2, nz - 1, nx)),
            dma(ex), dma(ex), dma(ex), dma(ex),
        ],
        compiler_params=pltpu.CompilerParams(collective_id=0, has_side_effects=True),
        name="gather_inputs",
    )(nuc, loc)


def attend_kernel(nz, nm, heads, qk, vd, sharp, nuc, loc, gain, wqk, wv, mix, out, mix_all,
                  q_s, k_s, v_s, xs, xr, ys, yr, cs, cr, os, orr):
    share_mix(nz, nm, mix, mix_all, xs, xr, ys, yr, cs, cr, os, orr, 0)
    t, j = pl.program_id(0), pl.program_id(1)
    z = lax.axis_index("seq")
    rows = nuc.shape[0]
    b = 128

    def body(flip):
        r_i = lax.broadcasted_iota(jnp.int32, (b, b), 0)
        c_i = lax.broadcasted_iota(jnp.int32, (b, b), 1)
        anti = jnp.where(r_i + c_i == b - 1, 1.0, 0.0).astype(bf16)
        parts = []
        nb = rows // b
        for i in range(nb):
            if flip:
                l = jnp.dot(anti, loc[(nb - 1 - i) * b:(nb - i) * b, :], preferred_element_type=f32)
            else:
                l = loc[i * b:(i + 1) * b, :].astype(f32)
            s = nuc[i * b:(i + 1) * b, :].astype(f32) + l
            parts.append((normalize(s) * gain[...]).astype(bf16))
        normed = jnp.concatenate(parts, axis=0)
        here = pl.ds(pl.multiple_of(j * rows, rows), rows)
        key = jnp.dot(normed, wqk[1], preferred_element_type=f32)
        for h in range(heads):
            k_s[here, h * qk:(h + 1) * qk] = normalize(key[:, h * qk:(h + 1) * qk]).astype(bf16)
        v_s[here, :] = jnp.dot(normed, wv[...], preferred_element_type=f32).astype(bf16)

        @pl.when(j == z)
        def _():
            query = jnp.dot(normed, wqk[0], preferred_element_type=f32)
            for h in range(heads):
                q_s[:, h * qk:(h + 1) * qk] = normalize(query[:, h * qk:(h + 1) * qk]).astype(bf16)

    @pl.when(t == 0)
    def _():
        body(False)

    @pl.when(t == 1)
    def _():
        body(True)

    @pl.when(j == nz - 1)
    def _():
        s_all = k_s.shape[0]
        chunk = 128
        wide = heads * vd
        for i in range(rows // chunk):
            rr = slice(i * chunk, (i + 1) * chunk)
            if i == 1:
                share_mix(nz, nm, mix, mix_all, xs, xr, ys, yr, cs, cr, os, orr, 2)
            res = []
            for h in range(heads):
                lo = (h * vd) // 128 * 128
                hi = min(-(-((h + 1) * vd) // 128) * 128, wide)
                num = jnp.zeros((chunk, hi - lo), f32)
                tot = jnp.zeros((chunk, 1), f32)
                step = 1536
                for kk in range(0, s_all, step):
                    sc = lax.dot_general(
                        q_s[rr, h * qk:(h + 1) * qk], k_s[kk:kk + step, h * qk:(h + 1) * qk],
                        (((1,), (1,)), ((), ())), preferred_element_type=f32)
                    w = jnp.exp(sc * (sharp[h] / qk))
                    tot = tot + jnp.sum(w, axis=-1, keepdims=True)
                    num = num + jnp.dot(w.astype(bf16), v_s[kk:kk + step, lo:hi],
                                        preferred_element_type=f32)
                res.append((lo, hi, num / tot))
            if heads == 1:
                out[rr, :] = res[0][2].astype(bf16)
            else:
                for lo in range(0, wide, 128):
                    hi = min(lo + 128, wide)
                    col = lo + lax.broadcasted_iota(jnp.int32, (chunk, hi - lo), 1)
                    val = None
                    for h in range(heads):
                        l0, h0, r = res[h]
                        if h * vd < hi and (h + 1) * vd > lo:
                            v = r[:, lo - l0:hi - l0]
                            val = v if val is None else jnp.where(col < h * vd, val, v)
                    out[rr, lo:hi] = val.astype(bf16)

    share_mix(nz, nm, mix, mix_all, xs, xr, ys, yr, cs, cr, os, orr, 1)


def share_mix(nz, nm, mix, mix_all, xs, xr, ys, yr, cs, cr, os, orr, phase):
    nx = nm // 2
    step = pl.program_id(0) * nz + pl.program_id(1)
    m = lax.axis_index("mp")
    g = lax.axis_index("groups")
    x, c = m // 2, m % 2
    n = 4 if mix.shape[0] % 128 == 0 else 2
    size = mix.shape[0] // (2 * n)

    def rows(gg, p):
        return pl.ds(pl.multiple_of((gg * n + p) * size, size), size)

    def xcopy(p, d, mine):
        o = lax.rem(x + d, nx) if mine else lax.rem(x - d + nx, nx)
        k = m if mine else o * 2 + c
        return pltpu.make_async_remote_copy(
            src_ref=mix.at[rows(g, p)], dst_ref=mix_all.at[k, rows(g, p)],
            send_sem=xs.at[p, d - 1], recv_sem=xr.at[p, d - 1],
            device_id={"mp": o * 2 + c}, device_id_type=MESH)

    def ycopy(p, d, mine):
        k = lax.rem(x - d + nx, nx) * 2 + c
        r = rows(g if mine else 1 - g, p)
        return pltpu.make_async_remote_copy(
            src_ref=mix_all.at[k, r], dst_ref=mix_all.at[k, r],
            send_sem=ys.at[p, d - 1], recv_sem=yr.at[p, d - 1],
            device_id={"groups": 1 - g}, device_id_type=MESH)

    def ccopy(p, d, far, mine):
        k = lax.rem(x - d + nx, nx) * 2 + (c if mine else 1 - c)
        r = rows(1 - g if far else g, p)
        f = 1 if far else 0
        return pltpu.make_async_remote_copy(
            src_ref=mix_all.at[k, r], dst_ref=mix_all.at[k, r],
            send_sem=cs.at[p, d - 1, f], recv_sem=cr.at[p, d - 1, f],
            device_id={"mp": x * 2 + 1 - c}, device_id_type=MESH)

    def own(mine):
        return pltpu.make_async_remote_copy(
            src_ref=mix, dst_ref=mix_all.at[m if mine else x * 2 + 1 - c],
            send_sem=os, recv_sem=orr,
            device_id={"mp": x * 2 + 1 - c}, device_id_type=MESH)

    def pass_on(p):
        for d in range(1, nx):
            xcopy(p, d, False).wait_recv()
            ycopy(p, d, True).start()
            ccopy(p, d, False, True).start()

    def bring(p):
        for d in range(1, nx):
            ycopy(p, d, False).wait_recv()
            ccopy(p, d, True, True).start()

    if phase == 0:
        @pl.when(step == 0)
        def _():
            barrier = pltpu.get_barrier_semaphore()
            for d in range(1, nx):
                pl.semaphore_signal(barrier, inc=1, device_id={"mp": lax.rem(x + d, nx) * 2 + c}, device_id_type=MESH)
            pl.semaphore_signal(barrier, inc=1, device_id={"mp": x * 2 + 1 - c}, device_id_type=MESH)
            pl.semaphore_signal(barrier, inc=1, device_id={"groups": 1 - g}, device_id_type=MESH)
            pl.semaphore_wait(barrier, nx + 1)
            for p in range(n):
                for d in range(1, nx):
                    xcopy(p, d, True).start()
            own(True).start()

        turns = {4: (nz - 1, None, nz, nz + 2), 2: (nz, nz + 2)}[n]
        for p in range(n):
            if turns[p] is not None:
                pl.when(step == turns[p])(functools.partial(pass_on, p))

        @pl.when(step == 2 * nz - 1)
        def _():
            for p in range(n // 2):
                bring(p)
    elif phase == 2:
        if n == 4:
            pl.when(step == nz - 1)(functools.partial(pass_on, 1))
    else:
        @pl.when(step == 2 * nz - 1)
        def _():
            for p in range(n // 2, n):
                bring(p)
            own(True).wait_send()
            own(False).wait_recv()
            for p in range(n):
                for d in range(1, nx):
                    xcopy(p, d, True).wait_send()
                    ycopy(p, d, True).wait_send()
                    for far in (False, True):
                        ccopy(p, d, far, True).wait_send()
                        ccopy(p, d, far, False).wait_recv()


def attend(nuc_all, loc_all, gain, wqk, wv, sharp, mix, nz, nm, rows):
    heads = sharp.shape[0]
    width = nuc_all.shape[1]
    qk = wqk.shape[2] // heads
    vd = wv.shape[1] // heads
    s_all = nuc_all.shape[0]
    nx = nm // 2
    dma = pltpu.SemaphoreType.DMA
    full = lambda a: pl.BlockSpec(a.shape, lambda t, j: (0,) * a.ndim, pipeline_mode=pl.Buffered(1))
    anyspec = pl.BlockSpec(memory_space=pl.ANY)
    gain = gain.reshape(1, width)
    return pl.pallas_call(
        functools.partial(attend_kernel, nz, nm, heads, qk, vd),
        grid=(2, nz),
        out_shape=(jax.ShapeDtypeStruct((2, rows, heads * vd), bf16),
                   jax.ShapeDtypeStruct((nm,) + mix.shape, bf16)),
        in_specs=[
            pl.BlockSpec(memory_space=pltpu.SMEM),
            pl.BlockSpec((rows, width), lambda t, j: (j, 0)),
            pl.BlockSpec((rows, width), lambda t, j: (t * (nz - 1 - j) + (1 - t) * j, 0)),
            full(gain), full(wqk), full(wv), anyspec,
        ],
        out_specs=(pl.BlockSpec((pl.Squeezed(), rows, heads * vd), lambda t, j: (t, 0, 0)), anyspec),
        scratch_shapes=[
            pltpu.VMEM((rows, heads * qk), bf16),
            pltpu.VMEM((s_all, heads * qk), bf16),
            pltpu.VMEM((s_all, heads * vd), bf16),
            dma((4, nx)), dma((4, nx)), dma((4, nx)), dma((4, nx)),
            dma((4, nx, 2)), dma((4, nx, 2)), dma, dma,
        ],
        compiler_params=pltpu.CompilerParams(
            collective_id=2, has_side_effects=True, vmem_limit_bytes=56 << 20),
        name="attend",
    )(sharp, nuc_all, loc_all, gain, wqk, wv, mix)


def tail_kernel(nz, nm, att, nuc_h, loc_h, loc_all, gain, mix, mix_all, widen_h, narrow_h, out,
                att_all, nuc, loc, locm, mixv, widen, narrow, sbuf, rbuf, mid,
                lsem, msem, xs, xr, cs, cr, ss, sr):
    nx = nm // 2
    rows, width = nuc.shape
    share = width // nm
    b = 128
    parts = rows // b
    z = lax.axis_index("seq")
    m = lax.axis_index("mp")
    x, c = m // 2, m % 2
    barrier = pltpu.get_barrier_semaphore()
    for d in range(1, nm):
        pl.semaphore_signal(barrier, inc=1, device_id={"mp": lax.rem(m + d, nm)}, device_id_type=MESH)
    loads = [
        pltpu.make_async_copy(att, att_all.at[m], lsem.at[0]),
        pltpu.make_async_copy(nuc_h, nuc, lsem.at[1]),
        pltpu.make_async_copy(loc_h, loc, lsem.at[2]),
        pltpu.make_async_copy(loc_all.at[pl.ds(pl.multiple_of((nz - 1 - z) * rows, rows), rows)], locm, lsem.at[3]),
        pltpu.make_async_copy(widen_h, widen, lsem.at[4]),
        pltpu.make_async_copy(narrow_h, narrow, lsem.at[5]),
    ]
    mloads = [pltpu.make_async_copy(mix, mixv.at[m], msem.at[0])]
    for d in range(1, nm):
        k = lax.rem(m + d, nm)
        mloads.append(pltpu.make_async_copy(mix_all.at[k], mixv.at[k], msem.at[d]))
    for cp in loads[:4] + mloads + loads[4:]:
        cp.start()
    pl.semaphore_wait(barrier, nm - 1)

    def xcopy(i, d, mine):
        o = lax.rem(x + d, nx) if mine else lax.rem(x - d + nx, nx)
        k = m if mine else o * 2 + c
        r = pl.ds(i * b, b)
        return pltpu.make_async_remote_copy(
            src_ref=att.at[:, r], dst_ref=att_all.at[k, :, r], send_sem=xs.at[i, d - 1],
            recv_sem=xr.at[i, d - 1], device_id={"mp": o * 2 + c}, device_id_type=MESH)

    def ccopy(i, d, mine):
        o = lax.rem(x - d + nx, nx)
        k = o * 2 + (c if mine else 1 - c)
        r = pl.ds(i * b, b)
        ref = att.at[:, r] if d == 0 else att_all.at[k, :, r]
        return pltpu.make_async_remote_copy(
            src_ref=ref, dst_ref=att_all.at[k, :, r], send_sem=cs.at[i, d], recv_sem=cr.at[i, d],
            device_id={"mp": x * 2 + 1 - c}, device_id_type=MESH)

    def scopy(i, d):
        k = lax.rem(m + d, nm)
        return pltpu.make_async_remote_copy(
            src_ref=sbuf.at[i, k], dst_ref=rbuf.at[i, d - 1], send_sem=ss.at[i, d - 1],
            recv_sem=sr.at[i, d - 1], device_id={"mp": k}, device_id_type=MESH)

    for i in range(parts):
        for d in range(1, nx):
            xcopy(i, d, True).start()
        ccopy(i, 0, True).start()

    def pass_on(i):
        for d in range(1, nx):
            xcopy(i, d, False).wait_recv()
            ccopy(i, d, True).start()

    r_i = lax.broadcasted_iota(jnp.int32, (b, b), 0)
    c_i = lax.broadcasted_iota(jnp.int32, (b, b), 1)
    anti = jnp.where(r_i + c_i == b - 1, 1.0, 0.0).astype(bf16)
    for cp in loads[:4]:
        cp.wait()
    pass_on(0)
    for cp in mloads:
        cp.wait()
    for i in range(parts):
        r = slice(i * b, (i + 1) * b)
        n = nuc[r, :].astype(f32)
        s0 = n + loc[r, :].astype(f32)
        s1 = n + jnp.dot(anti, locm[(parts - 1 - i) * b:(parts - i) * b, :], preferred_element_type=f32)
        middle = jnp.concatenate([s0, s1], axis=0)
        for d in range(nx):
            ccopy(i, d, False).wait_recv()
        for k in range(nm):
            a = jnp.concatenate([att_all[k, 0, r, :], att_all[k, 1, r, :]], axis=0)
            middle = middle + jnp.dot(a, mixv[k], preferred_element_type=f32)
        if i + 1 < parts:
            pass_on(i + 1)
        normed = (normalize(middle) * gain[...]).astype(bf16)
        if i == 0:
            for cp in loads[4:]:
                cp.wait()
        up = jax.nn.gelu(jnp.dot(normed, widen[...], preferred_element_type=f32), approximate=True)
        both = (up[:b] + up[b:]).astype(bf16)
        down = jnp.dot(both, narrow[...], preferred_element_type=f32)
        total = middle[:b] + middle[b:] + down
        down = down.astype(bf16)
        for k in range(nm):
            sbuf[i, k] = down[:, k * share:(k + 1) * share]
            mid[i, k] = total[:, k * share:(k + 1) * share]
        for d in range(1, nm):
            scopy(i, d).start()
    for i in range(parts):
        acc = mid[i, m]
        for d in range(1, nm):
            scopy(i, d).wait_recv()
            acc = acc + rbuf[i, d - 1].astype(f32)
        out[i * b:(i + 1) * b, :] = 0.5 * acc
    for i in range(parts):
        for d in range(1, nx):
            xcopy(i, d, True).wait_send()
        for d in range(nx):
            ccopy(i, d, True).wait_send()
        for d in range(1, nm):
            scopy(i, d).wait_send()


def tail(att, nuc, loc, loc_all, gain, mix, mix_all, widen, narrow, nz, nm):
    rows, width = nuc.shape
    share = width // nm
    nx = nm // 2
    parts = rows // 128
    dma = pltpu.SemaphoreType.DMA
    anyspec = pl.BlockSpec(memory_space=pl.ANY)
    vm = pl.BlockSpec(memory_space=pltpu.VMEM)
    v = pltpu.VMEM
    return pl.pallas_call(
        functools.partial(tail_kernel, nz, nm),
        out_shape=jax.ShapeDtypeStruct((rows, share), f32),
        in_specs=[vm, anyspec, anyspec, anyspec, vm, anyspec, anyspec, anyspec, anyspec],
        out_specs=vm,
        scratch_shapes=[
            v((nm,) + att.shape, bf16), v(nuc.shape, bf16), v(nuc.shape, bf16), v(nuc.shape, bf16),
            v((nm,) + mix.shape, bf16), v(widen.shape, bf16), v(narrow.shape, bf16),
            v((parts, nm, 128, share), bf16), v((parts, nm - 1, 128, share), bf16),
            v((parts, nm, 128, share), f32),
            dma((6,)), dma((nm,)),
            dma((parts, nx)), dma((parts, nx)), dma((parts, nx)), dma((parts, nx)),
            dma((parts, nm)), dma((parts, nm)),
        ],
        compiler_params=pltpu.CompilerParams(
            collective_id=3, has_side_effects=True, vmem_limit_bytes=56 << 20),
        name="tail",
    )(att, nuc, loc, loc_all, gain.reshape(1, width), mix, mix_all, widen, narrow)


def fused(nz, nm, heads, qk, vd, rows):
    return nz == 4 and nm == 4 and heads == 2 and qk == 128 and vd == 192 and rows % 128 == 0


def block_kernel(nz, nm, sharp, gain1, gain2, nuc_h, loc_h, wqk_h, wv_h, mix_h, widen_h, narrow_h, out,
                 nuc, loc, locm, rloc, nbuf, raw, stage, far, wown, wpart, pq, pk, pv, qbuf, kbuf, vbuf,
                 asend, att, abuf, mixv, widen, narrow, mids, downs, sbuf, rbuf, xbuf, fbuf,
                 lsem, wsem, ms, mr, xs, xr, fs, fr, qs, qr, rs, rr, rl, hs, hr, ss, sr):
    rows, width = nuc.shape
    share = width // nm
    b = 128
    hb = b // 2
    parts = rows // b
    quarter = rows // nm
    depth = mix_h.shape[0]
    g = lax.axis_index("groups")
    z = lax.axis_index("seq")
    m = lax.axis_index("mp")
    x, c = m // 2, m % 2
    t_me, h_me = z // 2, z % 2
    lower, upper_half = z < nz // 2, z >= nz // 2
    mirror, twin = nz - 1 - z, z + 1 - 2 * lax.rem(z, 2)
    m_x = (1 - x) * 2 + c
    to_x = {"mp": m_x}
    to_y = {"groups": 1 - g}
    to_d = {"groups": 1 - g, "mp": m_x}
    to_c = {"mp": x * 2 + 1 - c}

    def remote(src, dst, ssem, rsem, dev):
        return pltpu.make_async_remote_copy(
            src_ref=src, dst_ref=dst, send_sem=ssem, recv_sem=rsem, device_id=dev, device_id_type=MESH)

    barrier = pltpu.get_barrier_semaphore()
    for d in range(1, nz):
        pl.semaphore_signal(barrier, inc=1, device_id={"seq": lax.rem(z + d, nz)}, device_id_type=MESH)
    for d in range(1, nm):
        pl.semaphore_signal(barrier, inc=1, device_id={"mp": lax.rem(m + d, nm)}, device_id_type=MESH)
    pl.semaphore_signal(barrier, inc=1, device_id=to_y, device_id_type=MESH)
    pl.semaphore_signal(barrier, inc=1, device_id=to_d, device_id_type=MESH)

    loads = [
        pltpu.make_async_copy(nuc_h, nuc, lsem.at[0]),
        pltpu.make_async_copy(loc_h, loc, lsem.at[1]),
        pltpu.make_async_copy(widen_h, widen, lsem.at[2]),
        pltpu.make_async_copy(narrow_h, narrow, lsem.at[3]),
        pltpu.make_async_copy(mix_h, mixv.at[pl.ds(pl.multiple_of(m * depth, depth), depth)], lsem.at[4]),
    ]
    wloads = []
    for k, (w, h) in enumerate(((wown, h_me), (wpart, 1 - h_me))):
        col = pl.ds(pl.multiple_of(h * b, b), b)
        wide = pl.ds(pl.multiple_of(h * 2 * b, b), b)
        wloads += [
            pltpu.make_async_copy(wqk_h.at[0, :, col], w.at[:, 0:b], wsem.at[k, 0]),
            pltpu.make_async_copy(wqk_h.at[1, :, col], w.at[:, b:2 * b], wsem.at[k, 1]),
            pltpu.make_async_copy(wv_h.at[:, wide], w.at[:, 2 * b:3 * b], wsem.at[k, 2]),
            pltpu.make_async_copy(wv_h.at[:, b:2 * b], w.at[:, 3 * b:4 * b], wsem.at[k, 3]),
        ]
    for cp in loads[:2] + wloads:
        cp.start()

    sl = rows // 8

    def piece(xx, gg, cc):
        return pl.ds(pl.multiple_of(((xx * 2 + gg) * 2 + cc) * sl, sl), sl)

    def loc_z():
        return remote(loc_h.at[piece(x, g, c)], locm.at[piece(x, g, c)], ms.at[0], mr.at[0], {"seq": mirror})

    def loc_on(k):
        r = locm.at[piece(x, g, c)]
        return remote(r, r, ms.at[1 + k], mr.at[1 + k], (to_x, to_y, to_d)[k])

    def loc_c(k):
        r = locm.at[piece(x if k % 2 == 0 else 1 - x, g if k < 2 else 1 - g, c)]
        return remote(r, r, ms.at[4 + k], mr.at[4 + k], to_c)

    size = depth // 4

    def mrows(mm, gg, p):
        return pl.ds(pl.multiple_of(mm * depth + (gg * 2 + p) * size, size), size)

    def mix_x(p):
        return remote(mix_h.at[mrows(0, g, p)], mixv.at[mrows(m, g, p)], xs.at[p], xr.at[p], to_x)

    def mix_y(p):
        r = mixv.at[mrows(m_x, g, p)]
        return remote(r, r, xs.at[2 + p], xr.at[2 + p], to_y)

    def mix_c(p, far_side):
        r = mixv.at[mrows(m_x, 1 - g if far_side else g, p)]
        k = (6 if far_side else 4) + p
        return remote(r, r, xs.at[k], xr.at[k], to_c)

    def mix_own():
        return remote(mix_h, mixv.at[pl.ds(pl.multiple_of(m * depth, depth), depth)], xs.at[8], xr.at[8], to_c)

    mine = pl.ds(pl.multiple_of(m * quarter, quarter), quarter)
    theirs = pl.ds(pl.multiple_of(m_x * quarter, quarter), quarter)
    j_near = lax.rem(mirror, 2)

    def far_raw():
        return remote(nuc_h.at[mine], raw, fs.at[0], fr.at[0], {"seq": mirror})

    def far_normed():
        return remote(stage, far.at[lax.rem(z, 2), mine], fs.at[0], fr.at[0], {"seq": mirror})

    def far_twin():
        r = far.at[j_near, mine]
        return remote(r, r, fs.at[1], fr.at[1], {"seq": twin})

    def far_x(k):
        r = far.at[j_near if k == 0 else 1 - j_near, mine]
        return remote(r, r, fs.at[2 + k], fr.at[2 + k], to_x)

    def far_c(k, q):
        r = far.at[j_near if k == 0 else 1 - j_near, mine if q == 0 else theirs]
        i = 4 + k * 2 + q
        return remote(r, r, fs.at[i], fr.at[i], to_c)

    pl.semaphore_wait(barrier, nz + nm)

    @pl.when(lower)
    def _():
        loc_z().start()
        mix_x(1).start()

    mix_x(0).start()
    mix_own().start()
    for cp in loads[2:]:
        cp.start()

    def turn(n):
        r_i = lax.broadcasted_iota(jnp.int32, (n, n), 0)
        c_i = lax.broadcasted_iota(jnp.int32, (n, n), 1)
        return jnp.where(r_i + c_i == n - 1, 1.0, 0.0).astype(bf16)

    low = lax.broadcasted_iota(jnp.int32, (hb, b), 1) < hb
    low_all = lax.broadcasted_iota(jnp.int32, (rows, b), 1) < hb

    def chunk(i):
        return slice(i * b, (i + 1) * b)

    def block_rows(blk):
        return pl.ds(pl.multiple_of(blk * rows, rows), rows)

    def twice(tile, h):
        return jnp.where(low_all == (h == 0), tile, pltpu.roll(tile, hb, 1)).astype(bf16)

    def sent(k):
        src, dst = ((pq, qbuf), (pk, kbuf), (pv, vbuf))[k]
        return remote(src, dst.at[block_rows(z)], qs.at[k], qr.at[k], {"seq": twin})

    def project_own(other):
        for i in range(parts):
            s = nuc[chunk(i), :].astype(f32) + other[chunk(i), :].astype(f32)
            nbuf[chunk(i), :] = (normalize(s) * gain1[...]).astype(bf16)
        p = jnp.dot(nbuf[...], wpart[...], preferred_element_type=f32)
        pq[...] = normalize(p[:, 0:b]).astype(bf16)
        pk[...] = normalize(p[:, b:2 * b]).astype(bf16)
        pv[:, 0:b] = p[:, 2 * b:3 * b].astype(bf16)
        pv[:, b:2 * b] = twice(p[:, 3 * b:4 * b], 1 - h_me)
        for k in range(3):
            sent(k).start()
        keep(nbuf[...], z)

    def keep(normed, blk):
        p = jnp.dot(normed, wown[...], preferred_element_type=f32)
        r = block_rows(blk)
        qbuf[r, :] = normalize(p[:, 0:b]).astype(bf16)
        kbuf[r, :] = normalize(p[:, b:2 * b]).astype(bf16)
        vbuf[r, 0:b] = p[:, 2 * b:3 * b].astype(bf16)
        vbuf[r, b:2 * b] = twice(p[:, 3 * b:4 * b], h_me)

    def att_send(blk, i):
        return remote(asend.at[blk, i], att.at[m, t_me, i, h_me], rs.at[blk, i], rr.at[t_me, h_me, i], {"seq": blk})

    def att_keep(i):
        return pltpu.make_async_copy(asend.at[z, i], att.at[m, t_me, i, h_me], rl.at[i])

    def attend():
        mask = low == (h_me == 0)
        scale = sharp[h_me] * (1.4426950408889634 / b)
        order = [mirror, nz - 1 - twin, twin, z]

        def step(i, carry):
            for s in range(nz):
                blk = order[s]
                q = qbuf[pl.ds(pl.multiple_of(blk * rows + i * b, b), b), :]
                sc = lax.dot_general(q, kbuf[...], (((1,), (1,)), ((), ())), preferred_element_type=f32)
                w = jnp.exp2(sc * scale)
                tot = jnp.sum(w, axis=-1, keepdims=True)
                res = jnp.dot(w.astype(bf16), vbuf[...], preferred_element_type=f32) / tot
                asend[blk, i, 0:b, :] = res[:, :b].astype(bf16)
                asend[blk, i, b:b + hb, :] = jnp.where(mask, res[:hb, b:], res[hb:, b:]).astype(bf16)
                if s < nz - 1:
                    att_send(blk, i).start()
                else:
                    att_keep(i).start()
            return carry

        lax.fori_loop(0, parts, step, 0)

    def share_x(t, i):
        r = att.at[m, t, i]
        return remote(r, r, hs.at[t, i, 0], hr.at[t, i, 0], to_x)

    def share_c(t, i, k):
        r = att.at[m if k == 0 else m_x, t, i]
        return remote(r, r, hs.at[t, i, 1 + k], hr.at[t, i, 1 + k], to_c)

    def relay(t, i):
        for h in range(2):
            src = 2 * t + h

            @pl.when(z != src)
            def _():
                r = att.at[m, t, i, h]
                remote(r, r, rs.at[0, i], rr.at[t, h, i], {"seq": src}).wait_recv()

            @pl.when(z == src)
            def _():
                att_keep(i).wait()
        share_x(t, i).start()
        share_c(t, i, 0).start()

    def relay_c(t, i):
        share_x(t, i).wait_recv()
        share_c(t, i, 1).start()

    def gather(t, i):
        for k in range(2):
            share_c(t, i, k).wait_recv()
        r0 = t * b
        for k in range(nm):
            f0, f1 = att[k, t, i, 0, b:b + hb, :].astype(f32), att[k, t, i, 1, b:b + hb, :].astype(f32)
            lo = k * 3 * b
            abuf[r0:r0 + b, lo:lo + b] = att[k, t, i, 0, 0:b, :]
            abuf[r0:r0 + hb, lo + b:lo + 2 * b] = jnp.where(low, f0, f1).astype(bf16)
            abuf[r0 + hb:r0 + b, lo + b:lo + 2 * b] = pltpu.roll(jnp.where(low, f1, f0), hb, 1).astype(bf16)
            abuf[r0:r0 + b, lo + 2 * b:lo + 3 * b] = att[k, t, i, 1, 0:b, :]

    def pair_copy(i):
        return remote(sbuf.at[i, 1 - c], rbuf.at[i], ss.at[i, 0], sr.at[i, 0], to_c)

    def sum_copy(i):
        return remote(xbuf.at[i], fbuf.at[i], ss.at[i, 1], sr.at[i, 1], to_x)

    def pass_sum(i):
        pair_copy(i).wait_recv()
        xbuf[i] = (downs[i, c, 1 - x] + rbuf[i, 1 - x].astype(f32)).astype(bf16)
        sum_copy(i).start()

    def loc_begin():
        loc_z().wait_recv()
        for k in (2, 0, 1):
            loc_on(k).start()
        loc_c(0).start()

    def loc_end():
        for k in range(3):
            loc_on(k).wait_recv()
            loc_c(k + 1).start()

    def loc_turn():
        for k in range(4):
            loc_c(k).wait_recv()
        for i in range(parts):
            rloc[chunk(i), :] = jnp.dot(
                turn(b), locm[chunk(parts - 1 - i), :], preferred_element_type=f32).astype(bf16)

    for cp in loads[:2]:
        cp.wait()

    @pl.when(upper_half)
    def _():
        s = nuc[mine, :].astype(f32) + loc[mine, :].astype(f32)
        stage[...] = (normalize(s) * gain1[...]).astype(bf16)
        far_normed().start()
        loc_z().start()

    for cp in wloads:
        cp.wait()

    @pl.when(lower)
    def _():
        far_raw().start()
        project_own(loc)

    @pl.when(upper_half)
    def _():
        loc_begin()
        loc_end()
        mix_x(1).start()
        loc_turn()
        project_own(rloc)

    far_raw().wait_recv()

    @pl.when(upper_half)
    def _():
        back = pl.ds(pl.multiple_of((nm - 1 - m) * quarter, quarter), quarter)
        l = jnp.dot(turn(quarter), loc[back, :], preferred_element_type=f32)
        far[j_near, mine, :] = (normalize(raw[...].astype(f32) + l) * gain1[...]).astype(bf16)

    far_twin().start()
    far_x(0).start()
    far_c(0, 0).start()
    mix_x(0).wait_recv()
    mix_y(0).start()
    mix_c(0, False).start()
    far_twin().wait_recv()
    far_x(1).start()
    far_c(1, 0).start()
    mix_x(1).wait_recv()
    mix_y(1).start()
    mix_c(1, False).start()
    pl.when(lower)(loc_begin)
    for k in range(2):
        far_x(k).wait_recv()
        far_c(k, 1).start()
    for k in range(2):
        for q in range(2):
            far_c(k, q).wait_recv()
        j = j_near if k == 0 else 1 - j_near
        keep(far[j], (1 - t_me) * 2 + j)
    mix_y(0).wait_recv()
    mix_c(0, True).start()
    for k in range(3):
        sent(k).wait_recv()
    attend()

    @pl.when(lower)
    def _():
        loc_end()
        loc_turn()

    relay(0, 0)
    relay(1, 0)
    mix_y(1).wait_recv()
    mix_c(1, True).start()
    for i in range(parts):
        if i + 1 < parts:
            for t in range(2):
                relay(t, i + 1)
        for t in range(2):
            relay_c(t, i)
        if i == 0:
            mix_own().wait_recv()
            for p in range(2):
                for far_side in (False, True):
                    mix_c(p, far_side).wait_recv()
            for cp in loads[2:]:
                cp.wait()
        else:
            pass_sum(i - 1)
        for t in range(2):
            gather(t, i)
        n = nuc[chunk(i), :].astype(f32)
        mid = jnp.concatenate([n + loc[chunk(i), :].astype(f32), n + rloc[chunk(i), :].astype(f32)], axis=0)
        mid = mid + jnp.dot(abuf[...], mixv[...], preferred_element_type=f32)
        normed = (normalize(mid) * gain2[...]).astype(bf16)
        up = jax.nn.gelu(jnp.dot(normed, widen[...], preferred_element_type=f32), approximate=True)
        both = (up[:b] + up[b:]).astype(bf16)
        down = jnp.dot(both, narrow[...], preferred_element_type=f32)
        total = mid[:b] + mid[b:] + down
        for k in range(nm):
            cols = slice(k * share, (k + 1) * share)
            sbuf[i, k % 2, k // 2] = down[:, cols].astype(bf16)
            downs[i, k % 2, k // 2] = down[:, cols]
            mids[i, k] = total[:, cols]
        pair_copy(i).start()
    pass_sum(parts - 1)
    for i in range(parts):
        sum_copy(i).wait_recv()
        out[chunk(i), :] = 0.5 * (mids[i, m] + rbuf[i, x].astype(f32) + fbuf[i].astype(f32))

    loc_z().wait_send()
    for k in range(3):
        loc_on(k).wait_send()
        sent(k).wait_send()
    for k in range(4):
        loc_c(k).wait_send()
    far_raw().wait_send()
    far_twin().wait_send()
    for k in range(2):
        far_x(k).wait_send()
        for q in range(2):
            far_c(k, q).wait_send()
    mix_own().wait_send()
    for p in range(2):
        mix_x(p).wait_send()
        mix_y(p).wait_send()
        for far_side in (False, True):
            mix_c(p, far_side).wait_send()
    for i in range(parts):
        for t in range(2):
            share_x(t, i).wait_send()
            for k in range(2):
                share_c(t, i, k).wait_send()
        for blk in range(nz):
            @pl.when(z != blk)
            def _():
                att_send(blk, i).wait_send()
        pair_copy(i).wait_send()
        sum_copy(i).wait_send()


def block(nuc, loc, premix, wqk, wv, sharp, mix, premlp, widen, narrow, nz, nm):
    rows, width = nuc.shape
    parts = rows // 128
    share = width // nm
    every = nz * rows
    dma = pltpu.SemaphoreType.DMA
    anyspec = pl.BlockSpec(memory_space=pl.ANY)
    vm = pl.BlockSpec(memory_space=pltpu.VMEM)
    v = pltpu.VMEM
    return pl.pallas_call(
        functools.partial(block_kernel, nz, nm),
        out_shape=jax.ShapeDtypeStruct((rows, share), f32),
        in_specs=[pl.BlockSpec(memory_space=pltpu.SMEM), vm, vm] + [anyspec] * 7,
        out_specs=vm,
        scratch_shapes=[
            v(nuc.shape, bf16), v(nuc.shape, bf16), v(nuc.shape, bf16), v(nuc.shape, bf16), v(nuc.shape, bf16),
            v((rows // nm, width), bf16), v((rows // nm, width), bf16), v((2, rows, width), bf16),
            v((width, 512), bf16), v((width, 512), bf16),
            v((rows, 128), bf16), v((rows, 128), bf16), v((rows, 256), bf16),
            v((every, 128), bf16), v((every, 128), bf16), v((every, 256), bf16),
            v((nz, parts, 192, 128), bf16), v((nm, 2, parts, 2, 192, 128), bf16), v((256, width), bf16),
            v((nm * mix.shape[0], width), bf16), v(widen.shape, bf16), v(narrow.shape, bf16),
            v((parts, nm, 128, share), f32), v((parts, 2, 2, 128, share), f32),
            v((parts, 2, 2, 128, share), bf16), v((parts, 2, 128, share), bf16),
            v((parts, 128, share), bf16), v((parts, 128, share), bf16),
            dma((5,)), dma((2, 4)), dma((8,)), dma((8,)), dma((9,)), dma((9,)), dma((8,)), dma((8,)),
            dma((3,)), dma((3,)), dma((nz, parts)), dma((2, 2, parts)), dma((parts,)),
            dma((2, parts, 3)), dma((2, parts, 3)), dma((parts, 2)), dma((parts, 2)),
        ],
        compiler_params=pltpu.CompilerParams(
            collective_id=1, has_side_effects=True, vmem_limit_bytes=58 << 20),
        name="block",
    )(sharp, premix, premlp, nuc, loc, wqk, wv, mix, widen, narrow)


def shards(nuc, loc, premix, wqk, wv, sharp, mixing, premlp, widen, narrow):
    rows = nuc.shape[0]
    nz, nm = lax.axis_size("seq"), lax.axis_size("mp")
    heads = sharp.shape[0]
    if fused(nz, nm, heads, wqk.shape[2] // heads, wv.shape[1] // heads, rows):
        return block(nuc, loc, premix, wqk, wv, sharp, mixing, premlp, widen, narrow, nz, nm)
    nuc_all, loc_all = gather_inputs(nuc, loc, nz, nm)
    att, mix_all = attend(nuc_all, loc_all, premix, wqk, wv, sharp, mixing, nz, nm, rows)
    return tail(att, nuc, loc, loc_all, premlp, mixing, mix_all, widen, narrow, nz, nm)


def solution(mesh):
    return jax.shard_map(
        shards,
        mesh=mesh,
        in_specs=(
            P(("groups", "seq"), None),
            P("seq", None),
            P(),
            P(None, None, "mp"),
            P(None, "mp"),
            P("mp"),
            P("mp", None),
            P(),
            P(None, "mp"),
            P("mp", None),
        ),
        out_specs=P(("groups", "seq"), "mp"),
        check_vma=False,
    )
```

```python
import functools

import jax
import jax.numpy as jnp
from jax import lax
from jax.experimental import pallas as pl
from jax.experimental.pallas import tpu as pltpu
from jax.sharding import PartitionSpec as P

epsilon = 1e-06
MESH = pl.DeviceIdType.MESH
f32 = jnp.float32
bf16 = jnp.bfloat16


def normalize(v):
    return v * lax.rsqrt(jnp.mean(v * v, axis=-1, keepdims=True) + epsilon)


def halves(rows, nm):
    return rows // nm % 32 == 0


def gather_kernel(nz, nm, *refs):
    src = refs[0:2]
    out = refs[2:4]
    stage, lsem, zs, zr, xs, xr, cs, cr, ys, yr, fs, fr = refs[4:]
    g = lax.axis_index("groups")
    nx = nm // 2
    z = lax.axis_index("seq")
    m = lax.axis_index("mp")
    x, c = m // 2, m % 2
    rows = src[0].shape[0]
    piece = rows // nm

    split = halves(rows, nm)
    half = piece // 2

    def at(a, zsrc, mm, peer=False):
        if a == 1 and split:
            gg = 1 - g if peer else g
            return pl.ds(pl.multiple_of(zsrc * rows + mm * piece + gg * half, half), half)
        return pl.ds(pl.multiple_of(zsrc * rows + mm * piece, piece), piece)

    others = [lax.rem(x + d, nx) for d in range(1, nx)]
    barrier = pltpu.get_barrier_semaphore()

    @pl.when(z > 0)
    def _():
        pl.semaphore_signal(barrier, inc=1, device_id={"seq": z - 1}, device_id_type=MESH)

    @pl.when(z < nz - 1)
    def _():
        pl.semaphore_signal(barrier, inc=1, device_id={"seq": z + 1}, device_id_type=MESH)

    for o in others:
        pl.semaphore_signal(barrier, inc=1, device_id={"mp": o * 2 + c}, device_id_type=MESH)
    pl.semaphore_signal(barrier, inc=1, device_id={"mp": x * 2 + 1 - c}, device_id_type=MESH)
    if split:
        pl.semaphore_signal(barrier, inc=1, device_id={"groups": 1 - g}, device_id_type=MESH)

    loads = [pltpu.make_async_copy(src[a], stage.at[a], lsem.at[a]) for a in range(2)]
    for cp in loads:
        cp.start()

    pl.semaphore_wait(barrier, nx + int(split) + jnp.where(z > 0, 1, 0) + jnp.where(z < nz - 1, 1, 0))

    def zsend(a, dist, right):
        zsrc = z - dist if right else z + dist
        s = at(a, zsrc, m)
        if dist == 0:
            ref = src[a].at[at(a, 0, m)]
        else:
            ref = out[a].at[s]
        k = 0 if right else 1
        return pltpu.make_async_remote_copy(
            src_ref=ref, dst_ref=out[a].at[s],
            send_sem=zs.at[a, k, dist], recv_sem=zr.at[a, k, dist],
            device_id={"seq": z + 1 if right else z - 1}, device_id_type=MESH)

    def zrecv(a, dist, right):
        zsrc = z - dist if right else z + dist
        s = at(a, zsrc, m)
        k = 0 if right else 1
        return pltpu.make_async_remote_copy(
            src_ref=out[a].at[s], dst_ref=out[a].at[s],
            send_sem=zs.at[a, k, dist - 1], recv_sem=zr.at[a, k, dist - 1],
            device_id={"seq": z + 1 if right else z - 1}, device_id_type=MESH)

    def xcopy(a, k, dist, d, right, mine):
        zsrc = z - dist if right else z + dist
        o = lax.rem(x + d, nx) if mine else lax.rem(x - d + nx, nx)
        s = at(a, zsrc, m if mine else o * 2 + c)
        return pltpu.make_async_remote_copy(
            src_ref=out[a].at[s], dst_ref=out[a].at[s],
            send_sem=xs.at[a, k, dist - 1, d - 1], recv_sem=xr.at[a, k, dist - 1, d - 1],
            device_id={"mp": o * 2 + c}, device_id_type=MESH)

    def ccopy(a, k, dist, d, right, mine):
        zsrc = z - dist if right else z + dist
        o = lax.rem(x - d + nx, nx)
        s = at(a, zsrc, o * 2 + (c if mine else 1 - c))
        return pltpu.make_async_remote_copy(
            src_ref=out[a].at[s], dst_ref=out[a].at[s],
            send_sem=cs.at[a, k, dist - 1, d], recv_sem=cr.at[a, k, dist - 1, d],
            device_id={"mp": x * 2 + 1 - c}, device_id_type=MESH)

    def ycopy(k, dist, d, right, mine):
        zsrc = z - dist if right else z + dist
        s = at(1, zsrc, lax.rem(x - d + nx, nx) * 2 + c, not mine)
        return pltpu.make_async_remote_copy(
            src_ref=out[1].at[s], dst_ref=out[1].at[s],
            send_sem=ys.at[k, dist - 1, d], recv_sem=yr.at[k, dist - 1, d],
            device_id={"groups": 1 - g}, device_id_type=MESH)

    def fcopy(k, dist, d, right, mine):
        zsrc = z - dist if right else z + dist
        s = at(1, zsrc, lax.rem(x - d + nx, nx) * 2 + (c if mine else 1 - c), True)
        return pltpu.make_async_remote_copy(
            src_ref=out[1].at[s], dst_ref=out[1].at[s],
            send_sem=fs.at[k, dist - 1, d], recv_sem=fr.at[k, dist - 1, d],
            device_id={"mp": x * 2 + 1 - c}, device_id_type=MESH)

    def when(cond, f):
        @pl.when(cond)
        def _():
            f()

    can = {True: z < nz - 1, False: z > 0}

    for a in (1, 0):
        for right in (True, False):
            when(can[right], lambda a=a, right=right: zsend(a, 0, right).start())
    for a in range(2):
        loads[a].wait()
        st = pltpu.make_async_copy(
            stage.at[a], out[a].at[pl.ds(pl.multiple_of(z * rows, rows), rows)], lsem.at[a])
        st.start()

    def has(dist, right):
        return z - dist >= 0 if right else z + dist <= nz - 1

    def zstep(dist):
        for a in (1, 0):
            for right in (True, False):
                k = 0 if right else 1

                def got(a=a, right=right, k=k):
                    zrecv(a, dist, right).wait_recv()
                    if dist < nz - 1:
                        when(can[right], lambda: zsend(a, dist, right).start())
                    for d in range(1, nx):
                        xcopy(a, k, dist, d, right, True).start()
                    if a == 1 and split:
                        ycopy(k, dist, 0, right, True).start()
                    ccopy(a, k, dist, 0, right, True).start()

                when(has(dist, right), got)

    def xstep(dist):
        for a in (1, 0):
            for right in (True, False):
                k = 0 if right else 1

                def got(a=a, right=right, k=k):
                    for d in range(1, nx):
                        xcopy(a, k, dist, d, right, False).wait_recv()
                        if a == 1 and split:
                            ycopy(k, dist, d, right, True).start()
                        ccopy(a, k, dist, d, right, True).start()

                when(has(dist, right), got)

    def ystep(dist, ds):
        if not split or dist < 1:
            return
        for right in (True, False):
            k = 0 if right else 1

            def got(right=right, k=k):
                for d in ds:
                    ycopy(k, dist, d, right, False).wait_recv()
                    fcopy(k, dist, d, right, True).start()

            when(has(dist, right), got)

    far = tuple(range(1, nx))
    for dist in range(1, nz):
        zstep(dist)
        if dist > 1:
            xstep(dist - 1)
        ystep(dist - 1, (0,))
        ystep(dist - 2, far)
    ystep(nz - 2, far)
    ystep(nz - 1, (0,))
    xstep(nz - 1)
    ystep(nz - 1, far)

    for a in range(2):
        pltpu.make_async_copy(
            stage.at[a], out[a].at[pl.ds(pl.multiple_of(z * rows, rows), rows)], lsem.at[a]).wait()
    for dist in range(0, nz):
        for a in range(2):
            for right in (True, False):
                k = 0 if right else 1
                if dist < nz - 1:
                    cond = can[right] if dist == 0 else has(dist, right) & can[right]
                    when(cond, lambda a=a, right=right: zsend(a, dist, right).wait_send())
                if dist > 0:
                    def fin(a=a, right=right, k=k):
                        for d in range(1, nx):
                            xcopy(a, k, dist, d, right, True).wait_send()
                        for d in range(nx):
                            ccopy(a, k, dist, d, right, True).wait_send()
                            ccopy(a, k, dist, d, right, False).wait_recv()
                            if a == 1 and split:
                                ycopy(k, dist, d, right, True).wait_send()
                                fcopy(k, dist, d, right, True).wait_send()
                                fcopy(k, dist, d, right, False).wait_recv()
                    when(has(dist, right), fin)


def gather_inputs(nuc, loc, nz, nm):
    rows, width = nuc.shape
    nx = nm // 2
    dma = pltpu.SemaphoreType.DMA
    anyspec = pl.BlockSpec(memory_space=pl.ANY)
    shape = jax.ShapeDtypeStruct((nz * rows, width), bf16)
    ex = (2, nz - 1, nx) if halves(rows, nm) else (1,)
    return pl.pallas_call(
        functools.partial(gather_kernel, nz, nm),
        out_shape=(shape, shape),
        in_specs=[anyspec] * 2,
        out_specs=[anyspec] * 2,
        scratch_shapes=[
            pltpu.VMEM((2, rows, width), bf16),
            dma((2,)),
            dma((2, 2, nz)), dma((2, 2, nz)),
            dma((2, 2, nz - 1, nx)), dma((2, 2, nz - 1, nx)),
            dma((2, 2, nz - 1, nx)), dma((2, 2, nz - 1, nx)),
            dma(ex), dma(ex), dma(ex), dma(ex),
        ],
        compiler_params=pltpu.CompilerParams(collective_id=0, has_side_effects=True),
        name="gather_inputs",
    )(nuc, loc)


def attend_kernel(nz, nm, heads, qk, vd, sharp, nuc, loc, gain, wqk, wv, mix, out, mix_all,
                  q_s, k_s, v_s, xs, xr, ys, yr, cs, cr, os, orr):
    share_mix(nz, nm, mix, mix_all, xs, xr, ys, yr, cs, cr, os, orr, 0)
    t, j = pl.program_id(0), pl.program_id(1)
    z = lax.axis_index("seq")
    rows = nuc.shape[0]
    b = 128

    def body(flip):
        r_i = lax.broadcasted_iota(jnp.int32, (b, b), 0)
        c_i = lax.broadcasted_iota(jnp.int32, (b, b), 1)
        anti = jnp.where(r_i + c_i == b - 1, 1.0, 0.0).astype(bf16)
        parts = []
        nb = rows // b
        for i in range(nb):
            if flip:
                l = jnp.dot(anti, loc[(nb - 1 - i) * b:(nb - i) * b, :], preferred_element_type=f32)
            else:
                l = loc[i * b:(i + 1) * b, :].astype(f32)
            s = nuc[i * b:(i + 1) * b, :].astype(f32) + l
            parts.append((normalize(s) * gain[...]).astype(bf16))
        normed = jnp.concatenate(parts, axis=0)
        here = pl.ds(pl.multiple_of(j * rows, rows), rows)
        key = jnp.dot(normed, wqk[1], preferred_element_type=f32)
        for h in range(heads):
            k_s[here, h * qk:(h + 1) * qk] = normalize(key[:, h * qk:(h + 1) * qk]).astype(bf16)
        v_s[here, :] = jnp.dot(normed, wv[...], preferred_element_type=f32).astype(bf16)

        @pl.when(j == z)
        def _():
            query = jnp.dot(normed, wqk[0], preferred_element_type=f32)
            for h in range(heads):
                q_s[:, h * qk:(h + 1) * qk] = normalize(query[:, h * qk:(h + 1) * qk]).astype(bf16)

    @pl.when(t == 0)
    def _():
        body(False)

    @pl.when(t == 1)
    def _():
        body(True)

    @pl.when(j == nz - 1)
    def _():
        s_all = k_s.shape[0]
        chunk = 128
        wide = heads * vd
        for i in range(rows // chunk):
            rr = slice(i * chunk, (i + 1) * chunk)
            if i == 1:
                share_mix(nz, nm, mix, mix_all, xs, xr, ys, yr, cs, cr, os, orr, 2)
            res = []
            for h in range(heads):
                lo = (h * vd) // 128 * 128
                hi = min(-(-((h + 1) * vd) // 128) * 128, wide)
                num = jnp.zeros((chunk, hi - lo), f32)
                tot = jnp.zeros((chunk, 1), f32)
                step = 1536
                for kk in range(0, s_all, step):
                    sc = lax.dot_general(
                        q_s[rr, h * qk:(h + 1) * qk], k_s[kk:kk + step, h * qk:(h + 1) * qk],
                        (((1,), (1,)), ((), ())), preferred_element_type=f32)
                    w = jnp.exp(sc * (sharp[h] / qk))
                    tot = tot + jnp.sum(w, axis=-1, keepdims=True)
                    num = num + jnp.dot(w.astype(bf16), v_s[kk:kk + step, lo:hi],
                                        preferred_element_type=f32)
                res.append((lo, hi, num / tot))
            if heads == 1:
                out[rr, :] = res[0][2].astype(bf16)
            else:
                for lo in range(0, wide, 128):
                    hi = min(lo + 128, wide)
                    col = lo + lax.broadcasted_iota(jnp.int32, (chunk, hi - lo), 1)
                    val = None
                    for h in range(heads):
                        l0, h0, r = res[h]
                        if h * vd < hi and (h + 1) * vd > lo:
                            v = r[:, lo - l0:hi - l0]
                            val = v if val is None else jnp.where(col < h * vd, val, v)
                    out[rr, lo:hi] = val.astype(bf16)

    share_mix(nz, nm, mix, mix_all, xs, xr, ys, yr, cs, cr, os, orr, 1)


def share_mix(nz, nm, mix, mix_all, xs, xr, ys, yr, cs, cr, os, orr, phase):
    nx = nm // 2
    step = pl.program_id(0) * nz + pl.program_id(1)
    m = lax.axis_index("mp")
    g = lax.axis_index("groups")
    x, c = m // 2, m % 2
    n = 4 if mix.shape[0] % 128 == 0 else 2
    size = mix.shape[0] // (2 * n)

    def rows(gg, p):
        return pl.ds(pl.multiple_of((gg * n + p) * size, size), size)

    def xcopy(p, d, mine):
        o = lax.rem(x + d, nx) if mine else lax.rem(x - d + nx, nx)
        k = m if mine else o * 2 + c
        return pltpu.make_async_remote_copy(
            src_ref=mix.at[rows(g, p)], dst_ref=mix_all.at[k, rows(g, p)],
            send_sem=xs.at[p, d - 1], recv_sem=xr.at[p, d - 1],
            device_id={"mp": o * 2 + c}, device_id_type=MESH)

    def ycopy(p, d, mine):
        k = lax.rem(x - d + nx, nx) * 2 + c
        r = rows(g if mine else 1 - g, p)
        return pltpu.make_async_remote_copy(
            src_ref=mix_all.at[k, r], dst_ref=mix_all.at[k, r],
            send_sem=ys.at[p, d - 1], recv_sem=yr.at[p, d - 1],
            device_id={"groups": 1 - g}, device_id_type=MESH)

    def ccopy(p, d, far, mine):
        k = lax.rem(x - d + nx, nx) * 2 + (c if mine else 1 - c)
        r = rows(1 - g if far else g, p)
        f = 1 if far else 0
        return pltpu.make_async_remote_copy(
            src_ref=mix_all.at[k, r], dst_ref=mix_all.at[k, r],
            send_sem=cs.at[p, d - 1, f], recv_sem=cr.at[p, d - 1, f],
            device_id={"mp": x * 2 + 1 - c}, device_id_type=MESH)

    def own(mine):
        return pltpu.make_async_remote_copy(
            src_ref=mix, dst_ref=mix_all.at[m if mine else x * 2 + 1 - c],
            send_sem=os, recv_sem=orr,
            device_id={"mp": x * 2 + 1 - c}, device_id_type=MESH)

    def pass_on(p):
        for d in range(1, nx):
            xcopy(p, d, False).wait_recv()
            ycopy(p, d, True).start()
            ccopy(p, d, False, True).start()

    def bring(p):
        for d in range(1, nx):
            ycopy(p, d, False).wait_recv()
            ccopy(p, d, True, True).start()

    if phase == 0:
        @pl.when(step == 0)
        def _():
            barrier = pltpu.get_barrier_semaphore()
            for d in range(1, nx):
                pl.semaphore_signal(barrier, inc=1, device_id={"mp": lax.rem(x + d, nx) * 2 + c}, device_id_type=MESH)
            pl.semaphore_signal(barrier, inc=1, device_id={"mp": x * 2 + 1 - c}, device_id_type=MESH)
            pl.semaphore_signal(barrier, inc=1, device_id={"groups": 1 - g}, device_id_type=MESH)
            pl.semaphore_wait(barrier, nx + 1)
            for p in range(n):
                for d in range(1, nx):
                    xcopy(p, d, True).start()
            own(True).start()

        turns = {4: (nz - 1, None, nz, nz + 2), 2: (nz, nz + 2)}[n]
        for p in range(n):
            if turns[p] is not None:
                pl.when(step == turns[p])(functools.partial(pass_on, p))

        @pl.when(step == 2 * nz - 1)
        def _():
            for p in range(n // 2):
                bring(p)
    elif phase == 2:
        if n == 4:
            pl.when(step == nz - 1)(functools.partial(pass_on, 1))
    else:
        @pl.when(step == 2 * nz - 1)
        def _():
            for p in range(n // 2, n):
                bring(p)
            own(True).wait_send()
            own(False).wait_recv()
            for p in range(n):
                for d in range(1, nx):
                    xcopy(p, d, True).wait_send()
                    ycopy(p, d, True).wait_send()
                    for far in (False, True):
                        ccopy(p, d, far, True).wait_send()
                        ccopy(p, d, far, False).wait_recv()


def attend(nuc_all, loc_all, gain, wqk, wv, sharp, mix, nz, nm, rows):
    heads = sharp.shape[0]
    width = nuc_all.shape[1]
    qk = wqk.shape[2] // heads
    vd = wv.shape[1] // heads
    s_all = nuc_all.shape[0]
    nx = nm // 2
    dma = pltpu.SemaphoreType.DMA
    full = lambda a: pl.BlockSpec(a.shape, lambda t, j: (0,) * a.ndim, pipeline_mode=pl.Buffered(1))
    anyspec = pl.BlockSpec(memory_space=pl.ANY)
    gain = gain.reshape(1, width)
    return pl.pallas_call(
        functools.partial(attend_kernel, nz, nm, heads, qk, vd),
        grid=(2, nz),
        out_shape=(jax.ShapeDtypeStruct((2, rows, heads * vd), bf16),
                   jax.ShapeDtypeStruct((nm,) + mix.shape, bf16)),
        in_specs=[
            pl.BlockSpec(memory_space=pltpu.SMEM),
            pl.BlockSpec((rows, width), lambda t, j: (j, 0)),
            pl.BlockSpec((rows, width), lambda t, j: (t * (nz - 1 - j) + (1 - t) * j, 0)),
            full(gain), full(wqk), full(wv), anyspec,
        ],
        out_specs=(pl.BlockSpec((pl.Squeezed(), rows, heads * vd), lambda t, j: (t, 0, 0)), anyspec),
        scratch_shapes=[
            pltpu.VMEM((rows, heads * qk), bf16),
            pltpu.VMEM((s_all, heads * qk), bf16),
            pltpu.VMEM((s_all, heads * vd), bf16),
            dma((4, nx)), dma((4, nx)), dma((4, nx)), dma((4, nx)),
            dma((4, nx, 2)), dma((4, nx, 2)), dma, dma,
        ],
        compiler_params=pltpu.CompilerParams(
            collective_id=2, has_side_effects=True, vmem_limit_bytes=56 << 20),
        name="attend",
    )(sharp, nuc_all, loc_all, gain, wqk, wv, mix)


def tail_kernel(nz, nm, att, nuc_h, loc_h, loc_all, gain, mix, mix_all, widen_h, narrow_h, out,
                att_all, nuc, loc, locm, mixv, widen, narrow, sbuf, rbuf, mid,
                lsem, msem, xs, xr, cs, cr, ss, sr):
    nx = nm // 2
    rows, width = nuc.shape
    share = width // nm
    b = 128
    parts = rows // b
    z = lax.axis_index("seq")
    m = lax.axis_index("mp")
    x, c = m // 2, m % 2
    barrier = pltpu.get_barrier_semaphore()
    for d in range(1, nm):
        pl.semaphore_signal(barrier, inc=1, device_id={"mp": lax.rem(m + d, nm)}, device_id_type=MESH)
    loads = [
        pltpu.make_async_copy(att, att_all.at[m], lsem.at[0]),
        pltpu.make_async_copy(nuc_h, nuc, lsem.at[1]),
        pltpu.make_async_copy(loc_h, loc, lsem.at[2]),
        pltpu.make_async_copy(loc_all.at[pl.ds(pl.multiple_of((nz - 1 - z) * rows, rows), rows)], locm, lsem.at[3]),
        pltpu.make_async_copy(widen_h, widen, lsem.at[4]),
        pltpu.make_async_copy(narrow_h, narrow, lsem.at[5]),
    ]
    mloads = [pltpu.make_async_copy(mix, mixv.at[m], msem.at[0])]
    for d in range(1, nm):
        k = lax.rem(m + d, nm)
        mloads.append(pltpu.make_async_copy(mix_all.at[k], mixv.at[k], msem.at[d]))
    for cp in loads[:4] + mloads + loads[4:]:
        cp.start()
    pl.semaphore_wait(barrier, nm - 1)

    def xcopy(i, d, mine):
        o = lax.rem(x + d, nx) if mine else lax.rem(x - d + nx, nx)
        k = m if mine else o * 2 + c
        r = pl.ds(i * b, b)
        return pltpu.make_async_remote_copy(
            src_ref=att.at[:, r], dst_ref=att_all.at[k, :, r], send_sem=xs.at[i, d - 1],
            recv_sem=xr.at[i, d - 1], device_id={"mp": o * 2 + c}, device_id_type=MESH)

    def ccopy(i, d, mine):
        o = lax.rem(x - d + nx, nx)
        k = o * 2 + (c if mine else 1 - c)
        r = pl.ds(i * b, b)
        ref = att.at[:, r] if d == 0 else att_all.at[k, :, r]
        return pltpu.make_async_remote_copy(
            src_ref=ref, dst_ref=att_all.at[k, :, r], send_sem=cs.at[i, d], recv_sem=cr.at[i, d],
            device_id={"mp": x * 2 + 1 - c}, device_id_type=MESH)

    def scopy(i, d):
        k = lax.rem(m + d, nm)
        return pltpu.make_async_remote_copy(
            src_ref=sbuf.at[i, k], dst_ref=rbuf.at[i, d - 1], send_sem=ss.at[i, d - 1],
            recv_sem=sr.at[i, d - 1], device_id={"mp": k}, device_id_type=MESH)

    for i in range(parts):
        for d in range(1, nx):
            xcopy(i, d, True).start()
        ccopy(i, 0, True).start()

    def pass_on(i):
        for d in range(1, nx):
            xcopy(i, d, False).wait_recv()
            ccopy(i, d, True).start()

    r_i = lax.broadcasted_iota(jnp.int32, (b, b), 0)
    c_i = lax.broadcasted_iota(jnp.int32, (b, b), 1)
    anti = jnp.where(r_i + c_i == b - 1, 1.0, 0.0).astype(bf16)
    for cp in loads[:4]:
        cp.wait()
    pass_on(0)
    for cp in mloads:
        cp.wait()
    for i in range(parts):
        r = slice(i * b, (i + 1) * b)
        n = nuc[r, :].astype(f32)
        s0 = n + loc[r, :].astype(f32)
        s1 = n + jnp.dot(anti, locm[(parts - 1 - i) * b:(parts - i) * b, :], preferred_element_type=f32)
        middle = jnp.concatenate([s0, s1], axis=0)
        for d in range(nx):
            ccopy(i, d, False).wait_recv()
        for k in range(nm):
            a = jnp.concatenate([att_all[k, 0, r, :], att_all[k, 1, r, :]], axis=0)
            middle = middle + jnp.dot(a, mixv[k], preferred_element_type=f32)
        if i + 1 < parts:
            pass_on(i + 1)
        normed = (normalize(middle) * gain[...]).astype(bf16)
        if i == 0:
            for cp in loads[4:]:
                cp.wait()
        up = jax.nn.gelu(jnp.dot(normed, widen[...], preferred_element_type=f32), approximate=True)
        both = (up[:b] + up[b:]).astype(bf16)
        down = jnp.dot(both, narrow[...], preferred_element_type=f32)
        total = middle[:b] + middle[b:] + down
        down = down.astype(bf16)
        for k in range(nm):
            sbuf[i, k] = down[:, k * share:(k + 1) * share]
            mid[i, k] = total[:, k * share:(k + 1) * share]
        for d in range(1, nm):
            scopy(i, d).start()
    for i in range(parts):
        acc = mid[i, m]
        for d in range(1, nm):
            scopy(i, d).wait_recv()
            acc = acc + rbuf[i, d - 1].astype(f32)
        out[i * b:(i + 1) * b, :] = 0.5 * acc
    for i in range(parts):
        for d in range(1, nx):
            xcopy(i, d, True).wait_send()
        for d in range(nx):
            ccopy(i, d, True).wait_send()
        for d in range(1, nm):
            scopy(i, d).wait_send()


def tail(att, nuc, loc, loc_all, gain, mix, mix_all, widen, narrow, nz, nm):
    rows, width = nuc.shape
    share = width // nm
    nx = nm // 2
    parts = rows // 128
    dma = pltpu.SemaphoreType.DMA
    anyspec = pl.BlockSpec(memory_space=pl.ANY)
    vm = pl.BlockSpec(memory_space=pltpu.VMEM)
    v = pltpu.VMEM
    return pl.pallas_call(
        functools.partial(tail_kernel, nz, nm),
        out_shape=jax.ShapeDtypeStruct((rows, share), f32),
        in_specs=[vm, anyspec, anyspec, anyspec, vm, anyspec, anyspec, anyspec, anyspec],
        out_specs=vm,
        scratch_shapes=[
            v((nm,) + att.shape, bf16), v(nuc.shape, bf16), v(nuc.shape, bf16), v(nuc.shape, bf16),
            v((nm,) + mix.shape, bf16), v(widen.shape, bf16), v(narrow.shape, bf16),
            v((parts, nm, 128, share), bf16), v((parts, nm - 1, 128, share), bf16),
            v((parts, nm, 128, share), f32),
            dma((6,)), dma((nm,)),
            dma((parts, nx)), dma((parts, nx)), dma((parts, nx)), dma((parts, nx)),
            dma((parts, nm)), dma((parts, nm)),
        ],
        compiler_params=pltpu.CompilerParams(
            collective_id=3, has_side_effects=True, vmem_limit_bytes=56 << 20),
        name="tail",
    )(att, nuc, loc, loc_all, gain.reshape(1, width), mix, mix_all, widen, narrow)


PLANES = ((0, 3), (1, 2))


def fused(nz, nm, heads, qk, vd, rows):
    return nz == 4 and nm == 4 and heads == 2 and qk == 128 and vd == 192 and rows % 128 == 0


def block_kernel(nz, nm, sharp, gain1, gain2, nuc_h, loc_h, wqk_h, wv_h, mix_h, widen_h, narrow_h, out,
                 nuc, loc, locm, rloc, nbuf, wqk, wv, send, recv, kbuf, vbuf, asend, att, abuf,
                 mixv, widen, narrow, mid0, up0, mids, downs, sbuf, rbuf, xbuf, fbuf,
                 lsem, ms, mr, xs, xr, qs, qr, ql, rs, rr, rl, hs, hr, ss, sr):
    rows, width = nuc.shape
    share = width // nm
    b = 128
    hb = b // 2
    parts = rows // b
    depth = mix_h.shape[0]
    g = lax.axis_index("groups")
    z = lax.axis_index("seq")
    m = lax.axis_index("mp")
    x, c = m // 2, m % 2
    to_x = {"mp": (1 - x) * 2 + c}
    to_y = {"groups": 1 - g}
    to_d = {"groups": 1 - g, "mp": (1 - x) * 2 + c}
    to_c = {"mp": x * 2 + 1 - c}

    def remote(src, dst, ssem, rsem, dev):
        return pltpu.make_async_remote_copy(
            src_ref=src, dst_ref=dst, send_sem=ssem, recv_sem=rsem, device_id=dev, device_id_type=MESH)

    barrier = pltpu.get_barrier_semaphore()
    for d in range(1, nz):
        pl.semaphore_signal(barrier, inc=1, device_id={"seq": lax.rem(z + d, nz)}, device_id_type=MESH)
    for d in range(1, nm):
        pl.semaphore_signal(barrier, inc=1, device_id={"mp": lax.rem(m + d, nm)}, device_id_type=MESH)
    pl.semaphore_signal(barrier, inc=1, device_id=to_y, device_id_type=MESH)
    pl.semaphore_signal(barrier, inc=1, device_id=to_d, device_id_type=MESH)

    loads = [
        pltpu.make_async_copy(nuc_h, nuc, lsem.at[0]),
        pltpu.make_async_copy(loc_h, loc, lsem.at[1]),
        pltpu.make_async_copy(wqk_h, wqk, lsem.at[2]),
        pltpu.make_async_copy(wv_h, wv, lsem.at[3]),
        pltpu.make_async_copy(widen_h, widen, lsem.at[4]),
        pltpu.make_async_copy(narrow_h, narrow, lsem.at[5]),
    ]
    own_mix = pltpu.make_async_copy(mix_h, mixv.at[pl.ds(pl.multiple_of(m * depth, depth), depth)], lsem.at[6])
    for cp in loads[:4]:
        cp.start()

    sl = rows // 8

    def piece(xx, gg, cc):
        return pl.ds(pl.multiple_of(((xx * 2 + gg) * 2 + cc) * sl, sl), sl)

    def loc_z():
        return remote(loc_h.at[piece(x, g, c)], locm.at[piece(x, g, c)], ms.at[0], mr.at[0], {"seq": nz - 1 - z})

    def loc_on(k):
        r = locm.at[piece(x, g, c)]
        return remote(r, r, ms.at[1 + k], mr.at[1 + k], (to_x, to_y, to_d)[k])

    def loc_c(k):
        r = locm.at[piece(x if k % 2 == 0 else 1 - x, g if k < 2 else 1 - g, c)]
        return remote(r, r, ms.at[4 + k], mr.at[4 + k], to_c)

    size = depth // 4

    def mrows(mm, gg, p):
        return pl.ds(pl.multiple_of(mm * depth + (gg * 2 + p) * size, size), size)

    def mix_x(p):
        return remote(mix_h.at[mrows(0, g, p)], mixv.at[mrows(m, g, p)], xs.at[p], xr.at[p], to_x)

    def mix_y(p):
        r = mixv.at[mrows((1 - x) * 2 + c, g, p)]
        return remote(r, r, xs.at[2 + p], xr.at[2 + p], to_y)

    def mix_c(p, far):
        r = mixv.at[mrows((1 - x) * 2 + c, 1 - g if far else g, p)]
        k = (6 if far else 4) + p
        return remote(r, r, xs.at[k], xr.at[k], to_c)

    def mix_own():
        return remote(mix_h, mixv.at[pl.ds(pl.multiple_of(m * depth, depth), depth)], xs.at[8], xr.at[8], to_c)

    pl.semaphore_wait(barrier, nz + nm)
    loc_z().start()
    mix_x(0).start()
    mix_own().start()
    own_mix.start()
    for cp in loads[4:]:
        cp.start()

    r_i = lax.broadcasted_iota(jnp.int32, (b, b), 0)
    c_i = lax.broadcasted_iota(jnp.int32, (b, b), 1)
    anti = jnp.where(r_i + c_i == b - 1, 1.0, 0.0).astype(bf16)
    low = lax.broadcasted_iota(jnp.int32, (hb, b), 1) < hb

    def chunk(i):
        return slice(i * b, (i + 1) * b)

    def qkv_send(t, h, i):
        return remote(send.at[t, h, i], recv.at[z, i], qs.at[t, h, i], qr.at[z, i], {"seq": PLANES[t][h]})

    def qkv_keep(t, h, i):
        return pltpu.make_async_copy(send.at[t, h, i], recv.at[z, i], ql.at[i])

    def project(t):
        other = loc if t == 0 else rloc
        for i in range(parts):
            if t == 1:
                rloc[chunk(i), :] = jnp.dot(
                    anti, locm[chunk(parts - 1 - i), :], preferred_element_type=f32).astype(bf16)
            s = nuc[chunk(i), :].astype(f32) + other[chunk(i), :].astype(f32)
            nbuf[chunk(i), :] = (normalize(s) * gain1[...]).astype(bf16)
        query = jnp.dot(nbuf[...], wqk[0], preferred_element_type=f32)
        key = jnp.dot(nbuf[...], wqk[1], preferred_element_type=f32)
        value = jnp.dot(nbuf[...], wv[...], preferred_element_type=f32)
        for i in range(parts):
            rest = value[chunk(i), b:2 * b]
            first, second = rest[:hb], pltpu.roll(rest[hb:], hb, 1)
            for h in range(2):
                send[t, h, i, 0:b, :] = normalize(query[chunk(i), h * b:(h + 1) * b]).astype(bf16)
                send[t, h, i, b:2 * b, :] = normalize(key[chunk(i), h * b:(h + 1) * b]).astype(bf16)
                send[t, h, i, 2 * b:3 * b, :] = value[chunk(i), 2 * h * b:(2 * h + 1) * b].astype(bf16)
                fold = jnp.where(low, first, second) if h == 0 else jnp.where(low, second, first)
                send[t, h, i, 3 * b:3 * b + hb, :] = fold.astype(bf16)
            for h in range(2):
                @pl.when(z != PLANES[t][h])
                def _(h=h, i=i):
                    qkv_send(t, h, i).start()

                @pl.when(z == PLANES[t][h])
                def _(h=h, i=i):
                    qkv_keep(t, h, i).start()

    def att_send(t, h, blk, i):
        return remote(asend.at[blk, i], att.at[m, t, i, h], rs.at[blk, i], rr.at[t, h, i], {"seq": blk})

    def att_keep(t, h, i):
        return pltpu.make_async_copy(asend.at[z, i], att.at[m, t, i, h], rl.at[i])

    def attend(t):
        h = jnp.where(z == PLANES[t][0], 0, 1)
        mask = low == (h == 0)
        for src in range(nz):
            for i in range(parts):
                @pl.when(z != src)
                def _():
                    remote(recv.at[src, i], recv.at[src, i], qs.at[0, 0, i], qr.at[src, i], {"seq": src}).wait_recv()

                @pl.when(z == src)
                def _():
                    qkv_keep(t, 0, i).wait()

                r0 = (src * parts + i) * b
                kbuf[r0:r0 + b, :] = recv[src, i, b:2 * b, :]
                vbuf[r0:r0 + b, 0:b] = recv[src, i, 2 * b:3 * b, :]
                fold = recv[src, i, 3 * b:3 * b + hb, :].astype(f32)
                turned = pltpu.roll(fold, hb, 1)
                vbuf[r0:r0 + hb, b:2 * b] = jnp.where(mask, fold, turned).astype(bf16)
                vbuf[r0 + hb:r0 + b, b:2 * b] = jnp.where(mask, turned, fold).astype(bf16)
        scale = sharp[h] * (1.4426950408889634 / b)
        up = z < nz // 2
        order = [jnp.where(up, 3, 0), jnp.where(up, 2, 1), z + 1 - 2 * lax.rem(z, 2), z]

        def step(i, carry):
            for s in range(nz):
                blk = order[s]
                sc = lax.dot_general(recv[blk, i, 0:b, :], kbuf[...], (((1,), (1,)), ((), ())),
                                     preferred_element_type=f32)
                w = jnp.exp2(sc * scale)
                tot = jnp.sum(w, axis=-1, keepdims=True)
                res = jnp.dot(w.astype(bf16), vbuf[...], preferred_element_type=f32) / tot
                asend[blk, i, 0:b, :] = res[:, :b].astype(bf16)
                asend[blk, i, b:b + hb, :] = jnp.where(mask, res[:hb, b:], res[hb:, b:]).astype(bf16)
                if s < nz - 1:
                    att_send(t, h, blk, i).start()
                else:
                    att_keep(t, h, i).start()
            return carry

        lax.fori_loop(0, parts, step, 0)

    def share_x(t, i):
        r = att.at[m, t, i]
        return remote(r, r, hs.at[t, i, 0], hr.at[t, i, 0], to_x)

    def share_c(t, i, k):
        r = att.at[m if k == 0 else (1 - x) * 2 + c, t, i]
        return remote(r, r, hs.at[t, i, 1 + k], hr.at[t, i, 1 + k], to_c)

    def relay(t, i):
        for h in range(2):
            src = PLANES[t][h]

            @pl.when(z != src)
            def _():
                r = att.at[m, t, i, h]
                remote(r, r, rs.at[0, i], rr.at[t, h, i], {"seq": src}).wait_recv()

            @pl.when(z == src)
            def _():
                att_keep(t, h, i).wait()
        share_x(t, i).start()
        share_c(t, i, 0).start()

    def relay_c(t, i):
        share_x(t, i).wait_recv()
        share_c(t, i, 1).start()

    def middle(t, i):
        for k in range(2):
            share_c(t, i, k).wait_recv()
        for k in range(nm):
            f0, f1 = att[k, t, i, 0, b:b + hb, :].astype(f32), att[k, t, i, 1, b:b + hb, :].astype(f32)
            lo = k * 3 * b
            abuf[chunk(i), lo:lo + b] = att[k, t, i, 0, 0:b, :]
            abuf[i * b:i * b + hb, lo + b:lo + 2 * b] = jnp.where(low, f0, f1).astype(bf16)
            abuf[i * b + hb:(i + 1) * b, lo + b:lo + 2 * b] = pltpu.roll(jnp.where(low, f1, f0), hb, 1).astype(bf16)
            abuf[chunk(i), lo + 2 * b:lo + 3 * b] = att[k, t, i, 1, 0:b, :]

    def upper(t, r):
        s = nuc[r, :].astype(f32) + (loc if t == 0 else rloc)[r, :].astype(f32)
        mid = s + jnp.dot(abuf[r, :], mixv[...], preferred_element_type=f32)
        normed = (normalize(mid) * gain2[...]).astype(bf16)
        return mid, jax.nn.gelu(jnp.dot(normed, widen[...], preferred_element_type=f32), approximate=True)

    def pair_copy(i):
        return remote(sbuf.at[i, 1 - c], rbuf.at[i], ss.at[i, 0], sr.at[i, 0], to_c)

    def sum_copy(i):
        return remote(xbuf.at[i], fbuf.at[i], ss.at[i, 1], sr.at[i, 1], to_x)

    def pass_sum(i):
        pair_copy(i).wait_recv()
        xbuf[i] = (downs[i, c, 1 - x] + rbuf[i, 1 - x].astype(f32)).astype(bf16)
        sum_copy(i).start()

    first = (z == PLANES[0][0]) | (z == PLANES[0][1])
    second = (z == PLANES[1][0]) | (z == PLANES[1][1])
    for cp in loads[:4]:
        cp.wait()
    project(0)
    loc_z().wait_recv()
    for k in (2, 0, 1):
        loc_on(k).start()
    loc_c(0).start()
    mix_x(0).wait_recv()
    mix_y(0).start()
    mix_c(0, False).start()
    for k in range(3):
        loc_on(k).wait_recv()
        loc_c(k + 1).start()
    mix_x(1).start()
    for k in range(4):
        loc_c(k).wait_recv()
    project(1)
    mix_y(0).wait_recv()
    mix_c(0, True).start()
    mix_x(1).wait_recv()
    mix_y(1).start()
    mix_c(1, False).start()

    @pl.when(first)
    def _():
        attend(0)

    for i in range(parts):
        relay(0, i)
    mix_y(1).wait_recv()
    mix_c(1, True).start()

    @pl.when(second)
    def _():
        attend(1)

    for i in range(parts):
        relay_c(0, i)
    own_mix.wait()
    mix_own().wait_recv()
    for p in range(2):
        for far in (False, True):
            mix_c(p, far).wait_recv()
    for cp in loads[4:]:
        cp.wait()
    for i in range(parts):
        middle(0, i)
    for i in range(parts):
        pl.when(second)(functools.partial(relay, 1, i))
        mid, up = upper(0, chunk(i))
        mid0[chunk(i), :] = mid
        up0[chunk(i), :] = up
    pl.when(first)(functools.partial(relay, 1, 0))
    for i in range(parts):
        if i + 1 < parts:
            pl.when(first)(functools.partial(relay, 1, i + 1))
        relay_c(1, i)
        if i > 0:
            pass_sum(i - 1)
        middle(1, i)
        mid, up = upper(1, chunk(i))
        both = (up + up0[chunk(i), :]).astype(bf16)
        down = jnp.dot(both, narrow[...], preferred_element_type=f32)
        total = mid + mid0[chunk(i), :] + down
        for k in range(nm):
            cols = slice(k * share, (k + 1) * share)
            sbuf[i, k % 2, k // 2] = down[:, cols].astype(bf16)
            downs[i, k % 2, k // 2] = down[:, cols]
            mids[i, k] = total[:, cols]
        pair_copy(i).start()
    pass_sum(parts - 1)
    for i in range(parts):
        sum_copy(i).wait_recv()
        out[chunk(i), :] = 0.5 * (mids[i, m] + rbuf[i, x].astype(f32) + fbuf[i].astype(f32))

    loc_z().wait_send()
    for k in range(3):
        loc_on(k).wait_send()
    for k in range(4):
        loc_c(k).wait_send()
    mix_own().wait_send()
    for p in range(2):
        mix_x(p).wait_send()
        mix_y(p).wait_send()
        for far in (False, True):
            mix_c(p, far).wait_send()
    for i in range(parts):
        for t in range(2):
            for h in range(2):
                @pl.when(z != PLANES[t][h])
                def _():
                    qkv_send(t, h, i).wait_send()
            share_x(t, i).wait_send()
            for k in range(2):
                share_c(t, i, k).wait_send()
        for blk in range(nz):
            @pl.when(z != blk)
            def _():
                att_send(0, 0, blk, i).wait_send()
        pair_copy(i).wait_send()
        sum_copy(i).wait_send()


def block(nuc, loc, premix, wqk, wv, sharp, mix, premlp, widen, narrow, nz, nm):
    rows, width = nuc.shape
    parts = rows // 128
    hidden = widen.shape[1]
    share = width // nm
    dma = pltpu.SemaphoreType.DMA
    anyspec = pl.BlockSpec(memory_space=pl.ANY)
    vm = pl.BlockSpec(memory_space=pltpu.VMEM)
    v = pltpu.VMEM
    return pl.pallas_call(
        functools.partial(block_kernel, nz, nm),
        out_shape=pltpu.VMEM((rows, share), f32),
        in_specs=[pl.BlockSpec(memory_space=pltpu.SMEM), vm, vm] + [anyspec] * 7,
        out_specs=vm,
        scratch_shapes=[
            v(nuc.shape, bf16), v(nuc.shape, bf16), v(nuc.shape, bf16), v(nuc.shape, bf16), v(nuc.shape, bf16),
            v(wqk.shape, bf16), v(wv.shape, bf16),
            v((2, 2, parts, 448, 128), bf16), v((nz, parts, 448, 128), bf16),
            v((nz * rows, 128), bf16), v((nz * rows, 256), bf16),
            v((nz, parts, 192, 128), bf16), v((nm, 2, parts, 2, 192, 128), bf16), v((rows, width), bf16),
            v((nm * mix.shape[0], width), bf16), v(widen.shape, bf16), v(narrow.shape, bf16),
            v((rows, width), f32), v((rows, hidden), f32),
            v((parts, nm, 128, share), f32), v((parts, 2, 2, 128, share), f32),
            v((parts, 2, 2, 128, share), bf16), v((parts, 2, 128, share), bf16),
            v((parts, 128, share), bf16), v((parts, 128, share), bf16),
            dma((7,)), dma((8,)), dma((8,)), dma((9,)), dma((9,)),
            dma((2, 2, parts)), dma((nz, parts)), dma((parts,)),
            dma((nz, parts)), dma((2, 2, parts)), dma((parts,)),
            dma((2, parts, 3)), dma((2, parts, 3)), dma((parts, 2)), dma((parts, 2)),
        ],
        compiler_params=pltpu.CompilerParams(
            collective_id=1, has_side_effects=True, vmem_limit_bytes=58 << 20),
        name="block",
    )(sharp, premix, premlp, nuc, loc, wqk, wv, mix, widen, narrow)


def shards(nuc, loc, premix, wqk, wv, sharp, mixing, premlp, widen, narrow):
    rows = nuc.shape[0]
    nz, nm = lax.axis_size("seq"), lax.axis_size("mp")
    heads = sharp.shape[0]
    if fused(nz, nm, heads, wqk.shape[2] // heads, wv.shape[1] // heads, rows):
        return block(nuc, loc, premix, wqk, wv, sharp, mixing, premlp, widen, narrow, nz, nm)
    nuc_all, loc_all = gather_inputs(nuc, loc, nz, nm)
    att, mix_all = attend(nuc_all, loc_all, premix, wqk, wv, sharp, mixing, nz, nm, rows)
    return tail(att, nuc, loc, loc_all, premlp, mixing, mix_all, widen, narrow, nz, nm)


def solution(mesh):
    return jax.shard_map(
        shards,
        mesh=mesh,
        in_specs=(
            P(("groups", "seq"), None),
            P("seq", None),
            P(),
            P(None, None, "mp"),
            P(None, "mp"),
            P("mp"),
            P("mp", None),
            P(),
            P(None, "mp"),
            P("mp", None),
        ),
        out_specs=P(("groups", "seq"), "mp"),
        check_vma=False,
    )
```

```python
import functools

import jax
import jax.numpy as jnp
from jax import lax
from jax.experimental import pallas as pl
from jax.experimental.pallas import tpu as pltpu
from jax.sharding import PartitionSpec as P

epsilon = 1e-06
MESH = pl.DeviceIdType.MESH
f32 = jnp.float32
bf16 = jnp.bfloat16


def normalize(v):
    return v * lax.rsqrt(jnp.mean(v * v, axis=-1, keepdims=True) + epsilon)


def halves(rows, nm):
    return rows // nm % 32 == 0


def gather_kernel(nz, nm, *refs):
    src = refs[0:2]
    out = refs[2:4]
    stage, lsem, zs, zr, xs, xr, cs, cr, ys, yr, fs, fr = refs[4:]
    g = lax.axis_index("groups")
    nx = nm // 2
    z = lax.axis_index("seq")
    m = lax.axis_index("mp")
    x, c = m // 2, m % 2
    rows = src[0].shape[0]
    piece = rows // nm

    split = halves(rows, nm)
    half = piece // 2

    def at(a, zsrc, mm, peer=False):
        if a == 1 and split:
            gg = 1 - g if peer else g
            return pl.ds(pl.multiple_of(zsrc * rows + mm * piece + gg * half, half), half)
        return pl.ds(pl.multiple_of(zsrc * rows + mm * piece, piece), piece)

    others = [lax.rem(x + d, nx) for d in range(1, nx)]
    barrier = pltpu.get_barrier_semaphore()

    @pl.when(z > 0)
    def _():
        pl.semaphore_signal(barrier, inc=1, device_id={"seq": z - 1}, device_id_type=MESH)

    @pl.when(z < nz - 1)
    def _():
        pl.semaphore_signal(barrier, inc=1, device_id={"seq": z + 1}, device_id_type=MESH)

    for o in others:
        pl.semaphore_signal(barrier, inc=1, device_id={"mp": o * 2 + c}, device_id_type=MESH)
    pl.semaphore_signal(barrier, inc=1, device_id={"mp": x * 2 + 1 - c}, device_id_type=MESH)
    if split:
        pl.semaphore_signal(barrier, inc=1, device_id={"groups": 1 - g}, device_id_type=MESH)

    loads = [pltpu.make_async_copy(src[a], stage.at[a], lsem.at[a]) for a in range(2)]
    for cp in loads:
        cp.start()

    pl.semaphore_wait(barrier, nx + int(split) + jnp.where(z > 0, 1, 0) + jnp.where(z < nz - 1, 1, 0))

    def zsend(a, dist, right):
        zsrc = z - dist if right else z + dist
        s = at(a, zsrc, m)
        if dist == 0:
            ref = src[a].at[at(a, 0, m)]
        else:
            ref = out[a].at[s]
        k = 0 if right else 1
        return pltpu.make_async_remote_copy(
            src_ref=ref, dst_ref=out[a].at[s],
            send_sem=zs.at[a, k, dist], recv_sem=zr.at[a, k, dist],
            device_id={"seq": z + 1 if right else z - 1}, device_id_type=MESH)

    def zrecv(a, dist, right):
        zsrc = z - dist if right else z + dist
        s = at(a, zsrc, m)
        k = 0 if right else 1
        return pltpu.make_async_remote_copy(
            src_ref=out[a].at[s], dst_ref=out[a].at[s],
            send_sem=zs.at[a, k, dist - 1], recv_sem=zr.at[a, k, dist - 1],
            device_id={"seq": z + 1 if right else z - 1}, device_id_type=MESH)

    def xcopy(a, k, dist, d, right, mine):
        zsrc = z - dist if right else z + dist
        o = lax.rem(x + d, nx) if mine else lax.rem(x - d + nx, nx)
        s = at(a, zsrc, m if mine else o * 2 + c)
        return pltpu.make_async_remote_copy(
            src_ref=out[a].at[s], dst_ref=out[a].at[s],
            send_sem=xs.at[a, k, dist - 1, d - 1], recv_sem=xr.at[a, k, dist - 1, d - 1],
            device_id={"mp": o * 2 + c}, device_id_type=MESH)

    def ccopy(a, k, dist, d, right, mine):
        zsrc = z - dist if right else z + dist
        o = lax.rem(x - d + nx, nx)
        s = at(a, zsrc, o * 2 + (c if mine else 1 - c))
        return pltpu.make_async_remote_copy(
            src_ref=out[a].at[s], dst_ref=out[a].at[s],
            send_sem=cs.at[a, k, dist - 1, d], recv_sem=cr.at[a, k, dist - 1, d],
            device_id={"mp": x * 2 + 1 - c}, device_id_type=MESH)

    def ycopy(k, dist, d, right, mine):
        zsrc = z - dist if right else z + dist
        s = at(1, zsrc, lax.rem(x - d + nx, nx) * 2 + c, not mine)
        return pltpu.make_async_remote_copy(
            src_ref=out[1].at[s], dst_ref=out[1].at[s],
            send_sem=ys.at[k, dist - 1, d], recv_sem=yr.at[k, dist - 1, d],
            device_id={"groups": 1 - g}, device_id_type=MESH)

    def fcopy(k, dist, d, right, mine):
        zsrc = z - dist if right else z + dist
        s = at(1, zsrc, lax.rem(x - d + nx, nx) * 2 + (c if mine else 1 - c), True)
        return pltpu.make_async_remote_copy(
            src_ref=out[1].at[s], dst_ref=out[1].at[s],
            send_sem=fs.at[k, dist - 1, d], recv_sem=fr.at[k, dist - 1, d],
            device_id={"mp": x * 2 + 1 - c}, device_id_type=MESH)

    def when(cond, f):
        @pl.when(cond)
        def _():
            f()

    can = {True: z < nz - 1, False: z > 0}

    for a in (1, 0):
        for right in (True, False):
            when(can[right], lambda a=a, right=right: zsend(a, 0, right).start())
    for a in range(2):
        loads[a].wait()
        st = pltpu.make_async_copy(
            stage.at[a], out[a].at[pl.ds(pl.multiple_of(z * rows, rows), rows)], lsem.at[a])
        st.start()

    def has(dist, right):
        return z - dist >= 0 if right else z + dist <= nz - 1

    def zstep(dist):
        for a in (1, 0):
            for right in (True, False):
                k = 0 if right else 1

                def got(a=a, right=right, k=k):
                    zrecv(a, dist, right).wait_recv()
                    if dist < nz - 1:
                        when(can[right], lambda: zsend(a, dist, right).start())
                    for d in range(1, nx):
                        xcopy(a, k, dist, d, right, True).start()
                    if a == 1 and split:
                        ycopy(k, dist, 0, right, True).start()
                    ccopy(a, k, dist, 0, right, True).start()

                when(has(dist, right), got)

    def xstep(dist):
        for a in (1, 0):
            for right in (True, False):
                k = 0 if right else 1

                def got(a=a, right=right, k=k):
                    for d in range(1, nx):
                        xcopy(a, k, dist, d, right, False).wait_recv()
                        if a == 1 and split:
                            ycopy(k, dist, d, right, True).start()
                        ccopy(a, k, dist, d, right, True).start()

                when(has(dist, right), got)

    def ystep(dist, ds):
        if not split or dist < 1:
            return
        for right in (True, False):
            k = 0 if right else 1

            def got(right=right, k=k):
                for d in ds:
                    ycopy(k, dist, d, right, False).wait_recv()
                    fcopy(k, dist, d, right, True).start()

            when(has(dist, right), got)

    far = tuple(range(1, nx))
    for dist in range(1, nz):
        zstep(dist)
        if dist > 1:
            xstep(dist - 1)
        ystep(dist - 1, (0,))
        ystep(dist - 2, far)
    ystep(nz - 2, far)
    ystep(nz - 1, (0,))
    xstep(nz - 1)
    ystep(nz - 1, far)

    for a in range(2):
        pltpu.make_async_copy(
            stage.at[a], out[a].at[pl.ds(pl.multiple_of(z * rows, rows), rows)], lsem.at[a]).wait()
    for dist in range(0, nz):
        for a in range(2):
            for right in (True, False):
                k = 0 if right else 1
                if dist < nz - 1:
                    cond = can[right] if dist == 0 else has(dist, right) & can[right]
                    when(cond, lambda a=a, right=right: zsend(a, dist, right).wait_send())
                if dist > 0:
                    def fin(a=a, right=right, k=k):
                        for d in range(1, nx):
                            xcopy(a, k, dist, d, right, True).wait_send()
                        for d in range(nx):
                            ccopy(a, k, dist, d, right, True).wait_send()
                            ccopy(a, k, dist, d, right, False).wait_recv()
                            if a == 1 and split:
                                ycopy(k, dist, d, right, True).wait_send()
                                fcopy(k, dist, d, right, True).wait_send()
                                fcopy(k, dist, d, right, False).wait_recv()
                    when(has(dist, right), fin)


def gather_inputs(nuc, loc, nz, nm):
    rows, width = nuc.shape
    nx = nm // 2
    dma = pltpu.SemaphoreType.DMA
    anyspec = pl.BlockSpec(memory_space=pl.ANY)
    shape = jax.ShapeDtypeStruct((nz * rows, width), bf16)
    ex = (2, nz - 1, nx) if halves(rows, nm) else (1,)
    return pl.pallas_call(
        functools.partial(gather_kernel, nz, nm),
        out_shape=(shape, shape),
        in_specs=[anyspec] * 2,
        out_specs=[anyspec] * 2,
        scratch_shapes=[
            pltpu.VMEM((2, rows, width), bf16),
            dma((2,)),
            dma((2, 2, nz)), dma((2, 2, nz)),
            dma((2, 2, nz - 1, nx)), dma((2, 2, nz - 1, nx)),
            dma((2, 2, nz - 1, nx)), dma((2, 2, nz - 1, nx)),
            dma(ex), dma(ex), dma(ex), dma(ex),
        ],
        compiler_params=pltpu.CompilerParams(collective_id=0, has_side_effects=True),
        name="gather_inputs",
    )(nuc, loc)


def attend_kernel(nz, nm, heads, qk, vd, sharp, nuc, loc, gain, wqk, wv, mix, out, mix_all,
                  q_s, k_s, v_s, xs, xr, ys, yr, cs, cr, os, orr):
    share_mix(nz, nm, mix, mix_all, xs, xr, ys, yr, cs, cr, os, orr, 0)
    t, j = pl.program_id(0), pl.program_id(1)
    z = lax.axis_index("seq")
    rows = nuc.shape[0]
    b = 128

    def body(flip):
        r_i = lax.broadcasted_iota(jnp.int32, (b, b), 0)
        c_i = lax.broadcasted_iota(jnp.int32, (b, b), 1)
        anti = jnp.where(r_i + c_i == b - 1, 1.0, 0.0).astype(bf16)
        parts = []
        nb = rows // b
        for i in range(nb):
            if flip:
                l = jnp.dot(anti, loc[(nb - 1 - i) * b:(nb - i) * b, :], preferred_element_type=f32)
            else:
                l = loc[i * b:(i + 1) * b, :].astype(f32)
            s = nuc[i * b:(i + 1) * b, :].astype(f32) + l
            parts.append((normalize(s) * gain[...]).astype(bf16))
        normed = jnp.concatenate(parts, axis=0)
        here = pl.ds(pl.multiple_of(j * rows, rows), rows)
        key = jnp.dot(normed, wqk[1], preferred_element_type=f32)
        for h in range(heads):
            k_s[here, h * qk:(h + 1) * qk] = normalize(key[:, h * qk:(h + 1) * qk]).astype(bf16)
        v_s[here, :] = jnp.dot(normed, wv[...], preferred_element_type=f32).astype(bf16)

        @pl.when(j == z)
        def _():
            query = jnp.dot(normed, wqk[0], preferred_element_type=f32)
            for h in range(heads):
                q_s[:, h * qk:(h + 1) * qk] = normalize(query[:, h * qk:(h + 1) * qk]).astype(bf16)

    @pl.when(t == 0)
    def _():
        body(False)

    @pl.when(t == 1)
    def _():
        body(True)

    @pl.when(j == nz - 1)
    def _():
        s_all = k_s.shape[0]
        chunk = 128
        wide = heads * vd
        for i in range(rows // chunk):
            rr = slice(i * chunk, (i + 1) * chunk)
            if i == 1:
                share_mix(nz, nm, mix, mix_all, xs, xr, ys, yr, cs, cr, os, orr, 2)
            res = []
            for h in range(heads):
                lo = (h * vd) // 128 * 128
                hi = min(-(-((h + 1) * vd) // 128) * 128, wide)
                num = jnp.zeros((chunk, hi - lo), f32)
                tot = jnp.zeros((chunk, 1), f32)
                step = 1536
                for kk in range(0, s_all, step):
                    sc = lax.dot_general(
                        q_s[rr, h * qk:(h + 1) * qk], k_s[kk:kk + step, h * qk:(h + 1) * qk],
                        (((1,), (1,)), ((), ())), preferred_element_type=f32)
                    w = jnp.exp(sc * (sharp[h] / qk))
                    tot = tot + jnp.sum(w, axis=-1, keepdims=True)
                    num = num + jnp.dot(w.astype(bf16), v_s[kk:kk + step, lo:hi],
                                        preferred_element_type=f32)
                res.append((lo, hi, num / tot))
            if heads == 1:
                out[rr, :] = res[0][2].astype(bf16)
            else:
                for lo in range(0, wide, 128):
                    hi = min(lo + 128, wide)
                    col = lo + lax.broadcasted_iota(jnp.int32, (chunk, hi - lo), 1)
                    val = None
                    for h in range(heads):
                        l0, h0, r = res[h]
                        if h * vd < hi and (h + 1) * vd > lo:
                            v = r[:, lo - l0:hi - l0]
                            val = v if val is None else jnp.where(col < h * vd, val, v)
                    out[rr, lo:hi] = val.astype(bf16)

    share_mix(nz, nm, mix, mix_all, xs, xr, ys, yr, cs, cr, os, orr, 1)


def share_mix(nz, nm, mix, mix_all, xs, xr, ys, yr, cs, cr, os, orr, phase):
    nx = nm // 2
    step = pl.program_id(0) * nz + pl.program_id(1)
    m = lax.axis_index("mp")
    g = lax.axis_index("groups")
    x, c = m // 2, m % 2
    n = 4 if mix.shape[0] % 128 == 0 else 2
    size = mix.shape[0] // (2 * n)

    def rows(gg, p):
        return pl.ds(pl.multiple_of((gg * n + p) * size, size), size)

    def xcopy(p, d, mine):
        o = lax.rem(x + d, nx) if mine else lax.rem(x - d + nx, nx)
        k = m if mine else o * 2 + c
        return pltpu.make_async_remote_copy(
            src_ref=mix.at[rows(g, p)], dst_ref=mix_all.at[k, rows(g, p)],
            send_sem=xs.at[p, d - 1], recv_sem=xr.at[p, d - 1],
            device_id={"mp": o * 2 + c}, device_id_type=MESH)

    def ycopy(p, d, mine):
        k = lax.rem(x - d + nx, nx) * 2 + c
        r = rows(g if mine else 1 - g, p)
        return pltpu.make_async_remote_copy(
            src_ref=mix_all.at[k, r], dst_ref=mix_all.at[k, r],
            send_sem=ys.at[p, d - 1], recv_sem=yr.at[p, d - 1],
            device_id={"groups": 1 - g}, device_id_type=MESH)

    def ccopy(p, d, far, mine):
        k = lax.rem(x - d + nx, nx) * 2 + (c if mine else 1 - c)
        r = rows(1 - g if far else g, p)
        f = 1 if far else 0
        return pltpu.make_async_remote_copy(
            src_ref=mix_all.at[k, r], dst_ref=mix_all.at[k, r],
            send_sem=cs.at[p, d - 1, f], recv_sem=cr.at[p, d - 1, f],
            device_id={"mp": x * 2 + 1 - c}, device_id_type=MESH)

    def own(mine):
        return pltpu.make_async_remote_copy(
            src_ref=mix, dst_ref=mix_all.at[m if mine else x * 2 + 1 - c],
            send_sem=os, recv_sem=orr,
            device_id={"mp": x * 2 + 1 - c}, device_id_type=MESH)

    def pass_on(p):
        for d in range(1, nx):
            xcopy(p, d, False).wait_recv()
            ycopy(p, d, True).start()
            ccopy(p, d, False, True).start()

    def bring(p):
        for d in range(1, nx):
            ycopy(p, d, False).wait_recv()
            ccopy(p, d, True, True).start()

    if phase == 0:
        @pl.when(step == 0)
        def _():
            barrier = pltpu.get_barrier_semaphore()
            for d in range(1, nx):
                pl.semaphore_signal(barrier, inc=1, device_id={"mp": lax.rem(x + d, nx) * 2 + c}, device_id_type=MESH)
            pl.semaphore_signal(barrier, inc=1, device_id={"mp": x * 2 + 1 - c}, device_id_type=MESH)
            pl.semaphore_signal(barrier, inc=1, device_id={"groups": 1 - g}, device_id_type=MESH)
            pl.semaphore_wait(barrier, nx + 1)
            for p in range(n):
                for d in range(1, nx):
                    xcopy(p, d, True).start()
            own(True).start()

        turns = {4: (nz - 1, None, nz, nz + 2), 2: (nz, nz + 2)}[n]
        for p in range(n):
            if turns[p] is not None:
                pl.when(step == turns[p])(functools.partial(pass_on, p))

        @pl.when(step == 2 * nz - 1)
        def _():
            for p in range(n // 2):
                bring(p)
    elif phase == 2:
        if n == 4:
            pl.when(step == nz - 1)(functools.partial(pass_on, 1))
    else:
        @pl.when(step == 2 * nz - 1)
        def _():
            for p in range(n // 2, n):
                bring(p)
            own(True).wait_send()
            own(False).wait_recv()
            for p in range(n):
                for d in range(1, nx):
                    xcopy(p, d, True).wait_send()
                    ycopy(p, d, True).wait_send()
                    for far in (False, True):
                        ccopy(p, d, far, True).wait_send()
                        ccopy(p, d, far, False).wait_recv()


def attend(nuc_all, loc_all, gain, wqk, wv, sharp, mix, nz, nm, rows):
    heads = sharp.shape[0]
    width = nuc_all.shape[1]
    qk = wqk.shape[2] // heads
    vd = wv.shape[1] // heads
    s_all = nuc_all.shape[0]
    nx = nm // 2
    dma = pltpu.SemaphoreType.DMA
    full = lambda a: pl.BlockSpec(a.shape, lambda t, j: (0,) * a.ndim, pipeline_mode=pl.Buffered(1))
    anyspec = pl.BlockSpec(memory_space=pl.ANY)
    gain = gain.reshape(1, width)
    return pl.pallas_call(
        functools.partial(attend_kernel, nz, nm, heads, qk, vd),
        grid=(2, nz),
        out_shape=(jax.ShapeDtypeStruct((2, rows, heads * vd), bf16),
                   jax.ShapeDtypeStruct((nm,) + mix.shape, bf16)),
        in_specs=[
            pl.BlockSpec(memory_space=pltpu.SMEM),
            pl.BlockSpec((rows, width), lambda t, j: (j, 0)),
            pl.BlockSpec((rows, width), lambda t, j: (t * (nz - 1 - j) + (1 - t) * j, 0)),
            full(gain), full(wqk), full(wv), anyspec,
        ],
        out_specs=(pl.BlockSpec((pl.Squeezed(), rows, heads * vd), lambda t, j: (t, 0, 0)), anyspec),
        scratch_shapes=[
            pltpu.VMEM((rows, heads * qk), bf16),
            pltpu.VMEM((s_all, heads * qk), bf16),
            pltpu.VMEM((s_all, heads * vd), bf16),
            dma((4, nx)), dma((4, nx)), dma((4, nx)), dma((4, nx)),
            dma((4, nx, 2)), dma((4, nx, 2)), dma, dma,
        ],
        compiler_params=pltpu.CompilerParams(
            collective_id=2, has_side_effects=True, vmem_limit_bytes=56 << 20),
        name="attend",
    )(sharp, nuc_all, loc_all, gain, wqk, wv, mix)


def tail_kernel(nz, nm, att, nuc_h, loc_h, loc_all, gain, mix, mix_all, widen_h, narrow_h, out,
                att_all, nuc, loc, locm, mixv, widen, narrow, sbuf, rbuf, mid,
                lsem, msem, xs, xr, cs, cr, ss, sr):
    nx = nm // 2
    rows, width = nuc.shape
    share = width // nm
    b = 128
    parts = rows // b
    z = lax.axis_index("seq")
    m = lax.axis_index("mp")
    x, c = m // 2, m % 2
    barrier = pltpu.get_barrier_semaphore()
    for d in range(1, nm):
        pl.semaphore_signal(barrier, inc=1, device_id={"mp": lax.rem(m + d, nm)}, device_id_type=MESH)
    loads = [
        pltpu.make_async_copy(att, att_all.at[m], lsem.at[0]),
        pltpu.make_async_copy(nuc_h, nuc, lsem.at[1]),
        pltpu.make_async_copy(loc_h, loc, lsem.at[2]),
        pltpu.make_async_copy(loc_all.at[pl.ds(pl.multiple_of((nz - 1 - z) * rows, rows), rows)], locm, lsem.at[3]),
        pltpu.make_async_copy(widen_h, widen, lsem.at[4]),
        pltpu.make_async_copy(narrow_h, narrow, lsem.at[5]),
    ]
    mloads = [pltpu.make_async_copy(mix, mixv.at[m], msem.at[0])]
    for d in range(1, nm):
        k = lax.rem(m + d, nm)
        mloads.append(pltpu.make_async_copy(mix_all.at[k], mixv.at[k], msem.at[d]))
    for cp in loads[:4] + mloads + loads[4:]:
        cp.start()
    pl.semaphore_wait(barrier, nm - 1)

    def xcopy(i, d, mine):
        o = lax.rem(x + d, nx) if mine else lax.rem(x - d + nx, nx)
        k = m if mine else o * 2 + c
        r = pl.ds(i * b, b)
        return pltpu.make_async_remote_copy(
            src_ref=att.at[:, r], dst_ref=att_all.at[k, :, r], send_sem=xs.at[i, d - 1],
            recv_sem=xr.at[i, d - 1], device_id={"mp": o * 2 + c}, device_id_type=MESH)

    def ccopy(i, d, mine):
        o = lax.rem(x - d + nx, nx)
        k = o * 2 + (c if mine else 1 - c)
        r = pl.ds(i * b, b)
        ref = att.at[:, r] if d == 0 else att_all.at[k, :, r]
        return pltpu.make_async_remote_copy(
            src_ref=ref, dst_ref=att_all.at[k, :, r], send_sem=cs.at[i, d], recv_sem=cr.at[i, d],
            device_id={"mp": x * 2 + 1 - c}, device_id_type=MESH)

    def scopy(i, d):
        k = lax.rem(m + d, nm)
        return pltpu.make_async_remote_copy(
            src_ref=sbuf.at[i, k], dst_ref=rbuf.at[i, d - 1], send_sem=ss.at[i, d - 1],
            recv_sem=sr.at[i, d - 1], device_id={"mp": k}, device_id_type=MESH)

    for i in range(parts):
        for d in range(1, nx):
            xcopy(i, d, True).start()
        ccopy(i, 0, True).start()

    def pass_on(i):
        for d in range(1, nx):
            xcopy(i, d, False).wait_recv()
            ccopy(i, d, True).start()

    r_i = lax.broadcasted_iota(jnp.int32, (b, b), 0)
    c_i = lax.broadcasted_iota(jnp.int32, (b, b), 1)
    anti = jnp.where(r_i + c_i == b - 1, 1.0, 0.0).astype(bf16)
    for cp in loads[:4]:
        cp.wait()
    pass_on(0)
    for cp in mloads:
        cp.wait()
    for i in range(parts):
        r = slice(i * b, (i + 1) * b)
        n = nuc[r, :].astype(f32)
        s0 = n + loc[r, :].astype(f32)
        s1 = n + jnp.dot(anti, locm[(parts - 1 - i) * b:(parts - i) * b, :], preferred_element_type=f32)
        middle = jnp.concatenate([s0, s1], axis=0)
        for d in range(nx):
            ccopy(i, d, False).wait_recv()
        for k in range(nm):
            a = jnp.concatenate([att_all[k, 0, r, :], att_all[k, 1, r, :]], axis=0)
            middle = middle + jnp.dot(a, mixv[k], preferred_element_type=f32)
        if i + 1 < parts:
            pass_on(i + 1)
        normed = (normalize(middle) * gain[...]).astype(bf16)
        if i == 0:
            for cp in loads[4:]:
                cp.wait()
        up = jax.nn.gelu(jnp.dot(normed, widen[...], preferred_element_type=f32), approximate=True)
        both = (up[:b] + up[b:]).astype(bf16)
        down = jnp.dot(both, narrow[...], preferred_element_type=f32)
        total = middle[:b] + middle[b:] + down
        down = down.astype(bf16)
        for k in range(nm):
            sbuf[i, k] = down[:, k * share:(k + 1) * share]
            mid[i, k] = total[:, k * share:(k + 1) * share]
        for d in range(1, nm):
            scopy(i, d).start()
    for i in range(parts):
        acc = mid[i, m]
        for d in range(1, nm):
            scopy(i, d).wait_recv()
            acc = acc + rbuf[i, d - 1].astype(f32)
        out[i * b:(i + 1) * b, :] = 0.5 * acc
    for i in range(parts):
        for d in range(1, nx):
            xcopy(i, d, True).wait_send()
        for d in range(nx):
            ccopy(i, d, True).wait_send()
        for d in range(1, nm):
            scopy(i, d).wait_send()


def tail(att, nuc, loc, loc_all, gain, mix, mix_all, widen, narrow, nz, nm):
    rows, width = nuc.shape
    share = width // nm
    nx = nm // 2
    parts = rows // 128
    dma = pltpu.SemaphoreType.DMA
    anyspec = pl.BlockSpec(memory_space=pl.ANY)
    vm = pl.BlockSpec(memory_space=pltpu.VMEM)
    v = pltpu.VMEM
    return pl.pallas_call(
        functools.partial(tail_kernel, nz, nm),
        out_shape=jax.ShapeDtypeStruct((rows, share), f32),
        in_specs=[vm, anyspec, anyspec, anyspec, vm, anyspec, anyspec, anyspec, anyspec],
        out_specs=vm,
        scratch_shapes=[
            v((nm,) + att.shape, bf16), v(nuc.shape, bf16), v(nuc.shape, bf16), v(nuc.shape, bf16),
            v((nm,) + mix.shape, bf16), v(widen.shape, bf16), v(narrow.shape, bf16),
            v((parts, nm, 128, share), bf16), v((parts, nm - 1, 128, share), bf16),
            v((parts, nm, 128, share), f32),
            dma((6,)), dma((nm,)),
            dma((parts, nx)), dma((parts, nx)), dma((parts, nx)), dma((parts, nx)),
            dma((parts, nm)), dma((parts, nm)),
        ],
        compiler_params=pltpu.CompilerParams(
            collective_id=3, has_side_effects=True, vmem_limit_bytes=56 << 20),
        name="tail",
    )(att, nuc, loc, loc_all, gain.reshape(1, width), mix, mix_all, widen, narrow)


PLANES = ((0, 3), (1, 2))


def fused(nz, nm, heads, qk, vd, rows):
    return nz == 4 and nm == 4 and heads == 2 and qk == 128 and vd == 192 and rows % 128 == 0


def block_kernel(nz, nm, sharp, gain1, gain2, nuc_h, loc_h, wqk_h, wv_h, mix_h, widen_h, narrow_h, out,
                 nuc, loc, locm, rloc, nbuf, wqk, wv, send, recv, kbuf, vbuf, asend, att, abuf,
                 mixv, widen, narrow, mid0, up0, mids, downs, sbuf, rbuf, xbuf, fbuf,
                 lsem, ms, mr, xs, xr, qs, qr, ql, rs, rr, rl, hs, hr, ss, sr):
    rows, width = nuc.shape
    share = width // nm
    b = 128
    hb = b // 2
    parts = rows // b
    depth = mix_h.shape[0]
    g = lax.axis_index("groups")
    z = lax.axis_index("seq")
    m = lax.axis_index("mp")
    x, c = m // 2, m % 2
    to_x = {"mp": (1 - x) * 2 + c}
    to_y = {"groups": 1 - g}
    to_d = {"groups": 1 - g, "mp": (1 - x) * 2 + c}
    to_c = {"mp": x * 2 + 1 - c}

    def remote(src, dst, ssem, rsem, dev):
        return pltpu.make_async_remote_copy(
            src_ref=src, dst_ref=dst, send_sem=ssem, recv_sem=rsem, device_id=dev, device_id_type=MESH)

    barrier = pltpu.get_barrier_semaphore()
    for d in range(1, nz):
        pl.semaphore_signal(barrier, inc=1, device_id={"seq": lax.rem(z + d, nz)}, device_id_type=MESH)
    for d in range(1, nm):
        pl.semaphore_signal(barrier, inc=1, device_id={"mp": lax.rem(m + d, nm)}, device_id_type=MESH)
    pl.semaphore_signal(barrier, inc=1, device_id=to_y, device_id_type=MESH)
    pl.semaphore_signal(barrier, inc=1, device_id=to_d, device_id_type=MESH)

    loads = [
        pltpu.make_async_copy(nuc_h, nuc, lsem.at[0]),
        pltpu.make_async_copy(loc_h, loc, lsem.at[1]),
        pltpu.make_async_copy(wqk_h, wqk, lsem.at[2]),
        pltpu.make_async_copy(wv_h, wv, lsem.at[3]),
        pltpu.make_async_copy(widen_h, widen, lsem.at[4]),
        pltpu.make_async_copy(narrow_h, narrow, lsem.at[5]),
    ]
    own_mix = pltpu.make_async_copy(mix_h, mixv.at[pl.ds(pl.multiple_of(m * depth, depth), depth)], lsem.at[6])
    for cp in loads[:4]:
        cp.start()

    sl = rows // 8

    def piece(xx, gg, cc):
        return pl.ds(pl.multiple_of(((xx * 2 + gg) * 2 + cc) * sl, sl), sl)

    def loc_z():
        return remote(loc_h.at[piece(x, g, c)], locm.at[piece(x, g, c)], ms.at[0], mr.at[0], {"seq": nz - 1 - z})

    def loc_on(k):
        r = locm.at[piece(x, g, c)]
        return remote(r, r, ms.at[1 + k], mr.at[1 + k], (to_x, to_y, to_d)[k])

    def loc_c(k):
        r = locm.at[piece(x if k % 2 == 0 else 1 - x, g if k < 2 else 1 - g, c)]
        return remote(r, r, ms.at[4 + k], mr.at[4 + k], to_c)

    size = depth // 4

    def mrows(mm, gg, p):
        return pl.ds(pl.multiple_of(mm * depth + (gg * 2 + p) * size, size), size)

    def mix_x(p):
        return remote(mix_h.at[mrows(0, g, p)], mixv.at[mrows(m, g, p)], xs.at[p], xr.at[p], to_x)

    def mix_y(p):
        r = mixv.at[mrows((1 - x) * 2 + c, g, p)]
        return remote(r, r, xs.at[2 + p], xr.at[2 + p], to_y)

    def mix_c(p, far):
        r = mixv.at[mrows((1 - x) * 2 + c, 1 - g if far else g, p)]
        k = (6 if far else 4) + p
        return remote(r, r, xs.at[k], xr.at[k], to_c)

    def mix_own():
        return remote(mix_h, mixv.at[pl.ds(pl.multiple_of(m * depth, depth), depth)], xs.at[8], xr.at[8], to_c)

    pl.semaphore_wait(barrier, nz + nm)
    loc_z().start()
    mix_x(0).start()
    mix_own().start()
    own_mix.start()
    for cp in loads[4:]:
        cp.start()

    r_i = lax.broadcasted_iota(jnp.int32, (b, b), 0)
    c_i = lax.broadcasted_iota(jnp.int32, (b, b), 1)
    anti = jnp.where(r_i + c_i == b - 1, 1.0, 0.0).astype(bf16)
    low = lax.broadcasted_iota(jnp.int32, (hb, b), 1) < hb

    def chunk(i):
        return slice(i * b, (i + 1) * b)

    def qkv_send(t, h, i):
        return remote(send.at[t, h, i], recv.at[z, i], qs.at[t, h, i], qr.at[z, i], {"seq": PLANES[t][h]})

    def qkv_keep(t, h, i):
        return pltpu.make_async_copy(send.at[t, h, i], recv.at[z, i], ql.at[i])

    def project(t):
        other = loc if t == 0 else rloc
        for i in range(parts):
            if t == 1:
                rloc[chunk(i), :] = jnp.dot(
                    anti, locm[chunk(parts - 1 - i), :], preferred_element_type=f32).astype(bf16)
            s = nuc[chunk(i), :].astype(f32) + other[chunk(i), :].astype(f32)
            nbuf[chunk(i), :] = (normalize(s) * gain1[...]).astype(bf16)
        query = jnp.dot(nbuf[...], wqk[0], preferred_element_type=f32)
        key = jnp.dot(nbuf[...], wqk[1], preferred_element_type=f32)
        value = jnp.dot(nbuf[...], wv[...], preferred_element_type=f32)
        for i in range(parts):
            rest = value[chunk(i), b:2 * b]
            first, second = rest[:hb], pltpu.roll(rest[hb:], hb, 1)
            for h in range(2):
                send[t, h, i, 0:b, :] = normalize(query[chunk(i), h * b:(h + 1) * b]).astype(bf16)
                send[t, h, i, b:2 * b, :] = normalize(key[chunk(i), h * b:(h + 1) * b]).astype(bf16)
                send[t, h, i, 2 * b:3 * b, :] = value[chunk(i), 2 * h * b:(2 * h + 1) * b].astype(bf16)
                fold = jnp.where(low, first, second) if h == 0 else jnp.where(low, second, first)
                send[t, h, i, 3 * b:3 * b + hb, :] = fold.astype(bf16)
            for h in range(2):
                @pl.when(z != PLANES[t][h])
                def _(h=h, i=i):
                    qkv_send(t, h, i).start()

                @pl.when(z == PLANES[t][h])
                def _(h=h, i=i):
                    qkv_keep(t, h, i).start()

    def att_send(t, h, blk, i):
        return remote(asend.at[blk, i], att.at[m, t, i, h], rs.at[blk, i], rr.at[t, h, i], {"seq": blk})

    def att_keep(t, h, i):
        return pltpu.make_async_copy(asend.at[z, i], att.at[m, t, i, h], rl.at[i])

    def attend(t):
        h = jnp.where(z == PLANES[t][0], 0, 1)
        mask = low == (h == 0)
        for src in range(nz):
            for i in range(parts):
                @pl.when(z != src)
                def _():
                    remote(recv.at[src, i], recv.at[src, i], qs.at[0, 0, i], qr.at[src, i], {"seq": src}).wait_recv()

                @pl.when(z == src)
                def _():
                    qkv_keep(t, 0, i).wait()

                r0 = (src * parts + i) * b
                kbuf[r0:r0 + b, :] = recv[src, i, b:2 * b, :]
                vbuf[r0:r0 + b, 0:b] = recv[src, i, 2 * b:3 * b, :]
                fold = recv[src, i, 3 * b:3 * b + hb, :].astype(f32)
                turned = pltpu.roll(fold, hb, 1)
                vbuf[r0:r0 + hb, b:2 * b] = jnp.where(mask, fold, turned).astype(bf16)
                vbuf[r0 + hb:r0 + b, b:2 * b] = jnp.where(mask, turned, fold).astype(bf16)
        scale = sharp[h] * (1.4426950408889634 / b)
        up = z < nz // 2
        order = [jnp.where(up, 3, 0), jnp.where(up, 2, 1), z + 1 - 2 * lax.rem(z, 2), z]

        def step(i, carry):
            for s in range(nz):
                blk = order[s]
                sc = lax.dot_general(recv[blk, i, 0:b, :], kbuf[...], (((1,), (1,)), ((), ())),
                                     preferred_element_type=f32)
                w = jnp.exp2(sc * scale)
                tot = jnp.sum(w, axis=-1, keepdims=True)
                res = jnp.dot(w.astype(bf16), vbuf[...], preferred_element_type=f32) / tot
                asend[blk, i, 0:b, :] = res[:, :b].astype(bf16)
                asend[blk, i, b:b + hb, :] = jnp.where(mask, res[:hb, b:], res[hb:, b:]).astype(bf16)
                if s < nz - 1:
                    att_send(t, h, blk, i).start()
                else:
                    att_keep(t, h, i).start()
            return carry

        lax.fori_loop(0, parts, step, 0)

    def share_x(t, i):
        r = att.at[m, t, i]
        return remote(r, r, hs.at[t, i, 0], hr.at[t, i, 0], to_x)

    def share_c(t, i, k):
        r = att.at[m if k == 0 else (1 - x) * 2 + c, t, i]
        return remote(r, r, hs.at[t, i, 1 + k], hr.at[t, i, 1 + k], to_c)

    def relay(t, i):
        for h in range(2):
            src = PLANES[t][h]

            @pl.when(z != src)
            def _():
                r = att.at[m, t, i, h]
                remote(r, r, rs.at[0, i], rr.at[t, h, i], {"seq": src}).wait_recv()

            @pl.when(z == src)
            def _():
                att_keep(t, h, i).wait()
        share_x(t, i).start()
        share_c(t, i, 0).start()

    def relay_c(t, i):
        share_x(t, i).wait_recv()
        share_c(t, i, 1).start()

    def middle(t, i):
        for k in range(2):
            share_c(t, i, k).wait_recv()
        for k in range(nm):
            f0, f1 = att[k, t, i, 0, b:b + hb, :].astype(f32), att[k, t, i, 1, b:b + hb, :].astype(f32)
            lo = k * 3 * b
            abuf[chunk(i), lo:lo + b] = att[k, t, i, 0, 0:b, :]
            abuf[i * b:i * b + hb, lo + b:lo + 2 * b] = jnp.where(low, f0, f1).astype(bf16)
            abuf[i * b + hb:(i + 1) * b, lo + b:lo + 2 * b] = pltpu.roll(jnp.where(low, f1, f0), hb, 1).astype(bf16)
            abuf[chunk(i), lo + 2 * b:lo + 3 * b] = att[k, t, i, 1, 0:b, :]

    def upper(t, r):
        s = nuc[r, :].astype(f32) + (loc if t == 0 else rloc)[r, :].astype(f32)
        mid = s + jnp.dot(abuf[r, :], mixv[...], preferred_element_type=f32)
        normed = (normalize(mid) * gain2[...]).astype(bf16)
        return mid, jax.nn.gelu(jnp.dot(normed, widen[...], preferred_element_type=f32), approximate=True)

    def pair_copy(i):
        return remote(sbuf.at[i, 1 - c], rbuf.at[i], ss.at[i, 0], sr.at[i, 0], to_c)

    def sum_copy(i):
        return remote(xbuf.at[i], fbuf.at[i], ss.at[i, 1], sr.at[i, 1], to_x)

    def pass_sum(i):
        pair_copy(i).wait_recv()
        xbuf[i] = (downs[i, c, 1 - x] + rbuf[i, 1 - x].astype(f32)).astype(bf16)
        sum_copy(i).start()

    first = (z == PLANES[0][0]) | (z == PLANES[0][1])
    second = (z == PLANES[1][0]) | (z == PLANES[1][1])
    for cp in loads[:4]:
        cp.wait()
    project(0)
    loc_z().wait_recv()
    for k in (2, 0, 1):
        loc_on(k).start()
    loc_c(0).start()
    mix_x(0).wait_recv()
    mix_y(0).start()
    mix_c(0, False).start()
    for k in range(3):
        loc_on(k).wait_recv()
        loc_c(k + 1).start()
    mix_x(1).start()
    for k in range(4):
        loc_c(k).wait_recv()
    project(1)

    @pl.when(first)
    def _():
        attend(0)

    mix_y(0).wait_recv()
    mix_c(0, True).start()
    mix_x(1).wait_recv()
    mix_y(1).start()
    mix_c(1, False).start()

    for i in range(parts):
        relay(0, i)
    mix_y(1).wait_recv()
    mix_c(1, True).start()

    @pl.when(second)
    def _():
        attend(1)

    for i in range(parts):
        relay_c(0, i)
    own_mix.wait()
    mix_own().wait_recv()
    for p in range(2):
        for far in (False, True):
            mix_c(p, far).wait_recv()
    for cp in loads[4:]:
        cp.wait()
    for i in range(parts):
        middle(0, i)
    for i in range(parts):
        pl.when(second)(functools.partial(relay, 1, i))
        mid, up = upper(0, chunk(i))
        mid0[chunk(i), :] = mid
        up0[chunk(i), :] = up
    pl.when(first)(functools.partial(relay, 1, 0))
    for i in range(parts):
        if i + 1 < parts:
            pl.when(first)(functools.partial(relay, 1, i + 1))
        relay_c(1, i)
        if i > 0:
            pass_sum(i - 1)
        middle(1, i)
        mid, up = upper(1, chunk(i))
        both = (up + up0[chunk(i), :]).astype(bf16)
        down = jnp.dot(both, narrow[...], preferred_element_type=f32)
        total = mid + mid0[chunk(i), :] + down
        for k in range(nm):
            cols = slice(k * share, (k + 1) * share)
            sbuf[i, k % 2, k // 2] = down[:, cols].astype(bf16)
            downs[i, k % 2, k // 2] = down[:, cols]
            mids[i, k] = total[:, cols]
        pair_copy(i).start()
    pass_sum(parts - 1)
    for i in range(parts):
        sum_copy(i).wait_recv()
        out[chunk(i), :] = 0.5 * (mids[i, m] + rbuf[i, x].astype(f32) + fbuf[i].astype(f32))

    loc_z().wait_send()
    for k in range(3):
        loc_on(k).wait_send()
    for k in range(4):
        loc_c(k).wait_send()
    mix_own().wait_send()
    for p in range(2):
        mix_x(p).wait_send()
        mix_y(p).wait_send()
        for far in (False, True):
            mix_c(p, far).wait_send()
    for i in range(parts):
        for t in range(2):
            for h in range(2):
                @pl.when(z != PLANES[t][h])
                def _():
                    qkv_send(t, h, i).wait_send()
            share_x(t, i).wait_send()
            for k in range(2):
                share_c(t, i, k).wait_send()
        for blk in range(nz):
            @pl.when(z != blk)
            def _():
                att_send(0, 0, blk, i).wait_send()
        pair_copy(i).wait_send()
        sum_copy(i).wait_send()


def block(nuc, loc, premix, wqk, wv, sharp, mix, premlp, widen, narrow, nz, nm):
    rows, width = nuc.shape
    parts = rows // 128
    hidden = widen.shape[1]
    share = width // nm
    dma = pltpu.SemaphoreType.DMA
    anyspec = pl.BlockSpec(memory_space=pl.ANY)
    vm = pl.BlockSpec(memory_space=pltpu.VMEM)
    v = pltpu.VMEM
    return pl.pallas_call(
        functools.partial(block_kernel, nz, nm),
        out_shape=pltpu.VMEM((rows, share), f32),
        in_specs=[pl.BlockSpec(memory_space=pltpu.SMEM), vm, vm] + [anyspec] * 7,
        out_specs=vm,
        scratch_shapes=[
            v(nuc.shape, bf16), v(nuc.shape, bf16), v(nuc.shape, bf16), v(nuc.shape, bf16), v(nuc.shape, bf16),
            v(wqk.shape, bf16), v(wv.shape, bf16),
            v((2, 2, parts, 448, 128), bf16), v((nz, parts, 448, 128), bf16),
            v((nz * rows, 128), bf16), v((nz * rows, 256), bf16),
            v((nz, parts, 192, 128), bf16), v((nm, 2, parts, 2, 192, 128), bf16), v((rows, width), bf16),
            v((nm * mix.shape[0], width), bf16), v(widen.shape, bf16), v(narrow.shape, bf16),
            v((rows, width), f32), v((rows, hidden), f32),
            v((parts, nm, 128, share), f32), v((parts, 2, 2, 128, share), f32),
            v((parts, 2, 2, 128, share), bf16), v((parts, 2, 128, share), bf16),
            v((parts, 128, share), bf16), v((parts, 128, share), bf16),
            dma((7,)), dma((8,)), dma((8,)), dma((9,)), dma((9,)),
            dma((2, 2, parts)), dma((nz, parts)), dma((parts,)),
            dma((nz, parts)), dma((2, 2, parts)), dma((parts,)),
            dma((2, parts, 3)), dma((2, parts, 3)), dma((parts, 2)), dma((parts, 2)),
        ],
        compiler_params=pltpu.CompilerParams(
            collective_id=1, has_side_effects=True, vmem_limit_bytes=58 << 20),
        name="block",
    )(sharp, premix, premlp, nuc, loc, wqk, wv, mix, widen, narrow)


def shards(nuc, loc, premix, wqk, wv, sharp, mixing, premlp, widen, narrow):
    rows = nuc.shape[0]
    nz, nm = lax.axis_size("seq"), lax.axis_size("mp")
    heads = sharp.shape[0]
    if fused(nz, nm, heads, wqk.shape[2] // heads, wv.shape[1] // heads, rows):
        return block(nuc, loc, premix, wqk, wv, sharp, mixing, premlp, widen, narrow, nz, nm)
    nuc_all, loc_all = gather_inputs(nuc, loc, nz, nm)
    att, mix_all = attend(nuc_all, loc_all, premix, wqk, wv, sharp, mixing, nz, nm, rows)
    return tail(att, nuc, loc, loc_all, premlp, mixing, mix_all, widen, narrow, nz, nm)


def solution(mesh):
    return jax.shard_map(
        shards,
        mesh=mesh,
        in_specs=(
            P(("groups", "seq"), None),
            P("seq", None),
            P(),
            P(None, None, "mp"),
            P(None, "mp"),
            P("mp"),
            P("mp", None),
            P(),
            P(None, "mp"),
            P("mp", None),
        ),
        out_specs=P(("groups", "seq"), "mp"),
        check_vma=False,
    )
```
